256 devices in a mesh: dp: 16 (over z, core), mp: 16 (over y, x).
Axes of the slice: x: 4, y: 4, z: 8, core: 2. Of those that a mesh axis runs over, the one named last changes fastest.
Arguments:
- hidden_states: bfloat16 [256, 640, 1280], P(('dp', 'mp')), may hold values from -6 to 6
- ln_attn_gain: float32 [1280], replicated, may hold values from 0.1 to 1.9
- w_qkv: bfloat16 [1280, 16, 192], P(None, 'mp'), may hold values from -0.15625 to 0.15625
- output_weight: bfloat16 [64, 16, 1280], P(None, 'mp'), may hold values from -0.75 to 0.75
- ln_final_gain: float32 [1280], replicated, may hold values from 0.1 to 1.9
- dense_weight: bfloat16 [1280, 1280], replicated, may hold values from -0.15625 to 0.15625
- decoder_weight: bfloat16 [1280, 33], replicated, may hold values from -0.5390625 to 0.5390625
- decoder_bias: float32 [33], replicated, may hold values from -4 to 4
- seq_tokens: int32 [24, 640], replicated, may hold values from 4 to 23
- seq_lengths: int32 [24], replicated, may hold values from 128 to 640
- copy_sequence: int32 [256], replicated, may hold values from 0 to 23
- mask_code: int32 [256, 64], replicated, may hold values from 0 to 1048575
- copy_owner: int32 [256], replicated, may hold values from 0 to 255, each once
Outputs:
- pll: float32 [256, 64], P('dp', 'mp')
The draws below stay inside these ranges and needn't reach their ends.
Inputs may be any that keep to these rules, and one draw needn't show every extreme that they name: `seq_tokens`: amino-acid token ids. `copy_owner`: every row of pll is named by exactly one copy.
All inputs are finite; a program needn't handle non-finite values.
Results may differ from the reference program's by a relative error of at most 0.0038.
Values may be sent and summed in bfloat16 or wider, within the bound.
No kernel may reach another device: no remote copies, remote signals or barrier semaphores. Data moves between devices by JAX's collectives and lax.ppermute only.
A program may use at most 128 MiB of HBM per device.

```python
import jax
import jax.numpy as jnp
from jax import lax

D = 1280
HD = 64
VOCAB = 33
HEADS = 16
LMAX = 640
MASKS = 64
SEQS = 24
COPIES = 256


def place_ends(entries, own_key, low, high):
    longest = entries.shape.index(max(entries.shape))
    spots = []
    for shift in (0, 1):
        where = [jax.random.randint(jax.random.fold_in(own_key, axis), (), 0, length) for axis, length in enumerate(entries.shape)]
        where[longest] = (where[longest] + shift) % entries.shape[longest]
        spots.append(tuple(where))
    return entries.at[spots[0]].set(low).at[spots[1]].set(high)


def levels(stream_key, dims, split, least, high):
    loudness, own = 1.0, jax.random.fold_in(stream_key, 6)
    for axis_at, blocks in split:
        steps = jnp.exp(jax.random.uniform(jax.random.fold_in(own, axis_at), (blocks,), jnp.float32, least / len(split), high / len(split)))
        loudness = loudness * jnp.repeat(steps, dims[axis_at] // blocks).reshape([-1 if axis == axis_at else 1 for axis in range(len(dims))])
    return loudness


def bell_draw(key, shape, spread, limit, cuts=(), kind=jnp.bfloat16):
    loudness = levels(key, shape, cuts, -0.22, 0.18) if cuts else 1.0
    array = jax.random.normal(key, shape, jnp.float32) * spread * loudness
    return jnp.minimum(jnp.maximum(array, -limit), limit).astype(kind)


def setup_inputs(seed: int = 0) -> dict:
    streams_of = jax.random.split(jax.random.key(seed), 14)
    hidden_states = bell_draw(streams_of[0], (COPIES, LMAX, D), 1.0, 6.0, ((0, 256),))
    ln_attn_gain = jnp.clip(1.0 + 0.18 * jax.random.normal(streams_of[1], (D,), jnp.float32), 0.1, 1.9)
    w_qkv = bell_draw(streams_of[2], (D, HEADS, 3 * HD), D ** -0.5, 0.15625, ((1, 16),))
    output_weight = bell_draw(streams_of[3], (HD, HEADS, D), 0.125, 0.75, ((1, 16),))
    ln_final_gain = jnp.clip(1.0 + 0.18 * jax.random.normal(streams_of[4], (D,), jnp.float32), 0.1, 1.9)
    dense_weight = bell_draw(streams_of[5], (D, D), D ** -0.5, 0.15625)
    decoder_weight = bell_draw(streams_of[6], (D, VOCAB), 0.09, 0.5390625)
    decoder_bias = bell_draw(streams_of[7], (VOCAB,), 1.0, 4.0, (), jnp.float32)
    seq_tokens = place_ends(jax.random.randint(streams_of[8], (SEQS, LMAX), 4, 24), jax.random.fold_in(streams_of[8], 1), 4, 23).astype(jnp.int32)
    seq_lengths = place_ends(jax.random.randint(streams_of[9], (SEQS,), LMAX // 5, LMAX + 1), jax.random.fold_in(streams_of[9], 1), LMAX // 5, LMAX).astype(jnp.int32)
    copy_sequence = place_ends(jax.random.randint(streams_of[10], (COPIES,), 0, SEQS), jax.random.fold_in(streams_of[10], 1), 0, SEQS - 1).astype(jnp.int32)
    mask_code = place_ends(jax.random.randint(streams_of[11], (COPIES, MASKS), 0, 1048576), jax.random.fold_in(streams_of[11], 1), 0, 1048575).astype(jnp.int32)
    copy_owner = jax.random.permutation(streams_of[12], COPIES).astype(jnp.int32)
    return {"hidden_states": hidden_states, "ln_attn_gain": ln_attn_gain, "w_qkv": w_qkv, "output_weight": output_weight, "ln_final_gain": ln_final_gain, "dense_weight": dense_weight, "decoder_weight": decoder_weight, "decoder_bias": decoder_bias, "seq_tokens": seq_tokens, "seq_lengths": seq_lengths, "copy_sequence": copy_sequence, "mask_code": mask_code, "copy_owner": copy_owner}


epsilon = 1e-05

def layer_norm(inputs):
    average = lax.optimization_barrier(jnp.mean(inputs, axis=-1, keepdims=True))
    centred = inputs - average
    variance = lax.optimization_barrier(jnp.mean(centred * centred, axis=-1, keepdims=True))
    return centred * lax.rsqrt(variance + epsilon)

def rotary_tables(seq_span, head_size):
    half_width = head_size // 2
    frequency = 1.0 / 10000.0 ** (jnp.arange(half_width, dtype=jnp.float32) * (2.0 / head_size))
    angles = jnp.arange(seq_span, dtype=jnp.float32)[:, None] * frequency[None, :]
    angles = jnp.concatenate([angles, angles], axis=-1)
    return (jnp.cos(angles), jnp.sin(angles))

def rotate(inputs, cosine, sine):
    half_width = inputs.shape[-1] // 2
    turned = jnp.concatenate([-inputs[..., half_width:], inputs[..., :half_width]], axis=-1)
    return inputs * cosine + turned * sine

def score_rows(residual, ln_final_gain, dense_weight, decoder_weight, decoder_bias, targets):
    feature = residual.shape[-1]
    normed_final = (layer_norm(residual) * ln_final_gain).astype(jnp.bfloat16).reshape(-1, feature)
    dense_out = jnp.dot(normed_final, dense_weight, preferred_element_type=jnp.float32)
    headed = layer_norm(jax.nn.gelu(dense_out, approximate=False)).astype(jnp.bfloat16)
    logits = jnp.dot(headed, decoder_weight, preferred_element_type=jnp.float32) + decoder_bias
    log_probs = logits - jax.nn.logsumexp(logits, axis=-1, keepdims=True)
    vocab_ids = jnp.arange(logits.shape[-1], dtype=jnp.int32)
    flat_targets = targets.reshape(-1)
    picked = lax.optimization_barrier(jnp.sum(jnp.where(flat_targets[:, None] == vocab_ids[None, :], log_probs, 0.0), axis=-1))
    return picked.reshape(targets.shape)

def one_copy(states, length, positions, ln_attn_gain, w_qkv, output_weight, cosine, sine):
    seq_span, feature = states.shape
    head_count = w_qkv.shape[1]
    head_size = w_qkv.shape[2] // 3
    normed = (layer_norm(states.astype(jnp.float32)) * ln_attn_gain).astype(jnp.bfloat16)
    projected = jnp.dot(normed, w_qkv.reshape(feature, -1), preferred_element_type=jnp.float32)
    projected = projected.reshape(seq_span, head_count, 3, head_size)
    key_matrix = rotate(projected[:, :, 1], cosine[:, None, :], sine[:, None, :]).astype(jnp.bfloat16)
    value_matrix = projected[:, :, 2].astype(jnp.bfloat16)
    query_matrix = projected[positions, :, 0] * head_size ** (-0.5)
    query_matrix = rotate(query_matrix, cosine[positions][:, None, :], sine[positions][:, None, :]).astype(jnp.bfloat16)
    attention_logits = jnp.einsum('fop,yop->ofy', query_matrix.astype(jnp.float32), key_matrix.astype(jnp.float32))
    alive = jnp.arange(seq_span, dtype=jnp.int32) < length
    attention_logits = jnp.where(alive[None, None, :], attention_logits, -1e+30)
    largest = lax.optimization_barrier(jnp.max(attention_logits, axis=-1, keepdims=True))
    weights = jnp.exp(attention_logits - largest)
    attention_probs = (weights / lax.optimization_barrier(jnp.sum(weights, axis=-1, keepdims=True))).astype(jnp.bfloat16)
    context_vectors = jnp.einsum('vuy,yvx->uvx', attention_probs.astype(jnp.float32), value_matrix.astype(jnp.float32)).astype(jnp.bfloat16)
    attention_mixed = jnp.einsum('frn,nrl->fl', context_vectors.astype(jnp.float32), output_weight.astype(jnp.float32))
    return states[positions].astype(jnp.float32) + attention_mixed

def reference(hidden_states, ln_attn_gain, w_qkv, output_weight, ln_final_gain, dense_weight, decoder_weight, decoder_bias, seq_tokens, seq_lengths, copy_sequence, mask_code, copy_owner):
    cosine, sine = rotary_tables(LMAX, HD)
    lengths = seq_lengths[copy_sequence]
    positions = (mask_code % lengths[:, None]).astype(jnp.int32)
    targets = jnp.take_along_axis(seq_tokens[copy_sequence], positions, axis=1)

    def per_copy(items):
        states, length, spots = items
        return one_copy(states, length, spots, ln_attn_gain, w_qkv, output_weight, cosine, sine)
    residual = lax.map(per_copy, (hidden_states, lengths, positions))
    attention_logits = score_rows(residual, ln_final_gain, dense_weight, decoder_weight, decoder_bias, targets)
    return jnp.zeros_like(attention_logits).at[copy_owner].set(attention_logits)
```

```python
import numpy as np
import jax
import jax.numpy as jnp
from jax import lax
from jax.experimental import pallas as pl
from jax.experimental.pallas import tpu as pltpu
from jax.sharding import Mesh, PartitionSpec as P

epsilon = 1e-05
F32 = jnp.float32
BF16 = jnp.bfloat16
VMEM = pltpu.MemorySpace.VMEM
SMEM = pltpu.MemorySpace.SMEM


def rotary_tables(seq_span, head_size):
    half = head_size // 2
    power = (np.arange(half, dtype=np.float32) * np.float32(2.0 / head_size)).astype(np.float32)
    frequency = (np.float32(1.0) / np.power(np.float32(10000.0), power)).astype(np.float32)
    angles = (np.arange(seq_span, dtype=np.float32)[:, None] * frequency[None, :]).astype(np.float32)
    cosine = np.cos(angles.astype(np.float64)).astype(np.float32)
    sine = np.sin(angles.astype(np.float64)).astype(np.float32)
    cos_table = np.concatenate([cosine] * 4, axis=1)
    sin_table = np.concatenate([-sine, sine] * 2, axis=1)
    return cos_table, sin_table


def nt_dot(a, b):
    return lax.dot_general(a, b, (((1,), (1,)), ((), ())), preferred_element_type=F32)


def nn_dot(a, b, **options):
    return lax.dot_general(a, b, (((1,), (0,)), ((), ())), preferred_element_type=F32, **options)


def rotate(part, cos_table, sin_table, half):
    width = part.shape[1]
    lane = lax.broadcasted_iota(jnp.int32, part.shape, 1) % (2 * half)
    turned = jnp.where(
        lane < half,
        pltpu.roll(part, width - half, 1),
        pltpu.roll(part, half, 1),
    )
    return part * cos_table + turned * sin_table


def whole(space=VMEM):
    return pl.BlockSpec(memory_space=space)


def call(kernel, outs, n_smem, args, vmem=48 * 1024 * 1024):
    specs = [whole(SMEM)] * n_smem + [whole()] * (len(args) - n_smem)
    return pl.pallas_call(
        kernel,
        out_shape=outs,
        in_specs=specs,
        out_specs=jax.tree.map(lambda _: whole(), outs),
        compiler_params=pltpu.CompilerParams(vmem_limit_bytes=vmem),
    )(*args)


def prepare_kernel(
    index_ref, sequence_ref, length_ref, codes_ref, tokens_ref, states_ref, gain_ref,
    cos_ref, sin_ref,
    normed_ref, picked_ref, rows_ref, qcos_ref, qsin_ref, targets_ref,
):
    copy = index_ref[0]
    sequence = sequence_ref[copy]
    length = length_ref[sequence]
    codes_all = codes_ref[...]
    lane = lax.broadcasted_iota(jnp.int32, codes_all.shape, 1)
    codes = jnp.sum(jnp.where(lane == copy, codes_all, 0), axis=1, keepdims=True)
    quotient = jnp.floor(codes.astype(F32) / length.astype(F32)).astype(jnp.int32)
    positions = codes - quotient * length
    positions = jnp.where(positions < 0, positions + length, positions)
    positions = jnp.where(positions >= length, positions - length, positions)
    span = states_ref.shape[0]
    spot = lax.broadcasted_iota(jnp.int32, (codes.shape[0], span), 1)
    hit = spot == positions
    tokens = tokens_ref[pl.ds(sequence, 1), :]
    targets = jnp.sum(jnp.where(hit, tokens, 0), axis=1, keepdims=True)
    targets_ref[...] = jnp.broadcast_to(targets, targets_ref.shape)
    hot = hit.astype(F32)
    qcos_ref[...] = nn_dot(hot, cos_ref[...], precision=lax.Precision.HIGHEST)
    qsin_ref[...] = nn_dot(hot, sin_ref[...], precision=lax.Precision.HIGHEST)
    hot = hot.astype(BF16)
    block = 128
    gain = gain_ref[...]

    def step(i, carry):
        at = pl.multiple_of(i * block, block)
        values = states_ref[pl.ds(at, block), :].astype(F32)
        average = jnp.mean(values, axis=1, keepdims=True)
        centred = values - average
        variance = jnp.mean(centred * centred, axis=1, keepdims=True)
        normed_ref[pl.ds(at, block), :] = (
            centred * lax.rsqrt(variance + epsilon) * gain
        ).astype(BF16)
        return carry

    lax.fori_loop(0, span // block, step, 0)
    rows_ref[...] = nn_dot(hot, states_ref[...])
    picked_ref[...] = nn_dot(hot, normed_ref[...]).astype(BF16)


def keys_kernel(
    index_ref, sequence_ref, length_ref, core_ref, normed_ref, picked_ref, mine_refs, other_refs,
    cos_ref, sin_ref, qcos_ref, qsin_ref, probs_ref,
):
    half = 32
    length = length_ref[sequence_ref[index_ref[0]]]
    first = core_ref[0] == 0
    mine = jnp.concatenate([r[...] for r in mine_refs], axis=0)
    other = jnp.concatenate([r[...] for r in other_refs], axis=0)
    key_weight = jnp.where(first, mine, other)
    query_weight = jnp.where(first, other, mine)
    keys = nt_dot(normed_ref[...], key_weight)
    queries = nt_dot(picked_ref[...], query_weight) * 0.125
    pairs = keys.shape[1] // 128
    keys = jnp.concatenate(
        [rotate(keys[:, 128 * i : 128 * i + 128], cos_ref[...], sin_ref[...], half) for i in range(pairs)],
        axis=1,
    ).astype(BF16)
    queries = jnp.concatenate(
        [rotate(queries[:, 128 * i : 128 * i + 128], qcos_ref[...], qsin_ref[...], half) for i in range(pairs)],
        axis=1,
    ).astype(BF16)
    heads = keys.shape[1] // 64
    masks = queries.shape[0]
    spread = jnp.concatenate([queries] * heads, axis=0)
    row = lax.broadcasted_iota(jnp.int32, spread.shape, 0) // masks
    lane = lax.broadcasted_iota(jnp.int32, spread.shape, 1) // 64
    spread = jnp.where(row == lane, spread, jnp.zeros_like(spread))
    logits = nt_dot(spread, keys)
    alive = lax.broadcasted_iota(jnp.int32, logits.shape, 1) < length
    logits = jnp.where(alive, logits, -1e30)
    largest = jnp.max(logits, axis=1, keepdims=True)
    weights = jnp.exp(logits - largest)
    total = jnp.sum(weights, axis=1, keepdims=True)
    probs_ref[...] = (weights * (1.0 / total)).astype(BF16)


def values_kernel(core_ref, normed_ref, mine_refs, other_refs, values_ref, out_ref):
    first = core_ref[0] == 0
    mine = jnp.concatenate([r[...] for r in mine_refs], axis=0)
    other = jnp.concatenate([r[...] for r in other_refs], axis=0)
    value_weight = jnp.where(first, mine, other)
    out_ref[...] = jnp.where(first, other, mine)
    values_ref[...] = nt_dot(normed_ref[...], value_weight).astype(BF16)


def final_kernel(
    rows_ref, targets_ref, gain_ref, bias_ref, dense_ref, decoder_ref, probs_refs, values_refs,
    out_refs, scores_ref,
):
    masks = rows_ref.shape[0]
    residual = rows_ref[...]
    for column in range(len(values_refs)):
        probs = jnp.concatenate(
            [r[masks * column : masks * (column + 1), :] for r in probs_refs], axis=0
        )
        mixed = nn_dot(probs, values_refs[column][...])
        heads = mixed.shape[1] // 64
        lane = lax.broadcasted_iota(jnp.int32, (masks, mixed.shape[1]), 1) // 64
        context = jnp.zeros((masks, mixed.shape[1]), F32)
        for head in range(heads):
            context = jnp.where(lane == head, mixed[masks * head : masks * (head + 1), :], context)
        residual = residual + nn_dot(context.astype(BF16), out_refs[column][...])
    average = jnp.mean(residual, axis=1, keepdims=True)
    centred = residual - average
    variance = jnp.mean(centred * centred, axis=1, keepdims=True)
    normed = (centred * lax.rsqrt(variance + epsilon) * gain_ref[...]).astype(BF16)
    dense = nn_dot(normed, dense_ref[...])
    active = 0.5 * dense * (1.0 + lax.erf(dense * np.float32(0.5**0.5)))
    average = jnp.mean(active, axis=1, keepdims=True)
    centred = active - average
    variance = jnp.mean(centred * centred, axis=1, keepdims=True)
    headed = (centred * lax.rsqrt(variance + epsilon)).astype(BF16)
    logits = nt_dot(headed, decoder_ref[...]) + bias_ref[...]
    largest = jnp.max(logits, axis=1, keepdims=True)
    total = jnp.sum(jnp.exp(logits - largest), axis=1, keepdims=True)
    vocab = lax.broadcasted_iota(jnp.int32, logits.shape, 1)
    chosen = jnp.sum(jnp.where(vocab == targets_ref[:, 0:1], logits, 0.0), axis=1, keepdims=True)
    score = chosen - largest - jnp.log(total)
    row = lax.broadcasted_iota(jnp.int32, (masks, masks), 0)
    lane = lax.broadcasted_iota(jnp.int32, (masks, masks), 1)
    scores_ref[...] = jnp.sum(jnp.where(row == lane, score, 0.0), axis=0, keepdims=True)


def pull(array, axis, offset):
    size = lax.axis_size(axis)
    return lax.ppermute(array, axis, [((i + offset) % size, i) for i in range(size)])


def swap(array):
    return lax.ppermute(array, "core", [(0, 1), (1, 0)])


def gather_plane(block, first_axis, second_axis):
    near = [block] + [pull(block, first_axis, d) for d in (1, 2, 3)]
    near = jnp.concatenate(near, axis=0)
    half = near.shape[0] // 2
    ahead = pull(near, second_axis, 1)
    behind = pull(near, second_axis, 3)
    far = [pull(ahead[:half], second_axis, 1), pull(behind[half:], second_axis, 3)]
    return [[near], [ahead], [behind], far]


def on_device(
    hidden_states,
    ln_attn_gain,
    w_qkv,
    output_weight,
    ln_final_gain,
    dense_weight,
    decoder_weight,
    decoder_bias,
    seq_tokens,
    seq_lengths,
    copy_sequence,
    mask_code,
    copy_owner,
):
    _, seq_span, feature = hidden_states.shape
    head_size = output_weight.shape[0]
    masks = mask_code.shape[1]
    vocab = decoder_weight.shape[1]
    core = lax.axis_index("core")
    group = lax.axis_index(("z", "core"))
    member = lax.axis_index(("y", "x"))
    members = lax.axis_size(("y", "x"))
    groups = lax.axis_size(("z", "core"))
    copy = (group * members + member).astype(jnp.int32).reshape(1)
    core_at = core.astype(jnp.int32).reshape(1)

    turned = jnp.transpose(w_qkv[:, 0, :])
    query_weight = turned[:head_size]
    key_weight = turned[head_size : 2 * head_size]
    value_weight = turned[2 * head_size :]
    out_weight = output_weight[:, 0, :]
    first = core == 0
    key_side = gather_plane(jnp.where(first, key_weight, query_weight), "x", "y")
    value_side = gather_plane(jnp.where(first, value_weight, out_weight), "y", "x")

    cos_table, sin_table = (jnp.asarray(t) for t in rotary_tables(seq_span, head_size))
    shape = jax.ShapeDtypeStruct
    normed, picked, rows, qcos, qsin, targets = call(
        prepare_kernel,
        [
            shape((seq_span, feature), BF16),
            shape((masks, feature), BF16),
            shape((masks, feature), F32),
            shape((masks, 128), F32),
            shape((masks, 128), F32),
            shape((masks, 128), jnp.int32),
        ],
        3,
        (
            copy, copy_sequence, seq_lengths, mask_code.T, seq_tokens, hidden_states[0],
            ln_attn_gain.reshape(1, -1), cos_table, sin_table,
        ),
    )

    def keys_call(parts):
        others = [swap(p) for p in parts]
        n = len(parts)
        width = sum(p.shape[0] for p in parts)

        def kernel(a, b, c, d, e, f, *refs):
            keys_kernel(a, b, c, d, e, f, refs[:n], refs[n : 2 * n], *refs[2 * n :])

        return call(
            kernel,
            shape((masks * width // head_size, seq_span), BF16),
            4,
            (copy, copy_sequence, seq_lengths, core_at, normed, picked, *parts, *others,
             cos_table, sin_table, qcos, qsin),
        )

    def values_call(parts):
        others = [swap(p) for p in parts]
        n = len(parts)
        width = sum(p.shape[0] for p in parts)

        def kernel(a, b, *refs):
            values_kernel(a, b, refs[:n], refs[n : 2 * n], *refs[2 * n :])

        return call(
            kernel,
            [shape((seq_span, width), BF16), shape((width, feature), BF16)],
            1,
            (core_at, normed, *parts, *others),
        )

    order = (0, 1, 3, 2)
    probs = [keys_call(key_side[i]) for i in order]
    mixed = [values_call(value_side[i]) for i in order]
    values = [m[0] for m in mixed]
    outs = [m[1] for m in mixed]
    n = len(probs)

    def kernel(a, b, c, d, e, f, *refs):
        final_kernel(a, b, c, d, e, f, refs[:n], refs[n : 2 * n], refs[2 * n : 3 * n], refs[3 * n])

    scores = call(
        kernel,
        shape((1, masks), F32),
        0,
        (rows, targets, ln_final_gain.reshape(1, -1), decoder_bias.reshape(1, -1), dense_weight,
         decoder_weight.T, *probs, *values, *outs),
    )

    own = masks // members
    pieces = lax.all_to_all(scores.reshape(members, own), ("y", "x"), 0, 0, tiled=True)
    owners = lax.dynamic_slice_in_dim(copy_owner, group * members, members, 0)
    slots = jnp.arange(groups * members, dtype=jnp.int32).reshape(groups, members)
    placed = jnp.where(
        slots[:, :, None, None] == owners[None, None, :, None], pieces[None, None, :, :], 0.0
    )
    placed = jnp.sum(placed, axis=2).reshape(groups, members * own)
    arrived = lax.all_to_all(placed, ("z", "core"), 0, 0, tiled=True)
    return jnp.sum(arrived.reshape(groups, members, own), axis=0)


def solution(mesh):
    fine = Mesh(mesh.devices.reshape(8, 2, 4, 4), ("z", "core", "y", "x"))
    dp, mp = ("z", "core"), ("y", "x")
    placed = (
        P(("z", "core", "y", "x"), None, None),
        P(),
        P(None, mp, None),
        P(None, mp, None),
        P(),
        P(),
        P(),
        P(),
        P(),
        P(),
        P(),
        P(),
        P(),
    )
    return jax.shard_map(
        on_device, mesh=fine, in_specs=placed, out_specs=P(dp, mp), check_vma=False
    )
```

```python
import numpy as np
import jax
import jax.numpy as jnp
from jax import lax
from jax.experimental import pallas as pl
from jax.experimental.pallas import tpu as pltpu
from jax.sharding import Mesh, PartitionSpec as P

epsilon = 1e-05
F32 = jnp.float32
BF16 = jnp.bfloat16


def rotary_tables(seq_span, head_size):
    half = head_size // 2
    power = (np.arange(half, dtype=np.float32) * np.float32(2.0 / head_size)).astype(np.float32)
    frequency = (np.float32(1.0) / np.power(np.float32(10000.0), power)).astype(np.float32)
    angles = (np.arange(seq_span, dtype=np.float32)[:, None] * frequency[None, :]).astype(np.float32)
    cosine = np.cos(angles.astype(np.float64)).astype(np.float32)
    sine = np.sin(angles.astype(np.float64)).astype(np.float32)
    cos_table = np.concatenate([cosine] * 4, axis=1)
    sin_table = np.concatenate([-sine, sine] * 2, axis=1)
    return cos_table, sin_table


def nt_dot(a, b):
    return lax.dot_general(a, b, (((1,), (1,)), ((), ())), preferred_element_type=F32)


def nn_dot(a, b, **options):
    return lax.dot_general(a, b, (((1,), (0,)), ((), ())), preferred_element_type=F32, **options)


def rotate(part, cos_table, sin_table, half):
    width = part.shape[1]
    lane = lax.broadcasted_iota(jnp.int32, part.shape, 1) % (2 * half)
    turned = jnp.where(
        lane < half,
        pltpu.roll(part, width - half, 1),
        pltpu.roll(part, half, 1),
    )
    return part * cos_table + turned * sin_table


def call(kernel, outs, n_smem, args, flops=0, exps=0, vmem=24 * 1024 * 1024):
    space = pltpu.MemorySpace
    specs = [pl.BlockSpec(memory_space=space.SMEM)] * n_smem
    specs += [pl.BlockSpec(memory_space=space.VMEM)] * (len(args) - n_smem)
    moved = sum(a.size * a.dtype.itemsize for a in list(args) + jax.tree.leaves(outs))
    return pl.pallas_call(
        kernel,
        out_shape=outs,
        in_specs=specs,
        out_specs=jax.tree.map(lambda _: pl.BlockSpec(memory_space=space.VMEM), outs),
        cost_estimate=pl.CostEstimate(flops=flops, transcendentals=exps, bytes_accessed=moved),
        compiler_params=pltpu.CompilerParams(vmem_limit_bytes=vmem),
    )(*args)


def copy_of(place_ref, core):
    return (place_ref[0] * 2 + core) * 16 + place_ref[2]


def prepare_kernel(
    place_ref, sequence_ref, length_ref, codes_ref, tokens_ref, mine_ref, other_ref, gain_ref,
    cos_ref, sin_ref,
    normed_ref, picked_ref, rows_ref, qcos_ref, qsin_ref, targets_ref,
):
    span = mine_ref.shape[0]
    masks = codes_ref.shape[0]
    gain = gain_ref[...]
    block = 128
    for states_ref, core in ((mine_ref, place_ref[1]), (other_ref, 1 - place_ref[1])):
        copy = copy_of(place_ref, core)
        sequence = sequence_ref[copy]
        length = length_ref[sequence]
        codes_all = codes_ref[...]
        lane = lax.broadcasted_iota(jnp.int32, codes_all.shape, 1)
        codes = jnp.sum(jnp.where(lane == copy, codes_all, 0), axis=1, keepdims=True)
        quotient = jnp.floor(codes.astype(F32) / length.astype(F32)).astype(jnp.int32)
        positions = codes - quotient * length
        positions = jnp.where(positions < 0, positions + length, positions)
        positions = jnp.where(positions >= length, positions - length, positions)
        hit = lax.broadcasted_iota(jnp.int32, (masks, span), 1) == positions
        tokens = tokens_ref[pl.ds(sequence, 1), :]
        targets = jnp.sum(jnp.where(hit, tokens, 0), axis=1, keepdims=True)
        base = pl.multiple_of(core * span, block)
        at_mask = pl.ds(pl.multiple_of(core * masks, masks), masks)
        targets_ref[at_mask, :] = jnp.broadcast_to(targets, (masks, targets_ref.shape[1]))
        hot = hit.astype(F32)
        qcos_ref[at_mask, :] = nn_dot(hot, cos_ref[...], precision=lax.Precision.HIGHEST)
        qsin_ref[at_mask, :] = nn_dot(hot, sin_ref[...], precision=lax.Precision.HIGHEST)
        hot = hot.astype(BF16)

        def step(i, carry):
            at = pl.multiple_of(i * block, block)
            values = states_ref[pl.ds(at, block), :].astype(F32)
            average = jnp.mean(values, axis=1, keepdims=True)
            centred = values - average
            variance = jnp.mean(centred * centred, axis=1, keepdims=True)
            normed_ref[pl.ds(base + at, block), :] = (
                centred * lax.rsqrt(variance + epsilon) * gain
            ).astype(BF16)
            return carry

        lax.fori_loop(0, span // block, step, 0)
        rows_ref[at_mask, :] = nn_dot(hot, states_ref[...])
        picked_ref[at_mask, :] = nn_dot(hot, normed_ref[pl.ds(base, span), :]).astype(BF16)


def keys_kernel(
    place_ref, sequence_ref, length_ref, normed_ref, picked_ref, cos_ref, sin_ref, qcos_ref,
    qsin_ref, block_refs, probs_ref,
):
    size = block_refs[0].shape[0] // 2
    span = normed_ref.shape[0] // 2
    masks = picked_ref.shape[0] // 2
    heads = len(block_refs)
    key_weight = jnp.concatenate([r[size:, :] for r in block_refs], axis=0)
    query_weight = jnp.concatenate([r[:size, :] for r in block_refs], axis=0)
    keys = nt_dot(normed_ref[...], key_weight)
    queries = nt_dot(picked_ref[...], query_weight) * 0.125
    for core in range(2):
        length = length_ref[sequence_ref[copy_of(place_ref, core)]]
        rows = slice(span * core, span * (core + 1))
        own = slice(masks * core, masks * (core + 1))
        turned_keys, turned_queries = [], []
        for i in range(heads // 2):
            lanes = slice(128 * i, 128 * (i + 1))
            turned_keys.append(rotate(keys[rows, lanes], cos_ref[...], sin_ref[...], size // 2))
            turned_queries.append(
                rotate(queries[own, lanes], qcos_ref[own, :], qsin_ref[own, :], size // 2)
            )
        key_rows = jnp.concatenate(turned_keys, axis=1).astype(BF16)
        query_rows = jnp.concatenate(turned_queries, axis=1).astype(BF16)
        spread = jnp.concatenate([query_rows] * heads, axis=0)
        row = lax.broadcasted_iota(jnp.int32, spread.shape, 0) // masks
        lane = lax.broadcasted_iota(jnp.int32, spread.shape, 1) // size
        spread = jnp.where(row == lane, spread, jnp.zeros_like(spread))
        logits = nt_dot(spread, key_rows)
        alive = lax.broadcasted_iota(jnp.int32, logits.shape, 1) < length
        logits = jnp.where(alive, logits, -1e30)
        largest = jnp.max(logits, axis=1, keepdims=True)
        weights = jnp.exp(logits - largest)
        total = jnp.sum(weights, axis=1, keepdims=True)
        probs_ref[core] = (weights * (1.0 / total)).astype(BF16)


def values_kernel(normed_ref, block_refs, values_ref):
    size = block_refs[0].shape[0] // 2
    weight = jnp.concatenate([r[:size, :] for r in block_refs], axis=0)
    values_ref[...] = nt_dot(normed_ref[...], weight).astype(BF16)


def mix_kernel(place_ref, probs_refs, values_refs, block_refs, partial_ref):
    right = place_ref[3] == 1
    own_probs, near_probs, far_probs = probs_refs
    size = block_refs[0].shape[0] // 2
    masks = own_probs.shape[1] // 2
    span = own_probs.shape[2]
    columns = ((0,), (1, 3), (2,))

    def rows_of(core, step, which):
        ref = (own_probs, near_probs, far_probs, near_probs)[step]
        start = masks * (which + (2 if step == 3 else 0))
        return ref[core, start : start + masks, :]

    contexts = []
    for core in range(2):
        parts = []
        for values_ref, group in zip(values_refs, columns):
            stack = []
            for column in group:
                which = (0, 1, 1, 0)[column]
                for i in range(2):
                    even = rows_of(core, (0, 2)[i], which)
                    odd = rows_of(core, (3, 1)[i], which)
                    if column % 2:
                        even, odd = odd, even
                    stack.append(jnp.where(right, even, odd))
            mixed = nn_dot(
                jnp.concatenate(stack, axis=0), values_ref[span * core : span * (core + 1), :]
            )
            lane = lax.broadcasted_iota(jnp.int32, (masks, mixed.shape[1]), 1) // size
            context = mixed[:masks, :]
            for head in range(1, len(stack)):
                context = jnp.where(
                    lane == head, mixed[masks * head : masks * (head + 1), :], context
                )
            parts.append(context.astype(BF16))
        contexts.append(jnp.concatenate(parts, axis=1))
    weight = jnp.concatenate([r[size:, :] for r in block_refs], axis=0)
    partial_ref[...] = nn_dot(jnp.concatenate(contexts, axis=0), weight)


def score_kernel(
    place_ref, owner_ref, rows_ref, mine_ref, other_ref, targets_ref, gain_ref, bias_ref,
    dense_ref, decoder_ref, placed_ref,
):
    residual = rows_ref[...] + (mine_ref[...] + other_ref[...])
    average = jnp.mean(residual, axis=1, keepdims=True)
    centred = residual - average
    variance = jnp.mean(centred * centred, axis=1, keepdims=True)
    normed = (centred * lax.rsqrt(variance + epsilon) * gain_ref[...]).astype(BF16)
    dense = nn_dot(normed, dense_ref[...])
    active = 0.5 * dense * (1.0 + lax.erf(dense * np.float32(0.5**0.5)))
    average = jnp.mean(active, axis=1, keepdims=True)
    centred = active - average
    variance = jnp.mean(centred * centred, axis=1, keepdims=True)
    headed = (centred * lax.rsqrt(variance + epsilon)).astype(BF16)
    logits = nt_dot(headed, decoder_ref[...]) + bias_ref[...]
    largest = jnp.max(logits, axis=1, keepdims=True)
    total = jnp.sum(jnp.exp(logits - largest), axis=1, keepdims=True)
    vocab = lax.broadcasted_iota(jnp.int32, logits.shape, 1)
    chosen = jnp.sum(jnp.where(vocab == targets_ref[:, 0:1], logits, 0.0), axis=1, keepdims=True)
    score = chosen - largest - jnp.log(total)
    masks = score.shape[0] // 2
    devices, width = placed_ref.shape
    member = lax.broadcasted_iota(jnp.int32, (devices, masks), 0) % 16
    part = lax.broadcasted_iota(jnp.int32, (devices, masks), 1) // 4
    take = (member == part).astype(F32)
    fits = (
        lax.broadcasted_iota(jnp.int32, (masks, width), 0) % 4
        == lax.broadcasted_iota(jnp.int32, (masks, width), 1) % 4
    )
    layer = lax.broadcasted_iota(jnp.int32, (devices, width), 0) // 16
    slot = lax.broadcasted_iota(jnp.int32, (devices, width), 1) // 4
    wanted = 16 * (2 * layer + place_ref[1]) + slot
    placed = jnp.zeros((devices, width), F32)
    for core in range(2):
        own = jnp.where(fits, score[masks * core : masks * (core + 1), :], 0.0)
        laid = nn_dot(take, own, precision=lax.Precision.HIGHEST)
        placed = jnp.where(wanted == owner_ref[copy_of(place_ref, core)], laid, placed)
    placed_ref[...] = placed


def pull(array, axis, offset):
    size = lax.axis_size(axis)
    return lax.ppermute(array, axis, [((i + offset) % size, i) for i in range(size)])


def swap(array):
    return lax.ppermute(array, "core", [(0, 1), (1, 0)])


def pull_right(array, axis, offset):
    pairs = []
    for core in range(2):
        for y in range(4):
            for x in range(4):
                if (x + y) % 2 == core:
                    to_y = (y - offset) % 4 if axis == "y" else y
                    to_x = (x - offset) % 4 if axis == "x" else x
                    pairs.append(((core * 4 + y) * 4 + x, (core * 4 + to_y) * 4 + to_x))
    return lax.ppermute(array, ("core", "y", "x"), pairs)


def gather_line(block, right, axis):
    behind = pull_right(block, axis, -1)
    ahead = pull_right(block, axis, 1)
    across = pull_right(block, axis, 2)
    return jnp.where(right, block, behind), jnp.where(right, across, ahead)


def gather_plane(low, high, axis):
    ahead_low = pull(low, axis, 1)
    behind_high = pull(high, axis, 3)
    ahead_high = pull(high, axis, 1)
    behind_low = pull(low, axis, 3)
    far_low = pull(ahead_low, axis, 1)
    far_high = pull(behind_high, axis, 3)
    return (
        (low, high),
        (ahead_low, ahead_high, behind_low, behind_high),
        (far_low, far_high),
    )


def on_device(
    hidden_states,
    ln_attn_gain,
    w_qkv,
    output_weight,
    ln_final_gain,
    dense_weight,
    decoder_weight,
    decoder_bias,
    seq_tokens,
    seq_lengths,
    copy_sequence,
    mask_code,
    copy_owner,
):
    _, span, feature = hidden_states.shape
    size = output_weight.shape[0]
    masks = mask_code.shape[1]
    core = lax.axis_index("core")
    member = lax.axis_index(("y", "x"))
    right = (lax.axis_index("x") + lax.axis_index("y")) % 2 == core
    place = jnp.stack([lax.axis_index("z"), core, member, right.astype(core.dtype)])
    place = place.astype(jnp.int32)

    turned = jnp.transpose(w_qkv[:, 0, :])
    key_block = turned[: 2 * size]
    value_block = jnp.concatenate([turned[2 * size :], output_weight[:, 0, :]], axis=0)
    key_low, key_high = gather_line(key_block, right, "x")
    value_low, value_high = gather_line(value_block, right, "y")
    key_groups = gather_plane(key_low, key_high, "y")
    value_groups = gather_plane(value_low, value_high, "x")
    states = hidden_states[0]
    states_other = swap(states)

    cos_table, sin_table = (jnp.asarray(t) for t in rotary_tables(span, size))
    shape = jax.ShapeDtypeStruct
    normed, picked, rows, qcos, qsin, targets = call(
        prepare_kernel,
        [
            shape((2 * span, feature), BF16),
            shape((2 * masks, feature), BF16),
            shape((2 * masks, feature), F32),
            shape((2 * masks, 128), F32),
            shape((2 * masks, 128), F32),
            shape((2 * masks, 128), jnp.int32),
        ],
        3,
        (
            place, copy_sequence, seq_lengths, mask_code.T, seq_tokens, states, states_other,
            ln_attn_gain.reshape(1, -1), cos_table, sin_table,
        ),
        flops=8 * masks * span * feature + 20 * span * feature,
    )

    def keys_call(blocks):
        heads = len(blocks)

        def kernel(*refs):
            keys_kernel(*refs[:9], refs[9 : 9 + heads], refs[9 + heads])

        return call(
            kernel,
            shape((2, heads * masks, span), BF16),
            3,
            (place, copy_sequence, seq_lengths, normed, picked, cos_table, sin_table, qcos, qsin,
             *blocks),
            flops=4 * span * feature * 256,
            exps=2 * heads * masks * span,
        )

    def values_call(blocks):
        heads = len(blocks)

        def kernel(*refs):
            values_kernel(refs[0], refs[1 : 1 + heads], refs[1 + heads])

        return call(
            kernel,
            shape((2 * span, heads * size), BF16),
            0,
            (normed, *blocks),
            flops=4 * span * feature * 256,
        )

    probs = [keys_call(blocks) for blocks in key_groups]
    values = [values_call(blocks) for blocks in value_groups]
    value_blocks = [b for group in value_groups for b in group]

    def kernel(*refs):
        mix_kernel(refs[0], refs[1:4], refs[4:7], refs[7:15], refs[15])

    partial = call(
        kernel,
        shape((2 * masks, feature), F32),
        1,
        (place, *probs, *values, *value_blocks),
        flops=4 * masks * feature * 8 * size,
    )
    placed = call(
        score_kernel,
        shape((128, 64), F32),
        2,
        (
            place, copy_owner, rows, partial, swap(partial), targets,
            ln_final_gain.reshape(1, -1), decoder_bias.reshape(1, -1), dense_weight,
            decoder_weight.T,
        ),
        flops=4 * masks * feature * feature,
    )
    arrived = lax.all_to_all(placed, ("z", "y", "x"), 0, 0, tiled=True)
    return jnp.sum(arrived, axis=0).reshape(16, 4)


def solution(mesh):
    fine = Mesh(mesh.devices.reshape(8, 2, 4, 4), ("z", "core", "y", "x"))
    dp, mp = ("z", "core"), ("y", "x")
    placed = (
        P(("z", "core", "y", "x"), None, None),
        P(),
        P(None, mp, None),
        P(None, mp, None),
        P(),
        P(),
        P(),
        P(),
        P(),
        P(),
        P(),
        P(),
        P(),
    )
    return jax.shard_map(
        on_device, mesh=fine, in_specs=placed, out_specs=P(dp, mp), check_vma=False
    )
```

```python
import numpy as np
import jax
import jax.numpy as jnp
from jax import lax
from jax.experimental import pallas as pl
from jax.experimental.pallas import tpu as pltpu
from jax.sharding import Mesh, PartitionSpec as P

epsilon = 1e-05
F32 = jnp.float32
BF16 = jnp.bfloat16


def rotary_tables(seq_span, head_size):
    half = head_size // 2
    power = (np.arange(half, dtype=np.float32) * np.float32(2.0 / head_size)).astype(np.float32)
    frequency = (np.float32(1.0) / np.power(np.float32(10000.0), power)).astype(np.float32)
    angles = (np.arange(seq_span, dtype=np.float32)[:, None] * frequency[None, :]).astype(np.float32)
    cosine = np.cos(angles.astype(np.float64)).astype(np.float32)
    sine = np.sin(angles.astype(np.float64)).astype(np.float32)
    cos_table = np.concatenate([cosine] * 4, axis=1)
    sin_table = np.concatenate([-sine, sine] * 2, axis=1)
    return cos_table, sin_table


def nt_dot(a, b):
    return lax.dot_general(a, b, (((1,), (1,)), ((), ())), preferred_element_type=F32)


def nn_dot(a, b, **options):
    return lax.dot_general(a, b, (((1,), (0,)), ((), ())), preferred_element_type=F32, **options)


def rotate(part, cos_table, sin_table, half):
    width = part.shape[1]
    lane = lax.broadcasted_iota(jnp.int32, part.shape, 1) % (2 * half)
    turned = jnp.where(
        lane < half,
        pltpu.roll(part, width - half, 1),
        pltpu.roll(part, half, 1),
    )
    return part * cos_table + turned * sin_table


def call(kernel, outs, n_smem, args, flops=0, exps=0, vmem=24 * 1024 * 1024):
    space = pltpu.MemorySpace
    specs = [pl.BlockSpec(memory_space=space.SMEM)] * n_smem
    specs += [pl.BlockSpec(memory_space=space.VMEM)] * (len(args) - n_smem)
    moved = sum(a.size * a.dtype.itemsize for a in list(args) + jax.tree.leaves(outs))
    return pl.pallas_call(
        kernel,
        out_shape=outs,
        in_specs=specs,
        out_specs=jax.tree.map(lambda _: pl.BlockSpec(memory_space=space.VMEM), outs),
        cost_estimate=pl.CostEstimate(flops=flops, transcendentals=exps, bytes_accessed=moved),
        compiler_params=pltpu.CompilerParams(vmem_limit_bytes=vmem),
    )(*args)


def pack_kernel(turned_ref, out_ref, key_ref, value_ref, sems):
    size = out_ref.shape[0]
    copies = (
        pltpu.make_async_copy(turned_ref.at[: 2 * size], key_ref, sems.at[0]),
        pltpu.make_async_copy(turned_ref.at[2 * size :], value_ref.at[:size], sems.at[1]),
        pltpu.make_async_copy(out_ref, value_ref.at[size:], sems.at[2]),
    )
    for copy in copies:
        copy.start()
    for copy in copies:
        copy.wait()


def pack(turned, out_weight):
    size, feature = out_weight.shape
    anywhere = pl.BlockSpec(memory_space=pl.ANY)
    return pl.pallas_call(
        pack_kernel,
        out_shape=[jax.ShapeDtypeStruct((2 * size, feature), BF16)] * 2,
        in_specs=[anywhere] * 2,
        out_specs=[anywhere] * 2,
        scratch_shapes=[pltpu.SemaphoreType.DMA((3,))],
    )(turned, out_weight)


def copy_of(place_ref, core):
    return (place_ref[0] * 2 + core) * 16 + place_ref[2]


def prepare_kernel(
    mine, place_ref, sequence_ref, length_ref, codes_ref, tokens_ref, states_ref, gain_ref,
    cos_ref, sin_ref,
    normed_ref, picked_ref, rows_ref, qcos_ref, qsin_ref, targets_ref,
):
    span = states_ref.shape[0]
    masks = codes_ref.shape[0]
    gain = gain_ref[...]
    block = 128
    copy = copy_of(place_ref, place_ref[1] if mine else 1 - place_ref[1])
    sequence = sequence_ref[copy]
    length = length_ref[sequence]
    codes_all = codes_ref[...]
    lane = lax.broadcasted_iota(jnp.int32, codes_all.shape, 1)
    codes = jnp.sum(jnp.where(lane == copy, codes_all, 0), axis=1, keepdims=True)
    quotient = jnp.floor(codes.astype(F32) / length.astype(F32)).astype(jnp.int32)
    positions = codes - quotient * length
    positions = jnp.where(positions < 0, positions + length, positions)
    positions = jnp.where(positions >= length, positions - length, positions)
    hit = lax.broadcasted_iota(jnp.int32, (masks, span), 1) == positions
    tokens = tokens_ref[pl.ds(sequence, 1), :]
    targets = jnp.sum(jnp.where(hit, tokens, 0), axis=1, keepdims=True)
    targets_ref[...] = jnp.broadcast_to(targets, targets_ref.shape)
    hot = hit.astype(F32)
    qcos_ref[...] = nn_dot(hot, cos_ref[...], precision=lax.Precision.HIGHEST)
    qsin_ref[...] = nn_dot(hot, sin_ref[...], precision=lax.Precision.HIGHEST)
    hot = hot.astype(BF16)

    def step(i, carry):
        at = pl.multiple_of(i * block, block)
        values = states_ref[pl.ds(at, block), :].astype(F32)
        average = jnp.mean(values, axis=1, keepdims=True)
        centred = values - average
        variance = jnp.mean(centred * centred, axis=1, keepdims=True)
        normed_ref[pl.ds(at, block), :] = (
            centred * lax.rsqrt(variance + epsilon) * gain
        ).astype(BF16)
        return carry

    lax.fori_loop(0, span // block, step, 0)
    rows_ref[...] = nn_dot(hot, states_ref[...])
    picked_ref[...] = nn_dot(hot, normed_ref[...]).astype(BF16)


def keys_kernel(
    place_ref, sequence_ref, length_ref, normed_refs, picked_refs, cos_ref, sin_ref, qcos_refs,
    qsin_refs, block_refs, probs_ref,
):
    size = block_refs[0].shape[0] // 2
    masks = picked_refs[0].shape[0]
    heads = len(block_refs)
    key_weight = jnp.concatenate([r[size:, :] for r in block_refs], axis=0)
    query_weight = jnp.concatenate([r[:size, :] for r in block_refs], axis=0)
    cores = (place_ref[1], 1 - place_ref[1])
    for which in range(2):
        length = length_ref[sequence_ref[copy_of(place_ref, cores[which])]]
        keys = nt_dot(normed_refs[which][...], key_weight)
        queries = nt_dot(picked_refs[which][...], query_weight) * 0.125
        turned_keys, turned_queries = [], []
        for i in range(heads // 2):
            lanes = slice(128 * i, 128 * (i + 1))
            turned_keys.append(rotate(keys[:, lanes], cos_ref[...], sin_ref[...], size // 2))
            turned_queries.append(
                rotate(queries[:, lanes], qcos_refs[which][...], qsin_refs[which][...], size // 2)
            )
        key_rows = jnp.concatenate(turned_keys, axis=1).astype(BF16)
        query_rows = jnp.concatenate(turned_queries, axis=1).astype(BF16)
        spread = jnp.concatenate([query_rows] * heads, axis=0)
        row = lax.broadcasted_iota(jnp.int32, spread.shape, 0) // masks
        lane = lax.broadcasted_iota(jnp.int32, spread.shape, 1) // size
        spread = jnp.where(row == lane, spread, jnp.zeros_like(spread))
        logits = nt_dot(spread, key_rows)
        alive = lax.broadcasted_iota(jnp.int32, logits.shape, 1) < length
        logits = jnp.where(alive, logits, -1e30)
        largest = jnp.max(logits, axis=1, keepdims=True)
        weights = jnp.exp(logits - largest)
        total = jnp.sum(weights, axis=1, keepdims=True)
        probs_ref[which] = (weights * (1.0 / total)).astype(BF16)


def values_kernel(normed_refs, block_refs, values_ref):
    size = block_refs[0].shape[0] // 2
    weight = jnp.concatenate([r[:size, :] for r in block_refs], axis=0)
    for which in range(2):
        values_ref[which] = nt_dot(normed_refs[which][...], weight).astype(BF16)


def mix_kernel(place_ref, probs_refs, values_refs, block_refs, partial_ref):
    right = place_ref[3] == 1
    own_probs, near_probs, far_probs = probs_refs
    size = block_refs[0].shape[0] // 2
    masks = own_probs.shape[1] // 2
    columns = ((0,), (1, 3), (2,))

    def rows_of(core, step, which):
        ref = (own_probs, near_probs, far_probs, near_probs)[step]
        start = masks * (which + (2 if step == 3 else 0))
        return ref[core, start : start + masks, :]

    contexts = []
    for core in range(2):
        parts = []
        for values_ref, group in zip(values_refs, columns):
            stack = []
            for column in group:
                which = column // 2
                for i in range(2):
                    even = rows_of(core, (0, 2)[i], which)
                    odd = rows_of(core, (1, 3)[i], which)
                    if column % 2:
                        even, odd = odd, even
                    stack.append(jnp.where(right, even, odd))
            mixed = nn_dot(jnp.concatenate(stack, axis=0), values_ref[core])
            lane = lax.broadcasted_iota(jnp.int32, (masks, mixed.shape[1]), 1) // size
            context = mixed[:masks, :]
            for head in range(1, len(stack)):
                context = jnp.where(
                    lane == head, mixed[masks * head : masks * (head + 1), :], context
                )
            parts.append(context.astype(BF16))
        contexts.append(jnp.concatenate(parts, axis=1))
    weight = jnp.concatenate([r[size:, :] for r in block_refs], axis=0)
    partial_ref[...] = nn_dot(jnp.concatenate(contexts, axis=0), weight)


def score_kernel(
    place_ref, owner_ref, rows_refs, partial_ref, arrived_ref, targets_refs, gain_ref, bias_ref,
    dense_ref, decoder_ref, placed_ref,
):
    masks = rows_refs[0].shape[0]
    residual = jnp.concatenate(
        [
            rows_refs[0][...] + (partial_ref[:masks, :] + arrived_ref[masks:, :]),
            rows_refs[1][...] + (partial_ref[masks:, :] + arrived_ref[:masks, :]),
        ],
        axis=0,
    )
    targets = jnp.concatenate([r[:, 0:1] for r in targets_refs], axis=0)
    average = jnp.mean(residual, axis=1, keepdims=True)
    centred = residual - average
    variance = jnp.mean(centred * centred, axis=1, keepdims=True)
    normed = (centred * lax.rsqrt(variance + epsilon) * gain_ref[...]).astype(BF16)
    dense = nn_dot(normed, dense_ref[...])
    active = 0.5 * dense * (1.0 + lax.erf(dense * np.float32(0.5**0.5)))
    average = jnp.mean(active, axis=1, keepdims=True)
    centred = active - average
    variance = jnp.mean(centred * centred, axis=1, keepdims=True)
    headed = (centred * lax.rsqrt(variance + epsilon)).astype(BF16)
    logits = nt_dot(headed, decoder_ref[...]) + bias_ref[...]
    largest = jnp.max(logits, axis=1, keepdims=True)
    total = jnp.sum(jnp.exp(logits - largest), axis=1, keepdims=True)
    vocab = lax.broadcasted_iota(jnp.int32, logits.shape, 1)
    chosen = jnp.sum(jnp.where(vocab == targets, logits, 0.0), axis=1, keepdims=True)
    score = chosen - largest - jnp.log(total)
    devices, width = placed_ref.shape
    member = lax.broadcasted_iota(jnp.int32, (devices, masks), 0) % 16
    part = lax.broadcasted_iota(jnp.int32, (devices, masks), 1) // 4
    take = (member == part).astype(F32)
    fits = (
        lax.broadcasted_iota(jnp.int32, (masks, width), 0) % 4
        == lax.broadcasted_iota(jnp.int32, (masks, width), 1) % 4
    )
    layer = lax.broadcasted_iota(jnp.int32, (devices, width), 0) // 16
    slot = lax.broadcasted_iota(jnp.int32, (devices, width), 1) // 4
    wanted = 16 * (2 * layer + place_ref[1]) + slot
    placed = jnp.zeros((devices, width), F32)
    cores = (place_ref[1], 1 - place_ref[1])
    for which in range(2):
        own = jnp.where(fits, score[masks * which : masks * (which + 1), :], 0.0)
        laid = nn_dot(take, own, precision=lax.Precision.HIGHEST)
        placed = jnp.where(wanted == owner_ref[copy_of(place_ref, cores[which])], laid, placed)
    placed_ref[...] = placed


def pull(array, axis, offset):
    size = lax.axis_size(axis)
    return lax.ppermute(array, axis, [((i + offset) % size, i) for i in range(size)])


def swap(array):
    return lax.ppermute(array, "core", [(0, 1), (1, 0)])


def after(array, *others):
    return lax.optimization_barrier((array, *others))[0]


def gather_line(block, axis):
    near, far = [], []
    for core in range(2):
        for y in range(4):
            for x in range(4):
                def device(step):
                    to_y = (y + step) % 4 if axis == "y" else y
                    to_x = (x + step) % 4 if axis == "x" else x
                    return (((x + y) % 2) * 4 + to_y) * 4 + to_x

                source = (core * 4 + y) * 4 + x
                own = (x + y) % 2 == core
                near.append((source, device(-1 if own else 0)))
                far.append((source, device(1 if own else 2)))
    axes = ("core", "y", "x")
    return lax.ppermute(block, axes, near), lax.ppermute(block, axes, far)


def on_device(
    hidden_states,
    ln_attn_gain,
    w_qkv,
    output_weight,
    ln_final_gain,
    dense_weight,
    decoder_weight,
    decoder_bias,
    seq_tokens,
    seq_lengths,
    copy_sequence,
    mask_code,
    copy_owner,
):
    _, span, feature = hidden_states.shape
    size = output_weight.shape[0]
    masks = mask_code.shape[1]
    core = lax.axis_index("core")
    member = lax.axis_index(("y", "x"))
    right = (lax.axis_index("x") + lax.axis_index("y")) % 2 == core
    place = jnp.stack([lax.axis_index("z"), core, member, right.astype(core.dtype)])
    place = place.astype(jnp.int32)
    cos_table, sin_table = (jnp.asarray(t) for t in rotary_tables(span, size))
    shape = jax.ShapeDtypeStruct

    def prepare_call(mine, states):
        def kernel(*refs):
            prepare_kernel(mine, *refs)

        return call(
            kernel,
            [
                shape((span, feature), BF16),
                shape((masks, feature), BF16),
                shape((masks, feature), F32),
                shape((masks, 128), F32),
                shape((masks, 128), F32),
                shape((masks, 128), jnp.int32),
            ],
            3,
            (
                place, copy_sequence, seq_lengths, mask_code.T, seq_tokens, states,
                ln_attn_gain.reshape(1, -1), cos_table, sin_table,
            ),
            flops=4 * masks * span * feature + 10 * span * feature,
        )

    def keys_call(ready, blocks):
        heads = len(blocks)

        def kernel(*refs):
            keys_kernel(
                *refs[:3], refs[3:5], refs[5:7], *refs[7:9], refs[9:11], refs[11:13],
                refs[13 : 13 + heads], refs[13 + heads],
            )

        return call(
            kernel,
            shape((2, heads * masks, span), BF16),
            3,
            (place, copy_sequence, seq_lengths, *(r[0] for r in ready), *(r[1] for r in ready),
             cos_table, sin_table, *(r[3] for r in ready), *(r[4] for r in ready), *blocks),
            flops=4 * span * feature * 256,
            exps=2 * heads * masks * span,
        )

    def values_call(ready, blocks):
        heads = len(blocks)

        def kernel(*refs):
            values_kernel(refs[:2], refs[2 : 2 + heads], refs[2 + heads])

        return call(
            kernel,
            shape((2, span, heads * size), BF16),
            0,
            (*(r[0] for r in ready), *blocks),
            flops=4 * span * feature * 256,
        )

    states = hidden_states[0]
    key_block, value_block = pack(jnp.transpose(w_qkv[:, 0, :]), output_weight[:, 0, :])
    key_low, key_high = gather_line(key_block, "x")
    value_low, value_high = gather_line(value_block, "y")
    states_other = swap(states)
    mine = prepare_call(True, states)
    key_low, key_high = after(key_low, mine[0]), after(key_high, mine[0])
    value_low, value_high = after(value_low, mine[0]), after(value_high, mine[0])
    key_ahead = [pull(key_low, "y", 1)]
    key_behind = [pull(key_high, "y", 3)]
    value_ahead = [pull(value_low, "x", 1)]
    value_behind = [pull(value_high, "x", 3)]
    key_ahead.append(pull(key_high, "y", 1))
    key_behind.insert(0, pull(key_low, "y", 3))
    value_ahead.append(pull(value_high, "x", 1))
    value_behind.insert(0, pull(value_low, "x", 3))
    other = prepare_call(False, states_other)
    ready = (mine, other)
    own_probs = keys_call(ready, (key_low, key_high))
    key_far = (
        pull(after(key_ahead[0], own_probs), "y", 1),
        pull(after(key_behind[1], own_probs), "y", 3),
    )
    value_far = (
        pull(after(value_ahead[0], own_probs), "x", 1),
        pull(after(value_behind[1], own_probs), "x", 3),
    )
    own_values = values_call(ready, (value_low, value_high))
    near_probs = keys_call(ready, (*key_ahead, *key_behind))
    near_values = values_call(ready, (*value_ahead, *value_behind))
    key_far = tuple(after(b, near_probs, near_values) for b in key_far)
    far_probs = keys_call(ready, key_far)
    far_values = values_call(ready, value_far)
    probs = (own_probs, near_probs, far_probs)
    values = (own_values, near_values, far_values)
    value_blocks = (value_low, value_high, *value_ahead, *value_behind, *value_far)

    def mix(*refs):
        mix_kernel(refs[0], refs[1:4], refs[4:7], refs[7:15], refs[15])

    partial = call(
        mix,
        shape((2 * masks, feature), F32),
        1,
        (place, *probs, *values, *value_blocks),
        flops=4 * masks * feature * 8 * size,
    )

    def score(*refs):
        score_kernel(*refs[:2], refs[2:4], *refs[4:6], refs[6:8], *refs[8:])

    placed = call(
        score,
        shape((128, 64), F32),
        2,
        (
            place, copy_owner, mine[2], other[2], partial, swap(partial), mine[5], other[5],
            ln_final_gain.reshape(1, -1), decoder_bias.reshape(1, -1), dense_weight,
            decoder_weight.T,
        ),
        flops=4 * masks * feature * feature,
    )
    arrived = lax.all_to_all(placed, ("z", "y", "x"), 0, 0, tiled=True)
    return jnp.sum(arrived, axis=0).reshape(16, 4)


def solution(mesh):
    fine = Mesh(mesh.devices.reshape(8, 2, 4, 4), ("z", "core", "y", "x"))
    dp, mp = ("z", "core"), ("y", "x")
    placed = (
        P(("z", "core", "y", "x"), None, None),
        P(),
        P(None, mp, None),
        P(None, mp, None),
        P(),
        P(),
        P(),
        P(),
        P(),
        P(),
        P(),
        P(),
        P(),
    )
    return jax.shard_map(
        on_device, mesh=fine, in_specs=placed, out_specs=P(dp, mp), check_vma=False
    )
```

```python
import numpy as np
import jax
import jax.numpy as jnp
from jax import lax
from jax.experimental import pallas as pl
from jax.experimental.pallas import tpu as pltpu
from jax.sharding import Mesh, PartitionSpec as P

epsilon = 1e-05
F32 = jnp.float32
BF16 = jnp.bfloat16


def rotary_tables(seq_span, head_size):
    half = head_size // 2
    power = (np.arange(half, dtype=np.float32) * np.float32(2.0 / head_size)).astype(np.float32)
    frequency = (np.float32(1.0) / np.power(np.float32(10000.0), power)).astype(np.float32)
    angles = (np.arange(seq_span, dtype=np.float32)[:, None] * frequency[None, :]).astype(np.float32)
    cosine = np.cos(angles.astype(np.float64)).astype(np.float32)
    sine = np.sin(angles.astype(np.float64)).astype(np.float32)
    cos_table = np.concatenate([cosine] * 4, axis=1)
    sin_table = np.concatenate([-sine, sine] * 2, axis=1)
    return np.concatenate([cos_table, sin_table], axis=1)


def nt_dot(a, b):
    return lax.dot_general(a, b, (((1,), (1,)), ((), ())), preferred_element_type=F32)


def nn_dot(a, b, **options):
    return lax.dot_general(a, b, (((1,), (0,)), ((), ())), preferred_element_type=F32, **options)


def rotate(part, table, half):
    cos_table, sin_table = table[:, :128], table[:, 128:]
    width = part.shape[1]
    lane = lax.broadcasted_iota(jnp.int32, part.shape, 1) % (2 * half)
    turned = jnp.where(
        lane < half,
        pltpu.roll(part, width - half, 1),
        pltpu.roll(part, half, 1),
    )
    return part * cos_table + turned * sin_table


IN_PLACE = pl.BlockSpec(memory_space=pltpu.MemorySpace.HBM)
ON_CHIP = pl.BlockSpec(memory_space=pltpu.MemorySpace.VMEM)


def call(kernel, outs, args, n_any=0, scratch=(), flops=0, exps=0, vmem=24 * 1024 * 1024):
    moved = sum(a.size * a.dtype.itemsize for a in list(args) + jax.tree.leaves(outs))
    place = pltpu.with_memory_space_constraint
    args = [place(a, pltpu.HBM) if i < n_any else a for i, a in enumerate(args)]
    return pl.pallas_call(
        kernel,
        out_shape=outs,
        in_specs=[IN_PLACE] * n_any + [ON_CHIP] * (len(args) - n_any),
        out_specs=jax.tree.map(lambda _: ON_CHIP, outs),
        scratch_shapes=list(scratch),
        cost_estimate=pl.CostEstimate(flops=flops, transcendentals=exps, bytes_accessed=moved),
        compiler_params=pltpu.CompilerParams(vmem_limit_bytes=vmem),
    )(*args)


def pack_kernel(turned_ref, out_ref, key_ref, value_ref, sems):
    size = out_ref.shape[0]
    copies = (
        pltpu.make_async_copy(turned_ref.at[: 2 * size], key_ref, sems.at[0]),
        pltpu.make_async_copy(turned_ref.at[2 * size :], value_ref.at[:size], sems.at[1]),
        pltpu.make_async_copy(out_ref, value_ref.at[size:], sems.at[2]),
    )
    for copy in copies:
        copy.start()
    for copy in copies:
        copy.wait()


def pack(turned, out_weight):
    size, feature = out_weight.shape
    return call(
        pack_kernel,
        [jax.ShapeDtypeStruct((2 * size, feature), BF16)] * 2,
        (turned, out_weight),
        n_any=2,
        scratch=[pltpu.SemaphoreType.DMA((3,))],
    )


def first(mask, values):
    picked = jnp.sum(jnp.where(mask, values, 0), axis=1, keepdims=True)
    return jnp.sum(picked, axis=0, keepdims=True)


def prepare_kernel(mine, *refs):
    n = 8 if mine else 7
    sources, refs = refs[:n], refs[n:]
    if not mine:
        states_ref, refs = refs[0], refs[1:]
    normed_ref, picked_ref, rows_ref, qtable_ref, meta_ref = refs[:5]
    refs = refs[5:]
    if mine:
        table_ref, refs = refs[0], refs[1:]
    scratch, sems = refs[:-1], refs[-1]
    if mine:
        targets = (*scratch[:6], table_ref, scratch[6])
        states_ref = scratch[6]
    else:
        targets = scratch
        table_ref = scratch[6]
    copies = [
        pltpu.make_async_copy(source, target, sems.at[i])
        for i, (source, target) in enumerate(zip(sources, targets))
    ]
    for copy in copies:
        copy.start()
    for copy in copies:
        copy.wait()
    sequence_ref, length_ref, owner_ref, codes_ref, tokens_ref, gain_ref = targets[:6]
    span = states_ref.shape[0]
    masks = codes_ref.shape[0]
    core = lax.axis_index("core")
    core = core if mine else 1 - core
    copy = ((lax.axis_index("z") * 2 + core) * 4 + lax.axis_index("y")) * 4 + lax.axis_index("x")

    def numbers(count):
        return lax.broadcasted_iota(jnp.int32, (1, count), 1)

    own = numbers(codes_ref.shape[1]) == copy
    sequence = first(own, sequence_ref[...].reshape(1, -1))
    owner = first(own, owner_ref[...].reshape(1, -1))
    length = first(numbers(length_ref.shape[0]) == sequence, length_ref[...].reshape(1, -1))
    codes = jnp.sum(jnp.where(own, codes_ref[...], 0), axis=1, keepdims=True)
    quotient = jnp.floor(codes.astype(F32) / length.astype(F32)).astype(jnp.int32)
    positions = codes - quotient * length
    positions = jnp.where(positions < 0, positions + length, positions)
    positions = jnp.where(positions >= length, positions - length, positions)
    hit = lax.broadcasted_iota(jnp.int32, (masks, span), 1) == positions
    line = lax.broadcasted_iota(jnp.int32, tokens_ref.shape, 0)
    tokens = jnp.sum(jnp.where(line == sequence, tokens_ref[...], 0), axis=0, keepdims=True)
    targets = jnp.sum(jnp.where(hit, tokens, 0), axis=1, keepdims=True)
    lane = lax.broadcasted_iota(jnp.int32, meta_ref.shape, 1)
    meta_ref[...] = jnp.where(lane == 0, targets, jnp.where(lane == 1, length, owner))
    hot = hit.astype(F32)
    qtable_ref[...] = nn_dot(hot, table_ref[...], precision=lax.Precision.HIGHEST)
    hot = hot.astype(BF16)
    gain = gain_ref[...].reshape(1, -1)
    block = 128

    def step(i, carry):
        at = pl.multiple_of(i * block, block)
        values = states_ref[pl.ds(at, block), :].astype(F32)
        average = jnp.mean(values, axis=1, keepdims=True)
        centred = values - average
        variance = jnp.mean(centred * centred, axis=1, keepdims=True)
        normed_ref[pl.ds(at, block), :] = (
            centred * lax.rsqrt(variance + epsilon) * gain
        ).astype(BF16)
        return carry

    lax.fori_loop(0, span // block, step, 0)
    rows_ref[...] = nn_dot(hot, states_ref[...])
    picked_ref[...] = nn_dot(hot, normed_ref[...]).astype(BF16)


def keys_kernel(
    table_ref, normed_refs, picked_refs, qtable_refs, meta_refs, block_refs, probs_ref
):
    size = block_refs[0].shape[0] // 2
    masks = picked_refs[0].shape[0]
    heads = len(block_refs)
    key_weight = jnp.concatenate([r[size:, :] for r in block_refs], axis=0)
    query_weight = jnp.concatenate([r[:size, :] for r in block_refs], axis=0)
    for which in range(2):
        length = meta_refs[which][0:1, 1:2]
        keys = nt_dot(normed_refs[which][...], key_weight)
        queries = nt_dot(picked_refs[which][...], query_weight) * 0.125
        turned_keys, turned_queries = [], []
        for i in range(heads // 2):
            lanes = slice(128 * i, 128 * (i + 1))
            turned_keys.append(rotate(keys[:, lanes], table_ref[...], size // 2))
            turned_queries.append(
                rotate(queries[:, lanes], qtable_refs[which][...], size // 2)
            )
        key_rows = jnp.concatenate(turned_keys, axis=1).astype(BF16)
        query_rows = jnp.concatenate(turned_queries, axis=1).astype(BF16)
        spread = jnp.concatenate([query_rows] * heads, axis=0)
        row = lax.broadcasted_iota(jnp.int32, spread.shape, 0) // masks
        lane = lax.broadcasted_iota(jnp.int32, spread.shape, 1) // size
        spread = jnp.where(row == lane, spread, jnp.zeros_like(spread))
        logits = nt_dot(spread, key_rows)
        alive = lax.broadcasted_iota(jnp.int32, logits.shape, 1) < length
        logits = jnp.where(alive, logits, -1e30)
        largest = jnp.max(logits, axis=1, keepdims=True)
        weights = jnp.exp(logits - largest)
        total = jnp.sum(weights, axis=1, keepdims=True)
        probs_ref[which] = (weights * (1.0 / total)).astype(BF16)


def values_kernel(normed_refs, block_refs, values_ref):
    size = block_refs[0].shape[0] // 2
    weight = jnp.concatenate([r[:size, :] for r in block_refs], axis=0)
    for which in range(2):
        values_ref[which] = nt_dot(normed_refs[which][...], weight).astype(BF16)


def mix_kernel(probs_refs, values_refs, block_refs, partial_ref):
    right = (lax.axis_index("x") + lax.axis_index("y")) % 2 == lax.axis_index("core")
    own_probs, near_probs, far_probs = probs_refs
    size = block_refs[0].shape[0] // 2
    masks = own_probs.shape[1] // 2
    columns = ((0,), (1, 3), (2,))

    def rows_of(core, step, which):
        ref = (own_probs, near_probs, far_probs, near_probs)[step]
        start = masks * (which + (2 if step == 3 else 0))
        return ref[core, start : start + masks, :]

    contexts = []
    for core in range(2):
        parts = []
        for values_ref, group in zip(values_refs, columns):
            stack = []
            for column in group:
                which = column // 2
                for i in range(2):
                    even = rows_of(core, (0, 2)[i], which)
                    odd = rows_of(core, (1, 3)[i], which)
                    if column % 2:
                        even, odd = odd, even
                    stack.append(jnp.where(right, even, odd))
            mixed = nn_dot(jnp.concatenate(stack, axis=0), values_ref[core])
            lane = lax.broadcasted_iota(jnp.int32, (masks, mixed.shape[1]), 1) // size
            context = mixed[:masks, :]
            for head in range(1, len(stack)):
                context = jnp.where(
                    lane == head, mixed[masks * head : masks * (head + 1), :], context
                )
            parts.append(context.astype(BF16))
        contexts.append(jnp.concatenate(parts, axis=1))
    weight = jnp.concatenate([r[size:, :] for r in block_refs], axis=0)
    partial_ref[...] = nn_dot(jnp.concatenate(contexts, axis=0), weight)


def score_kernel(
    rows_refs, partial_ref, arrived_ref, meta_refs, gain_ref, bias_ref, dense_ref, decoder_ref,
    placed_ref,
):
    masks = rows_refs[0].shape[0]
    residual = jnp.concatenate(
        [
            rows_refs[0][...] + (partial_ref[:masks, :] + arrived_ref[masks:, :]),
            rows_refs[1][...] + (partial_ref[masks:, :] + arrived_ref[:masks, :]),
        ],
        axis=0,
    )
    targets = jnp.concatenate([r[:, 0:1] for r in meta_refs], axis=0)
    average = jnp.mean(residual, axis=1, keepdims=True)
    centred = residual - average
    variance = jnp.mean(centred * centred, axis=1, keepdims=True)
    normed = (centred * lax.rsqrt(variance + epsilon) * gain_ref[...]).astype(BF16)
    dense = nn_dot(normed, dense_ref[...])
    active = 0.5 * dense * (1.0 + lax.erf(dense * np.float32(0.5**0.5)))
    average = jnp.mean(active, axis=1, keepdims=True)
    centred = active - average
    variance = jnp.mean(centred * centred, axis=1, keepdims=True)
    headed = (centred * lax.rsqrt(variance + epsilon)).astype(BF16)
    logits = nt_dot(headed, decoder_ref[...]) + bias_ref[...]
    largest = jnp.max(logits, axis=1, keepdims=True)
    total = jnp.sum(jnp.exp(logits - largest), axis=1, keepdims=True)
    vocab = lax.broadcasted_iota(jnp.int32, logits.shape, 1)
    chosen = jnp.sum(jnp.where(vocab == targets, logits, 0.0), axis=1, keepdims=True)
    score = chosen - largest - jnp.log(total)
    devices, width = placed_ref.shape
    member = lax.broadcasted_iota(jnp.int32, (devices, masks), 0) % 16
    part = lax.broadcasted_iota(jnp.int32, (devices, masks), 1) // 4
    take = (member == part).astype(F32)
    fits = (
        lax.broadcasted_iota(jnp.int32, (masks, width), 0) % 4
        == lax.broadcasted_iota(jnp.int32, (masks, width), 1) % 4
    )
    layer = lax.broadcasted_iota(jnp.int32, (devices, width), 0) // 16
    slot = lax.broadcasted_iota(jnp.int32, (devices, width), 1) // 4
    wanted = 16 * (2 * layer + lax.axis_index("core")) + slot
    placed = jnp.zeros((devices, width), F32)
    for which in range(2):
        own = jnp.where(fits, score[masks * which : masks * (which + 1), :], 0.0)
        laid = nn_dot(take, own, precision=lax.Precision.HIGHEST)
        placed = jnp.where(wanted == meta_refs[which][0:1, 2:3], laid, placed)
    placed_ref[...] = placed


def pull(array, axis, offset):
    size = lax.axis_size(axis)
    return lax.ppermute(array, axis, [((i + offset) % size, i) for i in range(size)])


def swap(array):
    return lax.ppermute(array, "core", [(0, 1), (1, 0)])


def after(array, *others):
    return lax.optimization_barrier((array, *others))[0]


def gather_line(block, axis):
    near, far = [], []
    for core in range(2):
        for y in range(4):
            for x in range(4):
                def device(step):
                    to_y = (y + step) % 4 if axis == "y" else y
                    to_x = (x + step) % 4 if axis == "x" else x
                    return (((x + y) % 2) * 4 + to_y) * 4 + to_x

                source = (core * 4 + y) * 4 + x
                own = (x + y) % 2 == core
                near.append((source, device(-1 if own else 0)))
                far.append((source, device(1 if own else 2)))
    axes = ("core", "y", "x")
    return lax.ppermute(block, axes, near), lax.ppermute(block, axes, far)


def on_device(
    hidden_states,
    ln_attn_gain,
    w_qkv,
    output_weight,
    ln_final_gain,
    dense_weight,
    decoder_weight,
    decoder_bias,
    seq_tokens,
    seq_lengths,
    copy_sequence,
    mask_code,
    copy_owner,
):
    _, span, feature = hidden_states.shape
    size = output_weight.shape[0]
    masks = mask_code.shape[1]
    table = jnp.asarray(rotary_tables(span, size))
    shape = jax.ShapeDtypeStruct

    def prepare_call(mine, states, table):
        small = [copy_sequence, seq_lengths, copy_owner, mask_code.T, seq_tokens, ln_attn_gain]
        outs = [
            shape((span, feature), BF16),
            shape((masks, feature), BF16),
            shape((masks, feature), F32),
            shape((masks, 256), F32),
            shape((masks, 128), jnp.int32),
        ]
        args = [*small, table, states]
        scratch = [pltpu.VMEM(a.shape, a.dtype) for a in small]
        if mine:
            outs.append(shape(table.shape, F32))
            scratch.append(pltpu.VMEM(states.shape, states.dtype))
        else:
            scratch.append(pltpu.VMEM(table.shape, table.dtype))

        def kernel(*refs):
            prepare_kernel(mine, *refs)

        return call(
            kernel,
            outs,
            args,
            n_any=8 if mine else 7,
            scratch=[*scratch, pltpu.SemaphoreType.DMA((8,))],
            flops=4 * masks * span * feature + 10 * span * feature,
        )

    def keys_call(ready, blocks):
        heads = len(blocks)

        def kernel(*refs):
            keys_kernel(
                refs[0], refs[1:3], refs[3:5], refs[5:7], refs[7:9], refs[9 : 9 + heads],
                refs[9 + heads],
            )

        per_copy = [r[i] for i in (0, 1, 3, 4) for r in ready]
        return call(
            kernel,
            shape((2, heads * masks, span), BF16),
            (ready[0][5], *per_copy, *blocks),
            flops=4 * span * feature * 256,
            exps=2 * heads * masks * span,
        )

    def values_call(ready, blocks):
        heads = len(blocks)

        def kernel(*refs):
            values_kernel(refs[:2], refs[2 : 2 + heads], refs[2 + heads])

        return call(
            kernel,
            shape((2, span, heads * size), BF16),
            (*(r[0] for r in ready), *blocks),
            flops=4 * span * feature * 256,
        )

    states = hidden_states[0]
    key_block, value_block = pack(jnp.transpose(w_qkv[:, 0, :]), output_weight[:, 0, :])
    key_low, key_high = gather_line(key_block, "x")
    value_low, value_high = gather_line(value_block, "y")
    states_other = swap(states)
    mine = prepare_call(True, states, table)
    key_ahead_low = pull(after(key_low, mine[0]), "y", 1)
    key_behind_high = pull(after(key_high, mine[0]), "y", 3)
    value_ahead_low = pull(after(value_low, mine[0]), "x", 1)
    value_behind_high = pull(after(value_high, mine[0]), "x", 3)
    other = prepare_call(False, after(states_other, mine[0]), table)
    ready = (mine, other)
    key_ahead_high = pull(after(key_high, key_ahead_low, other[0]), "y", 1)
    key_behind_low = pull(after(key_low, key_behind_high, other[0]), "y", 3)
    value_ahead_high = pull(after(value_high, value_ahead_low, other[0]), "x", 1)
    value_behind_low = pull(after(value_low, value_behind_high, other[0]), "x", 3)
    own_probs = keys_call(ready, (key_low, key_high))
    own_values = values_call(ready, (value_low, value_high))
    key_far = (
        pull(after(key_ahead_low, key_ahead_high, own_probs, own_values), "y", 1),
        pull(after(key_behind_high, key_behind_low, own_probs, own_values), "y", 3),
    )
    value_far = (
        pull(after(value_ahead_low, value_ahead_high, own_probs, own_values), "x", 1),
        pull(after(value_behind_high, value_behind_low, own_probs, own_values), "x", 3),
    )
    key_near = (key_ahead_low, key_ahead_high, key_behind_low, key_behind_high)
    value_near = (value_ahead_low, value_ahead_high, value_behind_low, value_behind_high)
    near_probs = keys_call(ready, key_near)
    near_values = values_call(ready, value_near)
    key_far = tuple(after(b, near_probs, near_values) for b in key_far)
    far_probs = keys_call(ready, key_far)
    far_values = values_call(ready, value_far)
    probs = (own_probs, near_probs, far_probs)
    values = (own_values, near_values, far_values)
    value_blocks = (value_low, value_high, *value_near, *value_far)

    def mix(*refs):
        mix_kernel(refs[:3], refs[3:6], refs[6:14], refs[14])

    partial = call(
        mix,
        shape((2 * masks, feature), F32),
        (*probs, *values, *value_blocks),
        flops=4 * masks * feature * 8 * size,
    )

    def score(*refs):
        score_kernel(refs[:2], *refs[2:4], refs[4:6], *refs[6:])

    placed = call(
        score,
        shape((128, 64), F32),
        (
            mine[2], other[2], partial, swap(partial), mine[4], other[4],
            ln_final_gain.reshape(1, -1), decoder_bias.reshape(1, -1), dense_weight,
            decoder_weight.T,
        ),
        flops=4 * masks * feature * feature,
    )
    arrived = lax.all_to_all(placed, ("z", "y", "x"), 0, 0, tiled=True)
    return jnp.sum(arrived, axis=0).reshape(16, 4)


def solution(mesh):
    fine = Mesh(mesh.devices.reshape(8, 2, 4, 4), ("z", "core", "y", "x"))
    dp, mp = ("z", "core"), ("y", "x")
    placed = (
        P(("z", "core", "y", "x"), None, None),
        P(),
        P(None, mp, None),
        P(None, mp, None),
        P(),
        P(),
        P(),
        P(),
        P(),
        P(),
        P(),
        P(),
        P(),
    )
    return jax.shard_map(
        on_device, mesh=fine, in_specs=placed, out_specs=P(dp, mp), check_vma=False
    )
```

```python
import numpy as np
import jax
import jax.numpy as jnp
from jax import lax
from jax.experimental import pallas as pl
from jax.experimental.pallas import tpu as pltpu
from jax.sharding import Mesh, PartitionSpec as P

epsilon = 1e-05
F32 = jnp.float32
BF16 = jnp.bfloat16


def rotary_tables(seq_span, head_size):
    half = head_size // 2
    power = (np.arange(half, dtype=np.float32) * np.float32(2.0 / head_size)).astype(np.float32)
    frequency = (np.float32(1.0) / np.power(np.float32(10000.0), power)).astype(np.float32)
    angles = (np.arange(seq_span, dtype=np.float32)[:, None] * frequency[None, :]).astype(np.float32)
    cosine = np.cos(angles.astype(np.float64)).astype(np.float32)
    sine = np.sin(angles.astype(np.float64)).astype(np.float32)
    wide = np.concatenate([cosine] * 4 + [-sine, sine] * 2, axis=1)
    rest = np.concatenate([cosine, sine], axis=1)
    parts = []
    for _ in range(3):
        parts.append(rest.astype(BF16))
        rest = rest - parts[-1].astype(np.float32)
    parts.append(np.zeros_like(parts[0]))
    return wide, np.concatenate(parts, axis=1)


def nt_dot(a, b):
    return lax.dot_general(a, b, (((1,), (1,)), ((), ())), preferred_element_type=F32)


def nn_dot(a, b, **options):
    return lax.dot_general(a, b, (((1,), (0,)), ((), ())), preferred_element_type=F32, **options)


def rotate(part, table, half):
    cos_table, sin_table = table[:, :128], table[:, 128:]
    width = part.shape[1]
    lane = lax.broadcasted_iota(jnp.int32, part.shape, 1) % (2 * half)
    turned = jnp.where(
        lane < half,
        pltpu.roll(part, width - half, 1),
        pltpu.roll(part, half, 1),
    )
    return part * cos_table + turned * sin_table


IN_PLACE = pl.BlockSpec(memory_space=pltpu.MemorySpace.HBM)
ON_CHIP = pl.BlockSpec(memory_space=pltpu.MemorySpace.VMEM)


def call(kernel, outs, args, n_any=0, scratch=(), flops=0, exps=0, vmem=24 * 1024 * 1024):
    moved = sum(a.size * a.dtype.itemsize for a in list(args) + jax.tree.leaves(outs))
    place = pltpu.with_memory_space_constraint
    args = [place(a, pltpu.HBM) if i < n_any else a for i, a in enumerate(args)]
    return pl.pallas_call(
        kernel,
        out_shape=outs,
        in_specs=[IN_PLACE] * n_any + [ON_CHIP] * (len(args) - n_any),
        out_specs=jax.tree.map(lambda _: ON_CHIP, outs),
        scratch_shapes=list(scratch),
        cost_estimate=pl.CostEstimate(flops=flops, transcendentals=exps, bytes_accessed=moved),
        compiler_params=pltpu.CompilerParams(vmem_limit_bytes=vmem),
    )(*args)


def pack_kernel(turned_ref, out_ref, key_ref, value_ref, sems):
    size = out_ref.shape[0]
    copies = (
        pltpu.make_async_copy(turned_ref.at[: 2 * size], key_ref, sems.at[0]),
        pltpu.make_async_copy(turned_ref.at[2 * size :], value_ref.at[:size], sems.at[1]),
        pltpu.make_async_copy(out_ref, value_ref.at[size:], sems.at[2]),
    )
    for copy in copies:
        copy.start()
    for copy in copies:
        copy.wait()


def pack(turned, out_weight):
    size, feature = out_weight.shape
    return call(
        pack_kernel,
        [jax.ShapeDtypeStruct((2 * size, feature), BF16)] * 2,
        (turned, out_weight),
        n_any=2,
        scratch=[pltpu.SemaphoreType.DMA((3,))],
    )


def first(mask, values):
    picked = jnp.sum(jnp.where(mask, values, 0), axis=1, keepdims=True)
    return jnp.sum(picked, axis=0, keepdims=True)


def norm_rows(values, gain):
    average = jnp.mean(values, axis=1, keepdims=True)
    centred = values - average
    variance = jnp.mean(centred * centred, axis=1, keepdims=True)
    return (centred * lax.rsqrt(variance + epsilon) * gain).astype(BF16)


def prepare_kernel(mine, small_refs, pick_ref, states_from, table_from, out_refs, scratch, sems):
    normed_ref, picked_ref, rows_ref, qtable_ref, meta_ref = out_refs[:5]
    copies = [
        pltpu.make_async_copy(source, target, sems.at[i])
        for i, (source, target) in enumerate(zip((*small_refs, pick_ref), scratch))
    ]
    late = []
    if mine:
        states_ref = scratch[7]
        late = [
            pltpu.make_async_copy(states_from, states_ref, sems.at[7]),
            pltpu.make_async_copy(table_from, out_refs[5], sems.at[8]),
        ]
    else:
        states_ref = states_from
    for copy in (*copies, *late):
        copy.start()
    sequence_ref, length_ref, owner_ref, codes_ref, tokens_ref, gain_ref, pick_ref = scratch[:7]
    span, feature = normed_ref.shape
    masks = codes_ref.shape[0]
    core = lax.axis_index("core")
    core = core if mine else 1 - core
    copy_id = (
        (lax.axis_index("z") * 2 + core) * 4 + lax.axis_index("y")
    ) * 4 + lax.axis_index("x")
    copies[5].wait()
    block = 16

    def norm_all():
        gain = gain_ref[...].reshape(1, -1)

        def step(i, carry):
            at = pl.multiple_of(i * block, block)
            values = states_ref[pl.ds(at, block), :].astype(F32)
            normed_ref[pl.ds(at, block), :] = norm_rows(values, gain)
            return carry

        lax.fori_loop(0, span // block, step, 0, unroll=20)

    if not mine:
        norm_all()
    for copy in (*copies[:5], copies[6]):
        copy.wait()

    def numbers(count):
        return lax.broadcasted_iota(jnp.int32, (1, count), 1)

    own = numbers(codes_ref.shape[1]) == copy_id
    sequence = first(own, sequence_ref[...].reshape(1, -1))
    owner = first(own, owner_ref[...].reshape(1, -1))
    length = first(numbers(length_ref.shape[0]) == sequence, length_ref[...].reshape(1, -1))
    codes = jnp.sum(jnp.where(own, codes_ref[...], 0), axis=1, keepdims=True)
    quotient = jnp.floor(codes.astype(F32) / length.astype(F32)).astype(jnp.int32)
    positions = codes - quotient * length
    positions = jnp.where(positions < 0, positions + length, positions)
    positions = jnp.where(positions >= length, positions - length, positions)
    hit = lax.broadcasted_iota(jnp.int32, (masks, span), 1) == positions
    line = lax.broadcasted_iota(jnp.int32, tokens_ref.shape, 0)
    tokens = jnp.sum(jnp.where(line == sequence, tokens_ref[...], 0), axis=0, keepdims=True)
    targets = jnp.sum(jnp.where(hit, tokens, 0), axis=1, keepdims=True)
    lane = lax.broadcasted_iota(jnp.int32, meta_ref.shape, 1)
    meta_ref[...] = jnp.where(lane == 0, targets, jnp.where(lane == 1, length, owner))
    hot = hit.astype(F32).astype(BF16)
    picks = nn_dot(hot, pick_ref[...])
    wide = picks.shape[1] // 4
    picks = picks[:, :wide] + picks[:, wide : 2 * wide] + picks[:, 2 * wide : 3 * wide]
    cosine, sine = picks[:, : wide // 2], picks[:, wide // 2 :]
    qtable_ref[...] = jnp.concatenate([cosine] * 4 + [-sine, sine] * 2, axis=1)
    for copy in late:
        copy.wait()
    if mine:
        norm_all()
    rows = nn_dot(hot, states_ref[...])
    rows_ref[...] = rows
    picked_ref[...] = norm_rows(rows, gain_ref[...].reshape(1, -1))


def attend(table_ref, normed_refs, picked_refs, qtable_refs, meta_refs, key_refs, value_refs):
    size = key_refs[0].shape[0] // 2
    masks = picked_refs[0].shape[0]
    heads = len(key_refs)
    width = heads * size
    weight = jnp.concatenate(
        [r[size:, :] for r in key_refs] + [r[:size, :] for r in value_refs], axis=0
    )
    query_weight = jnp.concatenate([r[:size, :] for r in key_refs], axis=0)
    picked = jnp.concatenate([r[...] for r in picked_refs], axis=0)
    queries = nt_dot(picked, query_weight) * 0.125
    results = []
    for which in range(2):
        length = meta_refs[which][0:1, 1:2]
        projected = nt_dot(normed_refs[which][...], weight)
        own = queries[masks * which : masks * (which + 1), :]
        turned_keys, turned_queries = [], []
        for i in range(heads // 2):
            lanes = slice(128 * i, 128 * (i + 1))
            turned_keys.append(rotate(projected[:, lanes], table_ref[...], size // 2))
            turned_queries.append(rotate(own[:, lanes], qtable_refs[which][...], size // 2))
        key_rows = jnp.concatenate(turned_keys, axis=1).astype(BF16)
        query_rows = jnp.concatenate(turned_queries, axis=1).astype(BF16)
        spread = jnp.concatenate([query_rows] * heads, axis=0)
        row = lax.broadcasted_iota(jnp.int32, spread.shape, 0) // masks
        lane = lax.broadcasted_iota(jnp.int32, spread.shape, 1) // size
        spread = jnp.where(row == lane, spread, jnp.zeros_like(spread))
        logits = nt_dot(spread, key_rows)
        alive = lax.broadcasted_iota(jnp.int32, logits.shape, 1) < length
        logits = jnp.where(alive, logits, -1e30)
        largest = jnp.max(logits, axis=1, keepdims=True)
        weights = jnp.exp(logits - largest)
        total = jnp.sum(weights, axis=1, keepdims=True)
        probs = (weights * (1.0 / total)).astype(BF16)
        results.append((probs, projected[:, width:].astype(BF16)))
    return results


def attend_kernel(*refs):
    inputs, (probs_ref, values_ref) = refs[:-2], refs[-2:]
    for which, (probs, values) in enumerate(attend(*inputs)):
        probs_ref[which] = probs
        values_ref[which] = values


def mix_kernel(probs_refs, values_refs, block_refs, inputs, partial_ref):
    last = attend(*inputs)
    right = (lax.axis_index("x") + lax.axis_index("y")) % 2 == lax.axis_index("core")
    own_probs, near_probs = probs_refs
    size = block_refs[0].shape[0] // 2
    masks = own_probs.shape[1] // 2

    def rows_of(copy, step, which):
        start = masks * (which + (2 if step == 3 else 0))
        if step == 2:
            return last[copy][0][start : start + masks, :]
        ref = near_probs if step % 2 else own_probs
        return ref[copy, start : start + masks, :]

    contexts = []
    for copy in range(2):
        parts = []
        groups = (
            (values_refs[0][copy], (0,)),
            (values_refs[1][copy], (1, 3)),
            (last[copy][1], (2,)),
        )
        for values, columns in groups:
            stack = []
            for column in columns:
                which = column // 2
                for i in range(2):
                    even = rows_of(copy, (0, 2)[i], which)
                    odd = rows_of(copy, (1, 3)[i], which)
                    if column % 2:
                        even, odd = odd, even
                    stack.append(jnp.where(right, even, odd))
            mixed = nn_dot(jnp.concatenate(stack, axis=0), values)
            lane = lax.broadcasted_iota(jnp.int32, (masks, mixed.shape[1]), 1) // size
            context = mixed[:masks, :]
            for head in range(1, len(stack)):
                context = jnp.where(
                    lane == head, mixed[masks * head : masks * (head + 1), :], context
                )
            parts.append(context.astype(BF16))
        contexts.append(jnp.concatenate(parts, axis=1))
    weight = jnp.concatenate([r[size:, :] for r in block_refs], axis=0)
    partial_ref[...] = nn_dot(jnp.concatenate(contexts, axis=0), weight)


def score_kernel(
    rows_refs, partial_ref, arrived_ref, meta_refs, gain_ref, bias_ref, dense_ref, decoder_ref,
    placed_ref,
):
    masks = rows_refs[0].shape[0]
    residual = jnp.concatenate(
        [
            rows_refs[0][...] + (partial_ref[:masks, :] + arrived_ref[masks:, :]),
            rows_refs[1][...] + (partial_ref[masks:, :] + arrived_ref[:masks, :]),
        ],
        axis=0,
    )
    targets = jnp.concatenate([r[:, 0:1] for r in meta_refs], axis=0)
    average = jnp.mean(residual, axis=1, keepdims=True)
    centred = residual - average
    variance = jnp.mean(centred * centred, axis=1, keepdims=True)
    normed = (centred * lax.rsqrt(variance + epsilon) * gain_ref[...]).astype(BF16)
    dense = nn_dot(normed, dense_ref[...])
    active = 0.5 * dense * (1.0 + lax.erf(dense * np.float32(0.5**0.5)))
    average = jnp.mean(active, axis=1, keepdims=True)
    centred = active - average
    variance = jnp.mean(centred * centred, axis=1, keepdims=True)
    headed = (centred * lax.rsqrt(variance + epsilon)).astype(BF16)
    logits = nt_dot(headed, decoder_ref[...]) + bias_ref[...]
    largest = jnp.max(logits, axis=1, keepdims=True)
    total = jnp.sum(jnp.exp(logits - largest), axis=1, keepdims=True)
    vocab = lax.broadcasted_iota(jnp.int32, logits.shape, 1)
    chosen = jnp.sum(jnp.where(vocab == targets, logits, 0.0), axis=1, keepdims=True)
    score = chosen - largest - jnp.log(total)
    devices, width = placed_ref.shape
    member = lax.broadcasted_iota(jnp.int32, (devices, masks), 0) % 16
    part = lax.broadcasted_iota(jnp.int32, (devices, masks), 1) // 4
    take = (member == part).astype(F32)
    fits = (
        lax.broadcasted_iota(jnp.int32, (masks, width), 0) % 4
        == lax.broadcasted_iota(jnp.int32, (masks, width), 1) % 4
    )
    layer = lax.broadcasted_iota(jnp.int32, (devices, width), 0) // 16
    slot = lax.broadcasted_iota(jnp.int32, (devices, width), 1) // 4
    wanted = 16 * (2 * layer + lax.axis_index("core")) + slot
    placed = jnp.zeros((devices, width), F32)
    for which in range(2):
        own = jnp.where(fits, score[masks * which : masks * (which + 1), :], 0.0)
        laid = nn_dot(take, own, precision=lax.Precision.HIGHEST)
        placed = jnp.where(wanted == meta_refs[which][0:1, 2:3], laid, placed)
    placed_ref[...] = placed


def pull(array, axis, offset):
    size = lax.axis_size(axis)
    return lax.ppermute(array, axis, [((i + offset) % size, i) for i in range(size)])


def swap(array):
    return lax.ppermute(array, "core", [(0, 1), (1, 0)])


def after(array, *others):
    return lax.optimization_barrier((array, *others))[0]


def gather_line(block, axis):
    near, far = [], []
    for core in range(2):
        for y in range(4):
            for x in range(4):
                def device(step):
                    to_y = (y + step) % 4 if axis == "y" else y
                    to_x = (x + step) % 4 if axis == "x" else x
                    return (((x + y) % 2) * 4 + to_y) * 4 + to_x

                source = (core * 4 + y) * 4 + x
                own = (x + y) % 2 == core
                near.append((source, device(-1 if own else 0)))
                far.append((source, device(1 if own else 2)))
    axes = ("core", "y", "x")
    return lax.ppermute(block, axes, near), lax.ppermute(block, axes, far)


def on_device(
    hidden_states,
    ln_attn_gain,
    w_qkv,
    output_weight,
    ln_final_gain,
    dense_weight,
    decoder_weight,
    decoder_bias,
    seq_tokens,
    seq_lengths,
    copy_sequence,
    mask_code,
    copy_owner,
):
    _, span, feature = hidden_states.shape
    size = output_weight.shape[0]
    masks = mask_code.shape[1]
    table, pick_table = (jnp.asarray(t) for t in rotary_tables(span, size))
    shape = jax.ShapeDtypeStruct

    def prepare_call(mine, states):
        small = [copy_sequence, seq_lengths, copy_owner, mask_code.T, seq_tokens, ln_attn_gain]
        outs = [
            shape((span, feature), BF16),
            shape((masks, feature), BF16),
            shape((masks, feature), F32),
            shape((masks, 256), F32),
            shape((masks, 128), jnp.int32),
        ]
        args = [*small, pick_table, table, states] if mine else [*small, pick_table, states]
        scratch = [pltpu.VMEM(a.shape, a.dtype) for a in (*small, pick_table)]
        if mine:
            outs.append(shape(table.shape, F32))
            scratch.append(pltpu.VMEM(states.shape, states.dtype))
        n, m = len(args), len(outs)

        def kernel(*refs):
            prepare_kernel(
                mine, refs[:6], refs[6], refs[n - 1], refs[7], refs[n : n + m], refs[n + m : -1],
                refs[-1],
            )

        return call(
            kernel,
            outs,
            args,
            n_any=9 if mine else 7,
            scratch=[*scratch, pltpu.SemaphoreType.DMA((9,))],
            flops=4 * masks * span * feature + 10 * span * feature,
        )

    def attend_args(ready, key_blocks, value_blocks):
        per_copy = [r[i] for i in (0, 1, 3, 4) for r in ready]
        return (ready[0][5], *per_copy, *key_blocks, *value_blocks)

    def attend_refs(refs, heads):
        return (
            refs[0], refs[1:3], refs[3:5], refs[5:7], refs[7:9], refs[9 : 9 + heads],
            refs[9 + heads : 9 + 2 * heads],
        )

    def attend_call(ready, key_blocks, value_blocks):
        heads = len(key_blocks)

        def kernel(*refs):
            attend_kernel(*attend_refs(refs, heads), *refs[-2:])

        return call(
            kernel,
            [
                shape((2, heads * masks, span), BF16),
                shape((2, span, heads * size), BF16),
            ],
            attend_args(ready, key_blocks, value_blocks),
            flops=4 * span * feature * heads * 128,
            exps=2 * heads * masks * span,
        )

    states = hidden_states[0]
    key_block, value_block = pack(jnp.transpose(w_qkv[:, 0, :]), output_weight[:, 0, :])
    key_low, key_high = gather_line(key_block, "x")
    value_low, value_high = gather_line(value_block, "y")
    states_other = swap(states)
    mine = prepare_call(True, states)
    key_ahead_low = pull(after(key_low, mine[0]), "y", 1)
    key_behind_high = pull(after(key_high, mine[0]), "y", 3)
    value_ahead_low = pull(after(value_low, mine[0]), "x", 1)
    value_behind_high = pull(after(value_high, mine[0]), "x", 3)
    other = prepare_call(False, after(states_other, mine[0]))
    ready = (mine, other)
    key_ahead_high = pull(after(key_high, key_ahead_low, other[0]), "y", 1)
    key_behind_low = pull(after(key_low, key_behind_high, other[0]), "y", 3)
    value_ahead_high = pull(after(value_high, value_ahead_low, other[0]), "x", 1)
    value_behind_low = pull(after(value_low, value_behind_high, other[0]), "x", 3)
    own_probs, own_values = attend_call(ready, (key_low, key_high), (value_low, value_high))
    key_far = (
        pull(after(key_ahead_low, key_ahead_high, own_probs, own_values), "y", 1),
        pull(after(key_behind_high, key_behind_low, own_probs, own_values), "y", 3),
    )
    value_far = (
        pull(after(value_ahead_low, value_ahead_high, own_probs, own_values), "x", 1),
        pull(after(value_behind_high, value_behind_low, own_probs, own_values), "x", 3),
    )
    key_near = (key_ahead_low, key_ahead_high, key_behind_low, key_behind_high)
    value_near = (value_ahead_low, value_ahead_high, value_behind_low, value_behind_high)
    near_probs, near_values = attend_call(ready, key_near, value_near)
    key_far = tuple(after(b, near_probs) for b in key_far)
    value_blocks = (value_low, value_high, *value_near)

    def mix(*refs):
        mix_kernel(
            refs[0:2], refs[2:4], (*refs[4:10], *refs[-3:-1]), attend_refs(refs[10:], 2), refs[-1]
        )

    partial = call(
        mix,
        shape((2 * masks, feature), F32),
        (
            own_probs, near_probs, own_values, near_values, *value_blocks,
            *attend_args(ready, key_far, value_far),
        ),
        flops=4 * span * feature * 256 + 4 * masks * feature * 8 * size,
        exps=4 * masks * span,
    )

    def score(*refs):
        score_kernel(refs[:2], *refs[2:4], refs[4:6], *refs[6:])

    placed = call(
        score,
        shape((128, 64), F32),
        (
            mine[2], other[2], partial, swap(partial), mine[4], other[4],
            ln_final_gain.reshape(1, -1), decoder_bias.reshape(1, -1), dense_weight,
            decoder_weight.T,
        ),
        flops=4 * masks * feature * feature,
    )
    arrived = lax.all_to_all(placed, ("z", "y", "x"), 0, 0, tiled=True)
    return jnp.sum(arrived, axis=0).reshape(16, 4)


def solution(mesh):
    fine = Mesh(mesh.devices.reshape(8, 2, 4, 4), ("z", "core", "y", "x"))
    dp, mp = ("z", "core"), ("y", "x")
    placed = (
        P(("z", "core", "y", "x"), None, None),
        P(),
        P(None, mp, None),
        P(None, mp, None),
        P(),
        P(),
        P(),
        P(),
        P(),
        P(),
        P(),
        P(),
        P(),
    )
    return jax.shard_map(
        on_device, mesh=fine, in_specs=placed, out_specs=P(dp, mp), check_vma=False
    )
```

```python
import numpy as np
import jax
import jax.numpy as jnp
from jax import lax
from jax.experimental import pallas as pl
from jax.experimental.pallas import tpu as pltpu
from jax.sharding import Mesh, PartitionSpec as P

epsilon = 1e-05
F32 = jnp.float32
BF16 = jnp.bfloat16


def rotary_tables(seq_span, head_size):
    half = head_size // 2
    power = (np.arange(half, dtype=np.float32) * np.float32(2.0 / head_size)).astype(np.float32)
    frequency = (np.float32(1.0) / np.power(np.float32(10000.0), power)).astype(np.float32)
    angles = (np.arange(seq_span, dtype=np.float32)[:, None] * frequency[None, :]).astype(np.float32)
    cosine = np.cos(angles.astype(np.float64)).astype(np.float32)
    sine = np.sin(angles.astype(np.float64)).astype(np.float32)
    wide = np.concatenate([cosine] * 4 + [-sine, sine] * 2, axis=1)
    rest = np.concatenate([cosine, sine], axis=1)
    parts = []
    for _ in range(3):
        parts.append(rest.astype(BF16))
        rest = rest - parts[-1].astype(np.float32)
    parts.append(np.zeros_like(parts[0]))
    return wide, np.concatenate(parts, axis=1)


def nt_dot(a, b):
    return lax.dot_general(a, b, (((1,), (1,)), ((), ())), preferred_element_type=F32)


def nn_dot(a, b, **options):
    return lax.dot_general(a, b, (((1,), (0,)), ((), ())), preferred_element_type=F32, **options)


def rotate(part, table, half):
    cos_table, sin_table = table[:, :128], table[:, 128:]
    width = part.shape[1]
    lane = lax.broadcasted_iota(jnp.int32, part.shape, 1) % (2 * half)
    turned = jnp.where(
        lane < half,
        pltpu.roll(part, width - half, 1),
        pltpu.roll(part, half, 1),
    )
    return part * cos_table + turned * sin_table


IN_PLACE = pl.BlockSpec(memory_space=pltpu.MemorySpace.HBM)
ON_CHIP = pl.BlockSpec(memory_space=pltpu.MemorySpace.VMEM)


def call(kernel, outs, args, n_any=0, scratch=(), flops=0, exps=0, vmem=24 * 1024 * 1024):
    moved = sum(a.size * a.dtype.itemsize for a in list(args) + jax.tree.leaves(outs))
    place = pltpu.with_memory_space_constraint
    args = [place(a, pltpu.HBM) if i < n_any else a for i, a in enumerate(args)]
    return pl.pallas_call(
        kernel,
        out_shape=outs,
        in_specs=[IN_PLACE] * n_any + [ON_CHIP] * (len(args) - n_any),
        out_specs=jax.tree.map(lambda _: ON_CHIP, outs),
        scratch_shapes=list(scratch),
        cost_estimate=pl.CostEstimate(flops=flops, transcendentals=exps, bytes_accessed=moved),
        compiler_params=pltpu.CompilerParams(vmem_limit_bytes=vmem),
    )(*args)


def pack_kernel(turned_ref, out_ref, key_ref, value_ref, sems):
    size = out_ref.shape[0]
    copies = (
        pltpu.make_async_copy(turned_ref.at[: 2 * size], key_ref, sems.at[0]),
        pltpu.make_async_copy(turned_ref.at[2 * size :], value_ref.at[:size], sems.at[1]),
        pltpu.make_async_copy(out_ref, value_ref.at[size:], sems.at[2]),
    )
    for copy in copies:
        copy.start()
    for copy in copies:
        copy.wait()


def pack(turned, out_weight):
    size, feature = out_weight.shape
    return call(
        pack_kernel,
        [jax.ShapeDtypeStruct((2 * size, feature), BF16)] * 2,
        (turned, out_weight),
        n_any=2,
        scratch=[pltpu.SemaphoreType.DMA((3,))],
    )


def first(mask, values):
    picked = jnp.sum(jnp.where(mask, values, 0), axis=1, keepdims=True)
    return jnp.sum(picked, axis=0, keepdims=True)


def norm_rows(values, gain):
    average = jnp.mean(values, axis=1, keepdims=True)
    centred = values - average
    variance = jnp.mean(centred * centred, axis=1, keepdims=True)
    return (centred * lax.rsqrt(variance + epsilon) * gain).astype(BF16)


def prepare_kernel(mine, small_refs, pick_ref, states_from, table_from, out_refs, scratch, sems):
    normed_ref, picked_ref, rows_ref, qtable_ref, meta_ref = out_refs[:5]
    copies = [
        pltpu.make_async_copy(source, target, sems.at[i])
        for i, (source, target) in enumerate(zip((*small_refs, pick_ref), scratch))
    ]
    late = []
    if mine:
        states_ref = scratch[7]
        late = [
            pltpu.make_async_copy(states_from, states_ref, sems.at[7]),
            pltpu.make_async_copy(table_from, out_refs[5], sems.at[8]),
        ]
    else:
        states_ref = states_from
    for copy in (*copies, *late):
        copy.start()
    sequence_ref, length_ref, owner_ref, codes_ref, tokens_ref, gain_ref, pick_ref = scratch[:7]
    span, feature = normed_ref.shape
    masks = codes_ref.shape[0]
    core = lax.axis_index("core")
    core = core if mine else 1 - core
    copy_id = (
        (lax.axis_index("z") * 2 + core) * 4 + lax.axis_index("y")
    ) * 4 + lax.axis_index("x")
    copies[5].wait()
    block = 16

    def norm_all():
        gain = gain_ref[...].reshape(1, -1)

        def step(i, carry):
            at = pl.multiple_of(i * block, block)
            values = states_ref[pl.ds(at, block), :].astype(F32)
            normed_ref[pl.ds(at, block), :] = norm_rows(values, gain)
            return carry

        lax.fori_loop(0, span // block, step, 0, unroll=20)

    if not mine:
        norm_all()
    for copy in (*copies[:5], copies[6]):
        copy.wait()

    def numbers(count):
        return lax.broadcasted_iota(jnp.int32, (1, count), 1)

    own = numbers(codes_ref.shape[1]) == copy_id
    sequence = first(own, sequence_ref[...].reshape(1, -1))
    owner = first(own, owner_ref[...].reshape(1, -1))
    length = first(numbers(length_ref.shape[0]) == sequence, length_ref[...].reshape(1, -1))
    codes = jnp.sum(jnp.where(own, codes_ref[...], 0), axis=1, keepdims=True)
    quotient = jnp.floor(codes.astype(F32) / length.astype(F32)).astype(jnp.int32)
    positions = codes - quotient * length
    positions = jnp.where(positions < 0, positions + length, positions)
    positions = jnp.where(positions >= length, positions - length, positions)
    hit = lax.broadcasted_iota(jnp.int32, (masks, span), 1) == positions
    line = lax.broadcasted_iota(jnp.int32, tokens_ref.shape, 0)
    tokens = jnp.sum(jnp.where(line == sequence, tokens_ref[...], 0), axis=0, keepdims=True)
    targets = jnp.sum(jnp.where(hit, tokens, 0), axis=1, keepdims=True)
    lane = lax.broadcasted_iota(jnp.int32, meta_ref.shape, 1)
    meta_ref[...] = jnp.where(lane == 0, targets, jnp.where(lane == 1, length, owner))
    hot = hit.astype(F32).astype(BF16)
    picks = nn_dot(hot, pick_ref[...])
    wide = picks.shape[1] // 4
    picks = picks[:, :wide] + picks[:, wide : 2 * wide] + picks[:, 2 * wide : 3 * wide]
    cosine, sine = picks[:, : wide // 2], picks[:, wide // 2 :]
    qtable_ref[...] = jnp.concatenate([cosine] * 4 + [-sine, sine] * 2, axis=1)
    for copy in late:
        copy.wait()
    if mine:
        norm_all()
    rows = nn_dot(hot, states_ref[...])
    rows_ref[...] = rows
    picked_ref[...] = norm_rows(rows, gain_ref[...].reshape(1, -1))


def attend(table_ref, normed_refs, picked_refs, qtable_refs, meta_refs, key_refs, value_refs):
    size = key_refs[0].shape[0] // 2
    masks = picked_refs[0].shape[0]
    heads = len(key_refs)
    width = heads * size
    weight = jnp.concatenate(
        [r[size:, :] for r in key_refs] + [r[:size, :] for r in value_refs], axis=0
    )
    query_weight = jnp.concatenate([r[:size, :] for r in key_refs], axis=0)
    picked = jnp.concatenate([r[...] for r in picked_refs], axis=0)
    queries = nt_dot(picked, query_weight) * 0.125
    results = []
    for which in range(2):
        length = meta_refs[which][0:1, 1:2]
        projected = nt_dot(normed_refs[which][...], weight)
        own = queries[masks * which : masks * (which + 1), :]
        turned_keys, turned_queries = [], []
        for i in range(heads // 2):
            lanes = slice(128 * i, 128 * (i + 1))
            turned_keys.append(rotate(projected[:, lanes], table_ref[...], size // 2))
            turned_queries.append(rotate(own[:, lanes], qtable_refs[which][...], size // 2))
        key_rows = jnp.concatenate(turned_keys, axis=1).astype(BF16)
        query_rows = jnp.concatenate(turned_queries, axis=1).astype(BF16)
        spread = jnp.concatenate([query_rows] * heads, axis=0)
        row = lax.broadcasted_iota(jnp.int32, spread.shape, 0) // masks
        lane = lax.broadcasted_iota(jnp.int32, spread.shape, 1) // size
        spread = jnp.where(row == lane, spread, jnp.zeros_like(spread))
        logits = nt_dot(spread, key_rows)
        alive = lax.broadcasted_iota(jnp.int32, logits.shape, 1) < length
        logits = jnp.where(alive, logits, -1e30)
        largest = jnp.max(logits, axis=1, keepdims=True)
        weights = jnp.exp(logits - largest)
        total = jnp.sum(weights, axis=1, keepdims=True)
        probs = (weights * (1.0 / total)).astype(BF16)
        results.append((probs, projected[:, width:].astype(BF16)))
    return results


def attend_kernel(*refs):
    inputs, (probs_ref, values_ref) = refs[:-2], refs[-2:]
    for which, (probs, values) in enumerate(attend(*inputs)):
        probs_ref[which] = probs
        values_ref[which] = values


def mix_kernel(probs_refs, values_refs, block_refs, inputs, partial_ref):
    last = attend(*inputs)
    right = (lax.axis_index("x") + lax.axis_index("y")) % 2 == lax.axis_index("core")
    own_probs, near_probs = probs_refs
    size = block_refs[0].shape[0] // 2
    masks = own_probs.shape[1] // 2

    def rows_of(copy, step, which):
        start = masks * (which + (2 if step == 3 else 0))
        if step == 2:
            return last[copy][0][start : start + masks, :]
        ref = near_probs if step % 2 else own_probs
        return ref[copy, start : start + masks, :]

    contexts = []
    for copy in range(2):
        parts = []
        groups = (
            (values_refs[0][copy], (0,)),
            (values_refs[1][copy], (1, 3)),
            (last[copy][1], (2,)),
        )
        for values, columns in groups:
            stack = []
            for column in columns:
                which = column // 2
                for i in range(2):
                    even = rows_of(copy, (0, 2)[i], which)
                    odd = rows_of(copy, (1, 3)[i], which)
                    if column % 2:
                        even, odd = odd, even
                    stack.append(jnp.where(right, even, odd))
            mixed = nn_dot(jnp.concatenate(stack, axis=0), values)
            lane = lax.broadcasted_iota(jnp.int32, (masks, mixed.shape[1]), 1) // size
            context = mixed[:masks, :]
            for head in range(1, len(stack)):
                context = jnp.where(
                    lane == head, mixed[masks * head : masks * (head + 1), :], context
                )
            parts.append(context.astype(BF16))
        contexts.append(jnp.concatenate(parts, axis=1))
    weight = jnp.concatenate([r[size:, :] for r in block_refs], axis=0)
    partial_ref[...] = nn_dot(jnp.concatenate(contexts, axis=0), weight)


def score_kernel(
    rows_refs, partial_ref, arrived_ref, meta_refs, gain_ref, bias_ref, dense_ref, decoder_ref,
    placed_ref,
):
    masks = rows_refs[0].shape[0]
    residual = jnp.concatenate(
        [
            rows_refs[0][...] + (partial_ref[:masks, :] + arrived_ref[masks:, :]),
            rows_refs[1][...] + (partial_ref[masks:, :] + arrived_ref[:masks, :]),
        ],
        axis=0,
    )
    targets = jnp.concatenate([r[:, 0:1] for r in meta_refs], axis=0)
    average = jnp.mean(residual, axis=1, keepdims=True)
    centred = residual - average
    variance = jnp.mean(centred * centred, axis=1, keepdims=True)
    normed = (centred * lax.rsqrt(variance + epsilon) * gain_ref[...]).astype(BF16)
    dense = nn_dot(normed, dense_ref[...])
    active = 0.5 * dense * (1.0 + lax.erf(dense * np.float32(0.5**0.5)))
    average = jnp.mean(active, axis=1, keepdims=True)
    centred = active - average
    variance = jnp.mean(centred * centred, axis=1, keepdims=True)
    headed = (centred * lax.rsqrt(variance + epsilon)).astype(BF16)
    logits = nt_dot(headed, decoder_ref[...]) + bias_ref[...]
    largest = jnp.max(logits, axis=1, keepdims=True)
    total = jnp.sum(jnp.exp(logits - largest), axis=1, keepdims=True)
    vocab = lax.broadcasted_iota(jnp.int32, logits.shape, 1)
    chosen = jnp.sum(jnp.where(vocab == targets, logits, 0.0), axis=1, keepdims=True)
    score = chosen - largest - jnp.log(total)
    devices, width = placed_ref.shape
    member = lax.broadcasted_iota(jnp.int32, (devices, masks), 0) % 16
    part = lax.broadcasted_iota(jnp.int32, (devices, masks), 1) // 4
    take = (member == part).astype(F32)
    fits = (
        lax.broadcasted_iota(jnp.int32, (masks, width), 0) % 4
        == lax.broadcasted_iota(jnp.int32, (masks, width), 1) % 4
    )
    layer = lax.broadcasted_iota(jnp.int32, (devices, width), 0) // 16
    slot = lax.broadcasted_iota(jnp.int32, (devices, width), 1) // 4
    wanted = 16 * (2 * layer + lax.axis_index("core")) + slot
    placed = jnp.zeros((devices, width), F32)
    for which in range(2):
        own = jnp.where(fits, score[masks * which : masks * (which + 1), :], 0.0)
        laid = nn_dot(take, own, precision=lax.Precision.HIGHEST)
        placed = jnp.where(wanted == meta_refs[which][0:1, 2:3], laid, placed)
    placed_ref[...] = placed


def pull(array, axis, offset):
    size = lax.axis_size(axis)
    return lax.ppermute(array, axis, [((i + offset) % size, i) for i in range(size)])


def swap(array):
    return lax.ppermute(array, "core", [(0, 1), (1, 0)])


def after(array, *others):
    return lax.optimization_barrier((array, *others))[0]


def gather_line(block, axis):
    near, far = [], []
    for core in range(2):
        for y in range(4):
            for x in range(4):
                def device(step):
                    to_y = (y + step) % 4 if axis == "y" else y
                    to_x = (x + step) % 4 if axis == "x" else x
                    return (((x + y) % 2) * 4 + to_y) * 4 + to_x

                source = (core * 4 + y) * 4 + x
                own = (x + y) % 2 == core
                near.append((source, device(-1 if own else 0)))
                far.append((source, device(1 if own else 2)))
    axes = ("core", "y", "x")
    return lax.ppermute(block, axes, near), lax.ppermute(block, axes, far)


def on_device(
    hidden_states,
    ln_attn_gain,
    w_qkv,
    output_weight,
    ln_final_gain,
    dense_weight,
    decoder_weight,
    decoder_bias,
    seq_tokens,
    seq_lengths,
    copy_sequence,
    mask_code,
    copy_owner,
):
    _, span, feature = hidden_states.shape
    size = output_weight.shape[0]
    masks = mask_code.shape[1]
    table, pick_table = (jnp.asarray(t) for t in rotary_tables(span, size))
    shape = jax.ShapeDtypeStruct

    def prepare_call(mine, states):
        small = [copy_sequence, seq_lengths, copy_owner, mask_code.T, seq_tokens, ln_attn_gain]
        outs = [
            shape((span, feature), BF16),
            shape((masks, feature), BF16),
            shape((masks, feature), F32),
            shape((masks, 256), F32),
            shape((masks, 128), jnp.int32),
        ]
        args = [*small, pick_table, table, states] if mine else [*small, pick_table, states]
        scratch = [pltpu.VMEM(a.shape, a.dtype) for a in (*small, pick_table)]
        if mine:
            outs.append(shape(table.shape, F32))
            scratch.append(pltpu.VMEM(states.shape, states.dtype))
        n, m = len(args), len(outs)

        def kernel(*refs):
            prepare_kernel(
                mine, refs[:6], refs[6], refs[n - 1], refs[7], refs[n : n + m], refs[n + m : -1],
                refs[-1],
            )

        return call(
            kernel,
            outs,
            args,
            n_any=9 if mine else 7,
            scratch=[*scratch, pltpu.SemaphoreType.DMA((9,))],
            flops=4 * masks * span * feature + 10 * span * feature,
        )

    def attend_args(ready, key_blocks, value_blocks):
        per_copy = [r[i] for i in (0, 1, 3, 4) for r in ready]
        return (ready[0][5], *per_copy, *key_blocks, *value_blocks)

    def attend_refs(refs, heads):
        return (
            refs[0], refs[1:3], refs[3:5], refs[5:7], refs[7:9], refs[9 : 9 + heads],
            refs[9 + heads : 9 + 2 * heads],
        )

    def attend_call(ready, key_blocks, value_blocks):
        heads = len(key_blocks)

        def kernel(*refs):
            attend_kernel(*attend_refs(refs, heads), *refs[-2:])

        return call(
            kernel,
            [
                shape((2, heads * masks, span), BF16),
                shape((2, span, heads * size), BF16),
            ],
            attend_args(ready, key_blocks, value_blocks),
            flops=4 * span * feature * heads * 128,
            exps=2 * heads * masks * span,
        )

    states = hidden_states[0]
    key_block, value_block = pack(jnp.transpose(w_qkv[:, 0, :]), output_weight[:, 0, :])
    key_low, key_high = gather_line(key_block, "x")
    value_low, value_high = gather_line(value_block, "y")
    states_other = swap(states)
    key_ahead_low = pull(key_low, "y", 1)
    key_behind_high = pull(key_high, "y", 3)
    value_ahead_low = pull(value_low, "x", 1)
    value_behind_high = pull(value_high, "x", 3)
    mine = prepare_call(True, after(states, key_low, key_high, value_low, value_high))
    key_ahead_high = pull(after(key_high, key_ahead_low, mine[0]), "y", 1)
    key_behind_low = pull(after(key_low, key_behind_high, mine[0]), "y", 3)
    value_ahead_high = pull(after(value_high, value_ahead_low, mine[0]), "x", 1)
    value_behind_low = pull(after(value_low, value_behind_high, mine[0]), "x", 3)
    first_round = (key_ahead_low, key_behind_high, value_ahead_low, value_behind_high)
    other = prepare_call(False, after(states_other, mine[0], *first_round))
    ready = (mine, other)
    key_far = (
        pull(after(key_ahead_low, key_ahead_high, other[0]), "y", 1),
        pull(after(key_behind_high, key_behind_low, other[0]), "y", 3),
    )
    value_far = (
        pull(after(value_ahead_low, value_ahead_high, other[0]), "x", 1),
        pull(after(value_behind_high, value_behind_low, other[0]), "x", 3),
    )
    second_round = (key_ahead_high, key_behind_low, value_ahead_high, value_behind_low)
    own_key = after(key_low, *second_round)
    own_probs, own_values = attend_call(ready, (own_key, key_high), (value_low, value_high))
    key_near = (key_ahead_low, key_ahead_high, key_behind_low, key_behind_high)
    value_near = (value_ahead_low, value_ahead_high, value_behind_low, value_behind_high)
    near_probs, near_values = attend_call(ready, key_near, value_near)
    key_far = tuple(after(b, own_probs, near_probs) for b in key_far)
    value_blocks = (value_low, value_high, *value_near)

    def mix(*refs):
        mix_kernel(
            refs[0:2], refs[2:4], (*refs[4:10], *refs[-3:-1]), attend_refs(refs[10:], 2), refs[-1]
        )

    partial = call(
        mix,
        shape((2 * masks, feature), F32),
        (
            own_probs, near_probs, own_values, near_values, *value_blocks,
            *attend_args(ready, key_far, value_far),
        ),
        flops=4 * span * feature * 256 + 4 * masks * feature * 8 * size,
        exps=4 * masks * span,
    )

    def score(*refs):
        score_kernel(refs[:2], *refs[2:4], refs[4:6], *refs[6:])

    placed = call(
        score,
        shape((128, 64), F32),
        (
            mine[2], other[2], partial, swap(partial), mine[4], other[4],
            ln_final_gain.reshape(1, -1), decoder_bias.reshape(1, -1), dense_weight,
            decoder_weight.T,
        ),
        flops=4 * masks * feature * feature,
    )
    arrived = lax.all_to_all(placed, ("z", "y", "x"), 0, 0, tiled=True)
    return jnp.sum(arrived, axis=0).reshape(16, 4)


def solution(mesh):
    fine = Mesh(mesh.devices.reshape(8, 2, 4, 4), ("z", "core", "y", "x"))
    dp, mp = ("z", "core"), ("y", "x")
    placed = (
        P(("z", "core", "y", "x"), None, None),
        P(),
        P(None, mp, None),
        P(None, mp, None),
        P(),
        P(),
        P(),
        P(),
        P(),
        P(),
        P(),
        P(),
        P(),
    )
    return jax.shard_map(
        on_device, mesh=fine, in_specs=placed, out_specs=P(dp, mp), check_vma=False
    )
```

```python
import numpy as np
import jax
import jax.numpy as jnp
from jax import lax
from jax.experimental import pallas as pl
from jax.experimental.pallas import tpu as pltpu
from jax.sharding import Mesh, PartitionSpec as P

epsilon = 1e-05
F32 = jnp.float32
BF16 = jnp.bfloat16


def rotary_tables(seq_span, head_size):
    half = head_size // 2
    power = (np.arange(half, dtype=np.float32) * np.float32(2.0 / head_size)).astype(np.float32)
    frequency = (np.float32(1.0) / np.power(np.float32(10000.0), power)).astype(np.float32)
    angles = (np.arange(seq_span, dtype=np.float32)[:, None] * frequency[None, :]).astype(np.float32)
    cosine = np.cos(angles.astype(np.float64)).astype(np.float32)
    sine = np.sin(angles.astype(np.float64)).astype(np.float32)
    wide = np.concatenate([cosine] * 4 + [-sine, sine] * 2, axis=1)
    rest = np.concatenate([cosine, sine], axis=1)
    parts = []
    for _ in range(3):
        parts.append(rest.astype(BF16))
        rest = rest - parts[-1].astype(np.float32)
    parts.append(np.zeros_like(parts[0]))
    return wide, np.concatenate(parts, axis=1)


def nt_dot(a, b):
    return lax.dot_general(a, b, (((1,), (1,)), ((), ())), preferred_element_type=F32)


def nn_dot(a, b, **options):
    return lax.dot_general(a, b, (((1,), (0,)), ((), ())), preferred_element_type=F32, **options)


def rotate(part, table, half):
    cos_table, sin_table = table[:, :128], table[:, 128:]
    width = part.shape[1]
    lane = lax.broadcasted_iota(jnp.int32, part.shape, 1) % (2 * half)
    turned = jnp.where(
        lane < half,
        pltpu.roll(part, width - half, 1),
        pltpu.roll(part, half, 1),
    )
    return part * cos_table + turned * sin_table


IN_PLACE = pl.BlockSpec(memory_space=pltpu.MemorySpace.HBM)
ON_CHIP = pl.BlockSpec(memory_space=pltpu.MemorySpace.VMEM)


def call(kernel, outs, args, n_any=0, scratch=(), flops=0, exps=0, vmem=24 * 1024 * 1024):
    moved = sum(a.size * a.dtype.itemsize for a in list(args) + jax.tree.leaves(outs))
    place = pltpu.with_memory_space_constraint
    args = [place(a, pltpu.HBM) if i < n_any else a for i, a in enumerate(args)]
    return pl.pallas_call(
        kernel,
        out_shape=outs,
        in_specs=[IN_PLACE] * n_any + [ON_CHIP] * (len(args) - n_any),
        out_specs=jax.tree.map(lambda _: ON_CHIP, outs),
        scratch_shapes=list(scratch),
        cost_estimate=pl.CostEstimate(flops=flops, transcendentals=exps, bytes_accessed=moved),
        compiler_params=pltpu.CompilerParams(vmem_limit_bytes=vmem),
    )(*args)


def pack_kernel(turned_ref, out_ref, key_ref, value_ref, sems):
    size = out_ref.shape[0]
    copies = (
        pltpu.make_async_copy(turned_ref.at[: 2 * size], key_ref, sems.at[0]),
        pltpu.make_async_copy(turned_ref.at[2 * size :], value_ref.at[:size], sems.at[1]),
        pltpu.make_async_copy(out_ref, value_ref.at[size:], sems.at[2]),
    )
    for copy in copies:
        copy.start()
    for copy in copies:
        copy.wait()


def pack(turned, out_weight):
    size, feature = out_weight.shape
    return call(
        pack_kernel,
        [jax.ShapeDtypeStruct((2 * size, feature), BF16)] * 2,
        (turned, out_weight),
        n_any=2,
        scratch=[pltpu.SemaphoreType.DMA((3,))],
    )


def first(mask, values):
    picked = jnp.sum(jnp.where(mask, values, 0), axis=1, keepdims=True)
    return jnp.sum(picked, axis=0, keepdims=True)


def norm_rows(values, gain):
    average = jnp.mean(values, axis=1, keepdims=True)
    centred = values - average
    variance = jnp.mean(centred * centred, axis=1, keepdims=True)
    return (centred * lax.rsqrt(variance + epsilon) * gain).astype(BF16)


def prepare_kernel(mine, small_refs, pick_ref, states_from, table_from, out_refs, scratch, sems):
    normed_ref, picked_ref, rows_ref, qtable_ref, meta_ref = out_refs[:5]
    copies = [
        pltpu.make_async_copy(source, target, sems.at[i])
        for i, (source, target) in enumerate(zip((*small_refs, pick_ref), scratch))
    ]
    late = []
    if mine:
        states_ref = scratch[7]
        late = [
            pltpu.make_async_copy(states_from, states_ref, sems.at[7]),
            pltpu.make_async_copy(table_from, out_refs[5], sems.at[8]),
        ]
    else:
        states_ref = states_from
    for copy in (*copies, *late):
        copy.start()
    sequence_ref, length_ref, owner_ref, codes_ref, tokens_ref, gain_ref, pick_ref = scratch[:7]
    span, feature = normed_ref.shape
    masks = codes_ref.shape[0]
    core = lax.axis_index("core")
    core = core if mine else 1 - core
    copy_id = (
        (lax.axis_index("z") * 2 + core) * 4 + lax.axis_index("y")
    ) * 4 + lax.axis_index("x")
    copies[5].wait()
    block = 16

    def norm_all():
        gain = gain_ref[...].reshape(1, -1)

        def step(i, carry):
            at = pl.multiple_of(i * block, block)
            values = states_ref[pl.ds(at, block), :].astype(F32)
            normed_ref[pl.ds(at, block), :] = norm_rows(values, gain)
            return carry

        lax.fori_loop(0, span // block, step, 0, unroll=20)

    if not mine:
        norm_all()
    for copy in (*copies[:5], copies[6]):
        copy.wait()

    def numbers(count):
        return lax.broadcasted_iota(jnp.int32, (1, count), 1)

    own = numbers(codes_ref.shape[1]) == copy_id
    sequence = first(own, sequence_ref[...].reshape(1, -1))
    owner = first(own, owner_ref[...].reshape(1, -1))
    length = first(numbers(length_ref.shape[0]) == sequence, length_ref[...].reshape(1, -1))
    codes = jnp.sum(jnp.where(own, codes_ref[...], 0), axis=1, keepdims=True)
    quotient = jnp.floor(codes.astype(F32) / length.astype(F32)).astype(jnp.int32)
    positions = codes - quotient * length
    positions = jnp.where(positions < 0, positions + length, positions)
    positions = jnp.where(positions >= length, positions - length, positions)
    hit = lax.broadcasted_iota(jnp.int32, (masks, span), 1) == positions
    line = lax.broadcasted_iota(jnp.int32, tokens_ref.shape, 0)
    tokens = jnp.sum(jnp.where(line == sequence, tokens_ref[...], 0), axis=0, keepdims=True)
    targets = jnp.sum(jnp.where(hit, tokens, 0), axis=1, keepdims=True)
    lane = lax.broadcasted_iota(jnp.int32, meta_ref.shape, 1)
    meta_ref[...] = jnp.where(lane == 0, targets, jnp.where(lane == 1, length, owner))
    hot = hit.astype(F32).astype(BF16)
    picks = nn_dot(hot, pick_ref[...])
    wide = picks.shape[1] // 4
    picks = picks[:, :wide] + picks[:, wide : 2 * wide] + picks[:, 2 * wide : 3 * wide]
    cosine, sine = picks[:, : wide // 2], picks[:, wide // 2 :]
    qtable_ref[...] = jnp.concatenate([cosine] * 4 + [-sine, sine] * 2, axis=1)
    for copy in late:
        copy.wait()
    if mine:
        norm_all()
    rows = nn_dot(hot, states_ref[...])
    rows_ref[...] = rows
    picked_ref[...] = norm_rows(rows, gain_ref[...].reshape(1, -1))


def attend(table_ref, normed_refs, picked_refs, qtable_refs, meta_refs, key_refs, value_refs):
    size = key_refs[0].shape[0] // 2
    masks = picked_refs[0].shape[0]
    heads = len(key_refs)
    width = heads * size
    weight = jnp.concatenate(
        [r[size:, :] for r in key_refs] + [r[:size, :] for r in value_refs], axis=0
    )
    query_weight = jnp.concatenate([r[:size, :] for r in key_refs], axis=0)
    picked = jnp.concatenate([r[...] for r in picked_refs], axis=0)
    queries = nt_dot(picked, query_weight) * 0.125
    results = []
    for which in range(2):
        length = meta_refs[which][0:1, 1:2]
        projected = nt_dot(normed_refs[which][...], weight)
        own = queries[masks * which : masks * (which + 1), :]
        turned_keys, turned_queries = [], []
        for i in range(heads // 2):
            lanes = slice(128 * i, 128 * (i + 1))
            turned_keys.append(rotate(projected[:, lanes], table_ref[...], size // 2))
            turned_queries.append(rotate(own[:, lanes], qtable_refs[which][...], size // 2))
        key_rows = jnp.concatenate(turned_keys, axis=1).astype(BF16)
        query_rows = jnp.concatenate(turned_queries, axis=1).astype(BF16)
        spread = jnp.concatenate([query_rows] * heads, axis=0)
        row = lax.broadcasted_iota(jnp.int32, spread.shape, 0) // masks
        lane = lax.broadcasted_iota(jnp.int32, spread.shape, 1) // size
        spread = jnp.where(row == lane, spread, jnp.zeros_like(spread))
        logits = nt_dot(spread, key_rows)
        alive = lax.broadcasted_iota(jnp.int32, logits.shape, 1) < length
        logits = jnp.where(alive, logits, -1e30)
        largest = jnp.max(logits, axis=1, keepdims=True)
        weights = jnp.exp(logits - largest)
        total = jnp.sum(weights, axis=1, keepdims=True)
        probs = (weights * (1.0 / total)).astype(BF16)
        results.append((probs, projected[:, width:].astype(BF16)))
    return results


def attend_kernel(*refs):
    inputs, (probs_ref, values_ref) = refs[:-2], refs[-2:]
    for which, (probs, values) in enumerate(attend(*inputs)):
        probs_ref[which] = probs
        values_ref[which] = values


def mix_columns(columns, probs, values, masks, size):
    right = (lax.axis_index("x") + lax.axis_index("y")) % 2 == lax.axis_index("core")

    def rows_of(step, which):
        start = masks * (which + (2 if step == 3 else 0))
        return probs[(0, 1, 2, 1)[step]](start, start + masks)

    stack = []
    for column in columns:
        which = column // 2
        for i in range(2):
            even = rows_of((0, 2)[i], which)
            odd = rows_of((1, 3)[i], which)
            if column % 2:
                even, odd = odd, even
            stack.append(jnp.where(right, even, odd))
    mixed = nn_dot(jnp.concatenate(stack, axis=0), values)
    lane = lax.broadcasted_iota(jnp.int32, (masks, mixed.shape[1]), 1) // size
    context = mixed[:masks, :]
    for head in range(1, len(stack)):
        context = jnp.where(lane == head, mixed[masks * head : masks * (head + 1), :], context)
    return context.astype(BF16)


def rows_reader(ref, copy):
    return lambda start, end: ref[copy, start:end, :]


def first_mix_kernel(probs_refs, values_refs, block_refs, inputs, probs_ref, partial_ref):
    size = block_refs[0].shape[0] // 2
    masks = probs_refs[0].shape[1] // 2
    for copy, (probs, _) in enumerate(attend(*inputs)):
        probs_ref[copy] = probs
    contexts = []
    for copy in range(2):
        readers = [rows_reader(r, copy) for r in (*probs_refs, probs_ref)]
        contexts.append(
            jnp.concatenate(
                [
                    mix_columns(columns, readers, ref[copy], masks, size)
                    for columns, ref in zip(((0,), (1, 3)), values_refs)
                ],
                axis=1,
            )
        )
    weight = jnp.concatenate([r[size:, :] for r in block_refs], axis=0)
    partial_ref[...] = nn_dot(jnp.concatenate(contexts, axis=0), weight)


def last_mix_kernel(probs_refs, normed_refs, block_refs, sum_ref, partial_ref):
    size = block_refs[0].shape[0] // 2
    masks = probs_refs[0].shape[1] // 2
    value_weight = jnp.concatenate([r[:size, :] for r in block_refs], axis=0)
    contexts = []
    for copy in range(2):
        readers = [rows_reader(r, copy) for r in probs_refs]
        values = nt_dot(normed_refs[copy][...], value_weight).astype(BF16)
        contexts.append(mix_columns((2,), readers, values, masks, size))
    weight = jnp.concatenate([r[size:, :] for r in block_refs], axis=0)
    partial_ref[...] = sum_ref[...] + nn_dot(jnp.concatenate(contexts, axis=0), weight)


def score_kernel(
    rows_refs, partial_ref, arrived_ref, meta_refs, gain_ref, bias_ref, dense_ref, decoder_ref,
    placed_ref,
):
    masks = rows_refs[0].shape[0]
    residual = jnp.concatenate(
        [
            rows_refs[0][...] + (partial_ref[:masks, :] + arrived_ref[masks:, :]),
            rows_refs[1][...] + (partial_ref[masks:, :] + arrived_ref[:masks, :]),
        ],
        axis=0,
    )
    targets = jnp.concatenate([r[:, 0:1] for r in meta_refs], axis=0)
    average = jnp.mean(residual, axis=1, keepdims=True)
    centred = residual - average
    variance = jnp.mean(centred * centred, axis=1, keepdims=True)
    normed = (centred * lax.rsqrt(variance + epsilon) * gain_ref[...]).astype(BF16)
    dense = nn_dot(normed, dense_ref[...])
    active = 0.5 * dense * (1.0 + lax.erf(dense * np.float32(0.5**0.5)))
    average = jnp.mean(active, axis=1, keepdims=True)
    centred = active - average
    variance = jnp.mean(centred * centred, axis=1, keepdims=True)
    headed = (centred * lax.rsqrt(variance + epsilon)).astype(BF16)
    logits = nt_dot(headed, decoder_ref[...]) + bias_ref[...]
    largest = jnp.max(logits, axis=1, keepdims=True)
    total = jnp.sum(jnp.exp(logits - largest), axis=1, keepdims=True)
    vocab = lax.broadcasted_iota(jnp.int32, logits.shape, 1)
    chosen = jnp.sum(jnp.where(vocab == targets, logits, 0.0), axis=1, keepdims=True)
    score = chosen - largest - jnp.log(total)
    devices, width = placed_ref.shape
    member = lax.broadcasted_iota(jnp.int32, (devices, masks), 0) % 16
    part = lax.broadcasted_iota(jnp.int32, (devices, masks), 1) // 4
    take = (member == part).astype(F32)
    fits = (
        lax.broadcasted_iota(jnp.int32, (masks, width), 0) % 4
        == lax.broadcasted_iota(jnp.int32, (masks, width), 1) % 4
    )
    layer = lax.broadcasted_iota(jnp.int32, (devices, width), 0) // 16
    slot = lax.broadcasted_iota(jnp.int32, (devices, width), 1) // 4
    wanted = 16 * (2 * layer + lax.axis_index("core")) + slot
    placed = jnp.zeros((devices, width), F32)
    for which in range(2):
        own = jnp.where(fits, score[masks * which : masks * (which + 1), :], 0.0)
        laid = nn_dot(take, own, precision=lax.Precision.HIGHEST)
        placed = jnp.where(wanted == meta_refs[which][0:1, 2:3], laid, placed)
    placed_ref[...] = placed


def pull(array, axis, offset):
    size = lax.axis_size(axis)
    return lax.ppermute(array, axis, [((i + offset) % size, i) for i in range(size)])


def swap(array):
    return lax.ppermute(array, "core", [(0, 1), (1, 0)])


def after(array, *others):
    return lax.optimization_barrier((array, *others))[0]


def gather_line(block, axis):
    near, far = [], []
    for core in range(2):
        for y in range(4):
            for x in range(4):
                def device(step):
                    to_y = (y + step) % 4 if axis == "y" else y
                    to_x = (x + step) % 4 if axis == "x" else x
                    return (((x + y) % 2) * 4 + to_y) * 4 + to_x

                source = (core * 4 + y) * 4 + x
                own = (x + y) % 2 == core
                near.append((source, device(-1 if own else 0)))
                far.append((source, device(1 if own else 2)))
    axes = ("core", "y", "x")
    return lax.ppermute(block, axes, near), lax.ppermute(block, axes, far)


def on_device(
    hidden_states,
    ln_attn_gain,
    w_qkv,
    output_weight,
    ln_final_gain,
    dense_weight,
    decoder_weight,
    decoder_bias,
    seq_tokens,
    seq_lengths,
    copy_sequence,
    mask_code,
    copy_owner,
):
    _, span, feature = hidden_states.shape
    size = output_weight.shape[0]
    masks = mask_code.shape[1]
    table, pick_table = (jnp.asarray(t) for t in rotary_tables(span, size))
    shape = jax.ShapeDtypeStruct

    def prepare_call(mine, states):
        small = [copy_sequence, seq_lengths, copy_owner, mask_code.T, seq_tokens, ln_attn_gain]
        outs = [
            shape((span, feature), BF16),
            shape((masks, feature), BF16),
            shape((masks, feature), F32),
            shape((masks, 256), F32),
            shape((masks, 128), jnp.int32),
        ]
        args = [*small, pick_table, table, states] if mine else [*small, pick_table, states]
        scratch = [pltpu.VMEM(a.shape, a.dtype) for a in (*small, pick_table)]
        if mine:
            outs.append(shape(table.shape, F32))
            scratch.append(pltpu.VMEM(states.shape, states.dtype))
        n, m = len(args), len(outs)

        def kernel(*refs):
            prepare_kernel(
                mine, refs[:6], refs[6], refs[n - 1], refs[7], refs[n : n + m], refs[n + m : -1],
                refs[-1],
            )

        return call(
            kernel,
            outs,
            args,
            n_any=9 if mine else 7,
            scratch=[*scratch, pltpu.SemaphoreType.DMA((9,))],
            flops=4 * masks * span * feature + 10 * span * feature,
        )

    def attend_args(ready, key_blocks, value_blocks):
        per_copy = [r[i] for i in (0, 1, 3, 4) for r in ready]
        return (ready[0][5], *per_copy, *key_blocks, *value_blocks)

    def attend_refs(refs, heads, value_heads):
        keys_at = 9 + heads
        return (
            refs[0], refs[1:3], refs[3:5], refs[5:7], refs[7:9], refs[9:keys_at],
            refs[keys_at : keys_at + value_heads],
        )

    def attend_call(ready, key_blocks, value_blocks):
        heads = len(key_blocks)

        def kernel(*refs):
            attend_kernel(*attend_refs(refs, heads, heads), *refs[-2:])

        return call(
            kernel,
            [
                shape((2, heads * masks, span), BF16),
                shape((2, span, heads * size), BF16),
            ],
            attend_args(ready, key_blocks, value_blocks),
            flops=4 * span * feature * heads * 128,
            exps=2 * heads * masks * span,
        )

    states = hidden_states[0]
    key_block, value_block = pack(jnp.transpose(w_qkv[:, 0, :]), output_weight[:, 0, :])
    key_low, key_high = gather_line(key_block, "x")
    value_low, value_high = gather_line(value_block, "y")
    states_other = swap(states)
    key_ahead_low = pull(key_low, "y", 1)
    key_behind_high = pull(key_high, "y", 3)
    value_ahead_low = pull(value_low, "x", 1)
    value_behind_high = pull(value_high, "x", 3)
    mine = prepare_call(True, after(states, key_low, key_high, value_low, value_high))
    key_ahead_high = pull(after(key_high, key_ahead_low, mine[0]), "y", 1)
    key_behind_low = pull(after(key_low, key_behind_high, mine[0]), "y", 3)
    value_ahead_high = pull(after(value_high, value_ahead_low, mine[0]), "x", 1)
    value_behind_low = pull(after(value_low, value_behind_high, mine[0]), "x", 3)
    first_round = (key_ahead_low, key_behind_high, value_ahead_low, value_behind_high)
    other = prepare_call(False, after(states_other, mine[0], *first_round))
    ready = (mine, other)
    key_far = (
        pull(after(key_ahead_low, key_ahead_high, other[0]), "y", 1),
        pull(after(key_behind_high, key_behind_low, other[0]), "y", 3),
    )
    value_far = (
        pull(after(value_ahead_low, value_ahead_high, other[0]), "x", 1),
        pull(after(value_behind_high, value_behind_low, other[0]), "x", 3),
    )
    second_round = (key_ahead_high, key_behind_low, value_ahead_high, value_behind_low)
    own_key = after(key_low, *second_round)
    own_probs, own_values = attend_call(ready, (own_key, key_high), (value_low, value_high))
    key_near = (key_ahead_low, key_ahead_high, key_behind_low, key_behind_high)
    value_near = (value_ahead_low, value_ahead_high, value_behind_low, value_behind_high)
    near_probs, near_values = attend_call(ready, key_near, value_near)
    key_far = tuple(after(b, own_probs, near_probs) for b in key_far)
    value_blocks = (value_low, value_high, *value_near)

    def first_mix(*refs):
        first_mix_kernel(
            refs[0:2], refs[2:4], refs[4:10], attend_refs(refs[10:], 2, 0), *refs[-2:]
        )

    far_probs, first_sum = call(
        first_mix,
        [shape((2, 2 * masks, span), BF16), shape((2 * masks, feature), F32)],
        (
            own_probs, near_probs, own_values, near_values, *value_blocks,
            *attend_args(ready, key_far, ()),
        ),
        flops=4 * span * feature * 256 + 4 * masks * feature * 6 * size,
        exps=4 * masks * span,
    )
    value_far = tuple(after(b, far_probs) for b in value_far)

    def last_mix(*refs):
        last_mix_kernel(refs[:3], refs[3:5], refs[5:7], *refs[7:])

    partial = call(
        last_mix,
        shape((2 * masks, feature), F32),
        (own_probs, near_probs, far_probs, mine[0], other[0], *value_far, first_sum),
        flops=4 * span * feature * 256 + 4 * masks * feature * 2 * size,
    )

    def score(*refs):
        score_kernel(refs[:2], *refs[2:4], refs[4:6], *refs[6:])

    placed = call(
        score,
        shape((128, 64), F32),
        (
            mine[2], other[2], partial, swap(partial), mine[4], other[4],
            ln_final_gain.reshape(1, -1), decoder_bias.reshape(1, -1), dense_weight,
            decoder_weight.T,
        ),
        flops=4 * masks * feature * feature,
    )
    arrived = lax.all_to_all(placed, ("z", "y", "x"), 0, 0, tiled=True)
    return jnp.sum(arrived, axis=0).reshape(16, 4)


def solution(mesh):
    fine = Mesh(mesh.devices.reshape(8, 2, 4, 4), ("z", "core", "y", "x"))
    dp, mp = ("z", "core"), ("y", "x")
    placed = (
        P(("z", "core", "y", "x"), None, None),
        P(),
        P(None, mp, None),
        P(None, mp, None),
        P(),
        P(),
        P(),
        P(),
        P(),
        P(),
        P(),
        P(),
        P(),
    )
    return jax.shard_map(
        on_device, mesh=fine, in_specs=placed, out_specs=P(dp, mp), check_vma=False
    )
```

```python
import numpy as np
import jax
import jax.numpy as jnp
from jax import lax
from jax.experimental import pallas as pl
from jax.experimental.pallas import tpu as pltpu
from jax.sharding import Mesh, PartitionSpec as P

epsilon = 1e-05
F32 = jnp.float32
BF16 = jnp.bfloat16


def rotary_tables(seq_span, head_size):
    half = head_size // 2
    power = (np.arange(half, dtype=np.float32) * np.float32(2.0 / head_size)).astype(np.float32)
    frequency = (np.float32(1.0) / np.power(np.float32(10000.0), power)).astype(np.float32)
    angles = (np.arange(seq_span, dtype=np.float32)[:, None] * frequency[None, :]).astype(np.float32)
    cosine = np.cos(angles.astype(np.float64)).astype(np.float32)
    sine = np.sin(angles.astype(np.float64)).astype(np.float32)
    wide = np.concatenate([cosine] * 4 + [-sine, sine] * 2, axis=1)
    rest = np.concatenate([cosine, sine], axis=1)
    parts = []
    for _ in range(3):
        parts.append(rest.astype(BF16))
        rest = rest - parts[-1].astype(np.float32)
    parts.append(np.zeros_like(parts[0]))
    return wide, np.concatenate(parts, axis=1)


def nt_dot(a, b):
    return lax.dot_general(a, b, (((1,), (1,)), ((), ())), preferred_element_type=F32)


def nn_dot(a, b, **options):
    return lax.dot_general(a, b, (((1,), (0,)), ((), ())), preferred_element_type=F32, **options)


def rotate(part, table, half):
    cos_table, sin_table = table[:, :128], table[:, 128:]
    width = part.shape[1]
    lane = lax.broadcasted_iota(jnp.int32, part.shape, 1) % (2 * half)
    turned = jnp.where(
        lane < half,
        pltpu.roll(part, width - half, 1),
        pltpu.roll(part, half, 1),
    )
    return part * cos_table + turned * sin_table


IN_PLACE = pl.BlockSpec(memory_space=pltpu.MemorySpace.HBM)
ON_CHIP = pl.BlockSpec(memory_space=pltpu.MemorySpace.VMEM)


def call(kernel, outs, args, n_any=0, scratch=(), flops=0, exps=0, vmem=24 * 1024 * 1024):
    moved = sum(a.size * a.dtype.itemsize for a in list(args) + jax.tree.leaves(outs))
    place = pltpu.with_memory_space_constraint
    args = [place(a, pltpu.HBM) if i < n_any else a for i, a in enumerate(args)]
    return pl.pallas_call(
        kernel,
        out_shape=outs,
        in_specs=[IN_PLACE] * n_any + [ON_CHIP] * (len(args) - n_any),
        out_specs=jax.tree.map(lambda _: ON_CHIP, outs),
        scratch_shapes=list(scratch),
        cost_estimate=pl.CostEstimate(flops=flops, transcendentals=exps, bytes_accessed=moved),
        compiler_params=pltpu.CompilerParams(vmem_limit_bytes=vmem),
    )(*args)


def pack_kernel(turned_ref, out_ref, key_ref, value_ref, sems):
    size = out_ref.shape[0]
    copies = (
        pltpu.make_async_copy(turned_ref.at[: 2 * size], key_ref, sems.at[0]),
        pltpu.make_async_copy(turned_ref.at[2 * size :], value_ref.at[:size], sems.at[1]),
        pltpu.make_async_copy(out_ref, value_ref.at[size:], sems.at[2]),
    )
    for copy in copies:
        copy.start()
    for copy in copies:
        copy.wait()


def pack(turned, out_weight):
    size, feature = out_weight.shape
    return call(
        pack_kernel,
        [jax.ShapeDtypeStruct((2 * size, feature), BF16)] * 2,
        (turned, out_weight),
        n_any=2,
        scratch=[pltpu.SemaphoreType.DMA((3,))],
    )


def first(mask, values):
    picked = jnp.sum(jnp.where(mask, values, 0), axis=1, keepdims=True)
    return jnp.sum(picked, axis=0, keepdims=True)


def norm_rows(values, gain):
    average = jnp.mean(values, axis=1, keepdims=True)
    centred = values - average
    variance = jnp.mean(centred * centred, axis=1, keepdims=True)
    return (centred * lax.rsqrt(variance + epsilon) * gain).astype(BF16)


def prepare_kernel(mine, small_refs, pick_ref, states_from, table_from, out_refs, scratch, sems):
    normed_ref, picked_ref, rows_ref, qtable_ref, meta_ref = out_refs[:5]
    copies = [
        pltpu.make_async_copy(source, target, sems.at[i])
        for i, (source, target) in enumerate(zip((*small_refs, pick_ref), scratch))
    ]
    late = []
    if mine:
        states_ref = scratch[7]
        late = [
            pltpu.make_async_copy(states_from, states_ref, sems.at[7]),
            pltpu.make_async_copy(table_from, out_refs[5], sems.at[8]),
        ]
    else:
        states_ref = states_from
    for copy in (*copies, *late):
        copy.start()
    sequence_ref, length_ref, owner_ref, codes_ref, tokens_ref, gain_ref, pick_ref = scratch[:7]
    span, feature = normed_ref.shape
    masks = codes_ref.shape[0]
    core = lax.axis_index("core")
    core = core if mine else 1 - core
    copy_id = (
        (lax.axis_index("z") * 2 + core) * 4 + lax.axis_index("y")
    ) * 4 + lax.axis_index("x")
    copies[5].wait()
    block = 16

    def norm_all():
        gain = gain_ref[...].reshape(1, -1)

        def step(i, carry):
            at = pl.multiple_of(i * block, block)
            values = states_ref[pl.ds(at, block), :].astype(F32)
            normed_ref[pl.ds(at, block), :] = norm_rows(values, gain)
            return carry

        lax.fori_loop(0, span // block, step, 0, unroll=20)

    if not mine:
        norm_all()
    for copy in (*copies[:5], copies[6]):
        copy.wait()

    def numbers(count):
        return lax.broadcasted_iota(jnp.int32, (1, count), 1)

    own = numbers(codes_ref.shape[1]) == copy_id
    sequence = first(own, sequence_ref[...].reshape(1, -1))
    owner = first(own, owner_ref[...].reshape(1, -1))
    length = first(numbers(length_ref.shape[0]) == sequence, length_ref[...].reshape(1, -1))
    codes = jnp.sum(jnp.where(own, codes_ref[...], 0), axis=1, keepdims=True)
    quotient = jnp.floor(codes.astype(F32) / length.astype(F32)).astype(jnp.int32)
    positions = codes - quotient * length
    positions = jnp.where(positions < 0, positions + length, positions)
    positions = jnp.where(positions >= length, positions - length, positions)
    hit = lax.broadcasted_iota(jnp.int32, (masks, span), 1) == positions
    line = lax.broadcasted_iota(jnp.int32, tokens_ref.shape, 0)
    tokens = jnp.sum(jnp.where(line == sequence, tokens_ref[...], 0), axis=0, keepdims=True)
    targets = jnp.sum(jnp.where(hit, tokens, 0), axis=1, keepdims=True)
    lane = lax.broadcasted_iota(jnp.int32, meta_ref.shape, 1)
    meta_ref[...] = jnp.where(lane == 0, targets, jnp.where(lane == 1, length, owner))
    hot = hit.astype(F32).astype(BF16)
    picks = nn_dot(hot, pick_ref[...])
    wide = picks.shape[1] // 4
    picks = picks[:, :wide] + picks[:, wide : 2 * wide] + picks[:, 2 * wide : 3 * wide]
    cosine, sine = picks[:, : wide // 2], picks[:, wide // 2 :]
    qtable_ref[...] = jnp.concatenate([cosine] * 4 + [-sine, sine] * 2, axis=1)
    for copy in late:
        copy.wait()
    if mine:
        norm_all()
    rows = nn_dot(hot, states_ref[...])
    rows_ref[...] = rows
    picked_ref[...] = norm_rows(rows, gain_ref[...].reshape(1, -1))


def attend(table_ref, normed_refs, picked_refs, qtable_refs, meta_refs, key_refs, value_refs):
    size = key_refs[0].shape[0] // 2
    masks = picked_refs[0].shape[0]
    heads = len(key_refs)
    width = heads * size
    weight = jnp.concatenate(
        [r[size:, :] for r in key_refs] + [r[:size, :] for r in value_refs], axis=0
    )
    query_weight = jnp.concatenate([r[:size, :] for r in key_refs], axis=0)
    picked = jnp.concatenate([r[...] for r in picked_refs], axis=0)
    queries = nt_dot(picked, query_weight) * 0.125
    results = []
    for which in range(2):
        length = meta_refs[which][0:1, 1:2]
        projected = nt_dot(normed_refs[which][...], weight)
        own = queries[masks * which : masks * (which + 1), :]
        turned_keys, turned_queries = [], []
        for i in range(heads // 2):
            lanes = slice(128 * i, 128 * (i + 1))
            turned_keys.append(rotate(projected[:, lanes], table_ref[...], size // 2))
            turned_queries.append(rotate(own[:, lanes], qtable_refs[which][...], size // 2))
        key_rows = jnp.concatenate(turned_keys, axis=1).astype(BF16)
        query_rows = jnp.concatenate(turned_queries, axis=1).astype(BF16)
        spread = jnp.concatenate([query_rows] * heads, axis=0)
        row = lax.broadcasted_iota(jnp.int32, spread.shape, 0) // masks
        lane = lax.broadcasted_iota(jnp.int32, spread.shape, 1) // size
        spread = jnp.where(row == lane, spread, jnp.zeros_like(spread))
        logits = nt_dot(spread, key_rows)
        alive = lax.broadcasted_iota(jnp.int32, logits.shape, 1) < length
        logits = jnp.where(alive, logits, -1e30)
        largest = jnp.max(logits, axis=1, keepdims=True)
        weights = jnp.exp(logits - largest)
        total = jnp.sum(weights, axis=1, keepdims=True)
        probs = (weights * (1.0 / total)).astype(BF16)
        results.append((probs, projected[:, width:].astype(BF16)))
    return results


def attend_kernel(*refs):
    inputs, (probs_ref, values_ref) = refs[:-2], refs[-2:]
    for which, (probs, values) in enumerate(attend(*inputs)):
        probs_ref[which] = probs
        values_ref[which] = values


def mix_columns(columns, probs, values, masks, size):
    right = (lax.axis_index("x") + lax.axis_index("y")) % 2 == lax.axis_index("core")

    def rows_of(step, which):
        start = masks * (which + (2 if step == 3 else 0))
        return probs[(0, 1, 2, 1)[step]](start, start + masks)

    stack = []
    for column in columns:
        which = column // 2
        for i in range(2):
            even = rows_of((0, 2)[i], which)
            odd = rows_of((1, 3)[i], which)
            if column % 2:
                even, odd = odd, even
            stack.append(jnp.where(right, even, odd))
    mixed = nn_dot(jnp.concatenate(stack, axis=0), values)
    lane = lax.broadcasted_iota(jnp.int32, (masks, mixed.shape[1]), 1) // size
    context = mixed[:masks, :]
    for head in range(1, len(stack)):
        context = jnp.where(lane == head, mixed[masks * head : masks * (head + 1), :], context)
    return context.astype(BF16)


def rows_reader(ref, copy):
    return lambda start, end: ref[copy, start:end, :]


def probs_kernel(*refs):
    inputs, probs_ref = refs[:-1], refs[-1]
    for which, (probs, _) in enumerate(attend(*inputs)):
        probs_ref[which] = probs


def mix_kernel(probs_refs, values_refs, normed_refs, far_refs, block_refs, partial_ref):
    size = block_refs[0].shape[0] // 2
    masks = probs_refs[0].shape[1] // 2
    value_weight = jnp.concatenate([r[:size, :] for r in far_refs], axis=0)
    contexts = []
    for copy in range(2):
        readers = [rows_reader(r, copy) for r in probs_refs]
        far = nt_dot(normed_refs[copy][...], value_weight).astype(BF16)
        values = (values_refs[0][copy], values_refs[1][copy], far)
        contexts.append(
            jnp.concatenate(
                [
                    mix_columns(columns, readers, value, masks, size)
                    for columns, value in zip(((0,), (1, 3), (2,)), values)
                ],
                axis=1,
            )
        )
    weight = jnp.concatenate([r[size:, :] for r in (*block_refs, *far_refs)], axis=0)
    partial_ref[...] = nn_dot(jnp.concatenate(contexts, axis=0), weight)


def join_kernel(low_ref, high_ref, line_ref):
    rows = low_ref.shape[0]
    line_ref[:rows, :] = low_ref[...]
    line_ref[rows:, :] = high_ref[...]


def join(low, high):
    line = jax.ShapeDtypeStruct((2 * low.shape[0], low.shape[1]), low.dtype)
    return call(join_kernel, line, (low, high))


def split_kernel(ahead_ref, behind_ref, low_ref, high_ref):
    rows = low_ref.shape[0]
    low_ref[...] = ahead_ref[:rows, :]
    high_ref[...] = behind_ref[rows:, :]


def split(ahead, behind):
    half = jax.ShapeDtypeStruct((ahead.shape[0] // 2, ahead.shape[1]), ahead.dtype)
    return call(split_kernel, [half, half], (ahead, behind))


def halves(ref):
    rows = ref.shape[0] // 2
    return ref.at[:rows], ref.at[rows:]


def score_kernel(
    rows_refs, partial_ref, arrived_ref, meta_refs, gain_ref, bias_ref, dense_ref, decoder_ref,
    placed_ref,
):
    masks = rows_refs[0].shape[0]
    residual = jnp.concatenate(
        [
            rows_refs[0][...] + (partial_ref[:masks, :] + arrived_ref[masks:, :]),
            rows_refs[1][...] + (partial_ref[masks:, :] + arrived_ref[:masks, :]),
        ],
        axis=0,
    )
    targets = jnp.concatenate([r[:, 0:1] for r in meta_refs], axis=0)
    average = jnp.mean(residual, axis=1, keepdims=True)
    centred = residual - average
    variance = jnp.mean(centred * centred, axis=1, keepdims=True)
    normed = (centred * lax.rsqrt(variance + epsilon) * gain_ref[...]).astype(BF16)
    dense = nn_dot(normed, dense_ref[...])
    active = 0.5 * dense * (1.0 + lax.erf(dense * np.float32(0.5**0.5)))
    average = jnp.mean(active, axis=1, keepdims=True)
    centred = active - average
    variance = jnp.mean(centred * centred, axis=1, keepdims=True)
    headed = (centred * lax.rsqrt(variance + epsilon)).astype(BF16)
    logits = nt_dot(headed, decoder_ref[...]) + bias_ref[...]
    largest = jnp.max(logits, axis=1, keepdims=True)
    total = jnp.sum(jnp.exp(logits - largest), axis=1, keepdims=True)
    vocab = lax.broadcasted_iota(jnp.int32, logits.shape, 1)
    chosen = jnp.sum(jnp.where(vocab == targets, logits, 0.0), axis=1, keepdims=True)
    score = chosen - largest - jnp.log(total)
    devices, width = placed_ref.shape
    member = lax.broadcasted_iota(jnp.int32, (devices, masks), 0) % 16
    part = lax.broadcasted_iota(jnp.int32, (devices, masks), 1) // 4
    take = (member == part).astype(F32)
    fits = (
        lax.broadcasted_iota(jnp.int32, (masks, width), 0) % 4
        == lax.broadcasted_iota(jnp.int32, (masks, width), 1) % 4
    )
    layer = lax.broadcasted_iota(jnp.int32, (devices, width), 0) // 16
    slot = lax.broadcasted_iota(jnp.int32, (devices, width), 1) // 4
    wanted = 16 * (2 * layer + lax.axis_index("core")) + slot
    placed = jnp.zeros((devices, width), F32)
    for which in range(2):
        own = jnp.where(fits, score[masks * which : masks * (which + 1), :], 0.0)
        laid = nn_dot(take, own, precision=lax.Precision.HIGHEST)
        placed = jnp.where(wanted == meta_refs[which][0:1, 2:3], laid, placed)
    placed_ref[...] = placed


def pull(array, axis, offset):
    size = lax.axis_size(axis)
    return lax.ppermute(array, axis, [((i + offset) % size, i) for i in range(size)])


def swap(array):
    return lax.ppermute(array, "core", [(0, 1), (1, 0)])


def after(array, *others):
    return lax.optimization_barrier((array, *others))[0]


def gather_line(block, axis):
    near, far = [], []
    for core in range(2):
        for y in range(4):
            for x in range(4):
                def device(step):
                    to_y = (y + step) % 4 if axis == "y" else y
                    to_x = (x + step) % 4 if axis == "x" else x
                    return (((x + y) % 2) * 4 + to_y) * 4 + to_x

                source = (core * 4 + y) * 4 + x
                own = (x + y) % 2 == core
                near.append((source, device(-1 if own else 0)))
                far.append((source, device(1 if own else 2)))
    axes = ("core", "y", "x")
    return lax.ppermute(block, axes, near), lax.ppermute(block, axes, far)


def on_device(
    hidden_states,
    ln_attn_gain,
    w_qkv,
    output_weight,
    ln_final_gain,
    dense_weight,
    decoder_weight,
    decoder_bias,
    seq_tokens,
    seq_lengths,
    copy_sequence,
    mask_code,
    copy_owner,
):
    _, span, feature = hidden_states.shape
    size = output_weight.shape[0]
    masks = mask_code.shape[1]
    table, pick_table = (jnp.asarray(t) for t in rotary_tables(span, size))
    shape = jax.ShapeDtypeStruct

    def prepare_call(mine, states):
        small = [copy_sequence, seq_lengths, copy_owner, mask_code.T, seq_tokens, ln_attn_gain]
        outs = [
            shape((span, feature), BF16),
            shape((masks, feature), BF16),
            shape((masks, feature), F32),
            shape((masks, 256), F32),
            shape((masks, 128), jnp.int32),
        ]
        args = [*small, pick_table, table, states] if mine else [*small, pick_table, states]
        scratch = [pltpu.VMEM(a.shape, a.dtype) for a in (*small, pick_table)]
        if mine:
            outs.append(shape(table.shape, F32))
            scratch.append(pltpu.VMEM(states.shape, states.dtype))
        n, m = len(args), len(outs)

        def kernel(*refs):
            prepare_kernel(
                mine, refs[:6], refs[6], refs[n - 1], refs[7], refs[n : n + m], refs[n + m : -1],
                refs[-1],
            )

        return call(
            kernel,
            outs,
            args,
            n_any=9 if mine else 7,
            scratch=[*scratch, pltpu.SemaphoreType.DMA((9,))],
            flops=4 * masks * span * feature + 10 * span * feature,
        )

    def attend_args(ready, key_blocks, value_blocks):
        per_copy = [r[i] for i in (0, 1, 3, 4) for r in ready]
        return (ready[0][5], *per_copy, *key_blocks, *value_blocks)

    def attend_refs(refs, keys, values):
        return (refs[0], refs[1:3], refs[3:5], refs[5:7], refs[7:9], keys, values)

    def attend_call(ready, key_lines, value_lines):
        count = len(key_lines)

        def kernel(*refs):
            lines = [halves(r) for r in refs[9:-2]]
            keys = [h for line in lines[:count] for h in line]
            values = [h for line in lines[count:] for h in line]
            attend_kernel(*attend_refs(refs, keys, values), *refs[-2:])

        heads = 2 * count
        return call(
            kernel,
            [
                shape((2, heads * masks, span), BF16),
                shape((2, span, heads * size), BF16),
            ],
            attend_args(ready, key_lines, value_lines),
            flops=4 * span * feature * heads * 128,
            exps=2 * heads * masks * span,
        )

    states = hidden_states[0]
    key_block, value_block = pack(jnp.transpose(w_qkv[:, 0, :]), output_weight[:, 0, :])
    key_low, key_high = gather_line(key_block, "x")
    value_low, value_high = gather_line(value_block, "y")
    states_other = swap(states)
    key_line = join(key_low, key_high)
    key_ahead = pull(key_line, "y", 1)
    key_behind = pull(key_line, "y", 3)
    value_line = join(value_low, value_high)
    value_ahead = pull(value_line, "x", 1)
    value_behind = pull(value_line, "x", 3)
    mine = prepare_call(True, after(states, key_line, value_line))
    other = prepare_call(False, after(states_other, mine[0]))
    ready = (mine, other)
    own_probs, own_values = attend_call(ready, (key_line,), (value_line,))
    key_parts = split(after(key_ahead, own_probs), after(key_behind, own_probs))
    key_far = (pull(key_parts[0], "y", 1), pull(key_parts[1], "y", 3))
    value_parts = split(after(value_ahead, own_probs), after(value_behind, own_probs))
    value_far = (pull(value_parts[0], "x", 1), pull(value_parts[1], "x", 3))
    near_probs, near_values = attend_call(
        ready, (key_ahead, key_behind), (value_ahead, value_behind)
    )
    key_far = tuple(after(b, near_probs) for b in key_far)
    far_args = attend_args(ready, key_far, ())

    def far_kernel(*refs):
        probs_kernel(*attend_refs(refs, refs[9:11], ()), refs[-1])

    far_probs = call(
        far_kernel,
        shape((2, 2 * masks, span), BF16),
        far_args,
        flops=4 * span * feature * 256,
        exps=4 * masks * span,
    )
    value_far = tuple(after(b, far_probs) for b in value_far)

    def mix(*refs):
        blocks = [h for r in refs[9:12] for h in halves(r)]
        mix_kernel(refs[:3], refs[3:5], refs[5:7], refs[7:9], blocks, refs[12])

    partial = call(
        mix,
        shape((2 * masks, feature), F32),
        (
            own_probs, near_probs, far_probs, own_values, near_values, mine[0], other[0],
            *value_far, value_line, value_ahead, value_behind,
        ),
        flops=4 * span * feature * 256 + 4 * masks * feature * 8 * size,
    )

    def score(*refs):
        score_kernel(refs[:2], *refs[2:4], refs[4:6], *refs[6:])

    placed = call(
        score,
        shape((128, 64), F32),
        (
            mine[2], other[2], partial, swap(partial), mine[4], other[4],
            ln_final_gain.reshape(1, -1), decoder_bias.reshape(1, -1), dense_weight,
            decoder_weight.T,
        ),
        flops=4 * masks * feature * feature,
    )
    arrived = lax.all_to_all(placed, ("z", "y", "x"), 0, 0, tiled=True)
    return jnp.sum(arrived, axis=0).reshape(16, 4)


def solution(mesh):
    fine = Mesh(mesh.devices.reshape(8, 2, 4, 4), ("z", "core", "y", "x"))
    dp, mp = ("z", "core"), ("y", "x")
    placed = (
        P(("z", "core", "y", "x"), None, None),
        P(),
        P(None, mp, None),
        P(None, mp, None),
        P(),
        P(),
        P(),
        P(),
        P(),
        P(),
        P(),
        P(),
        P(),
    )
    return jax.shard_map(
        on_device, mesh=fine, in_specs=placed, out_specs=P(dp, mp), check_vma=False
    )
```

```python
import numpy as np
import jax
import jax.numpy as jnp
from jax import lax
from jax.experimental import pallas as pl
from jax.experimental.pallas import tpu as pltpu
from jax.sharding import Mesh, PartitionSpec as P

epsilon = 1e-05
F32 = jnp.float32
BF16 = jnp.bfloat16


def rotary_tables(seq_span, head_size):
    half = head_size // 2
    power = (np.arange(half, dtype=np.float32) * np.float32(2.0 / head_size)).astype(np.float32)
    frequency = (np.float32(1.0) / np.power(np.float32(10000.0), power)).astype(np.float32)
    angles = (np.arange(seq_span, dtype=np.float32)[:, None] * frequency[None, :]).astype(np.float32)
    cosine = np.cos(angles.astype(np.float64)).astype(np.float32)
    sine = np.sin(angles.astype(np.float64)).astype(np.float32)
    wide = np.concatenate([cosine] * 4 + [-sine, sine] * 2, axis=1)
    rest = np.concatenate([cosine, sine], axis=1)
    parts = []
    for _ in range(3):
        parts.append(rest.astype(BF16))
        rest = rest - parts[-1].astype(np.float32)
    parts.append(np.zeros_like(parts[0]))
    return wide, np.concatenate(parts, axis=1)


def nt_dot(a, b):
    return lax.dot_general(a, b, (((1,), (1,)), ((), ())), preferred_element_type=F32)


def nn_dot(a, b, **options):
    return lax.dot_general(a, b, (((1,), (0,)), ((), ())), preferred_element_type=F32, **options)


def rotate(part, table, half):
    cos_table, sin_table = table[:, :128], table[:, 128:]
    width = part.shape[1]
    lane = lax.broadcasted_iota(jnp.int32, part.shape, 1) % (2 * half)
    turned = jnp.where(
        lane < half,
        pltpu.roll(part, width - half, 1),
        pltpu.roll(part, half, 1),
    )
    return part * cos_table + turned * sin_table


IN_PLACE = pl.BlockSpec(memory_space=pltpu.MemorySpace.HBM)
ON_CHIP = pl.BlockSpec(memory_space=pltpu.MemorySpace.VMEM)


def call(kernel, outs, args, n_any=0, scratch=(), flops=0, exps=0, vmem=24 * 1024 * 1024):
    moved = sum(a.size * a.dtype.itemsize for a in list(args) + jax.tree.leaves(outs))
    place = pltpu.with_memory_space_constraint
    args = [place(a, pltpu.HBM) if i < n_any else a for i, a in enumerate(args)]
    return pl.pallas_call(
        kernel,
        out_shape=outs,
        in_specs=[IN_PLACE] * n_any + [ON_CHIP] * (len(args) - n_any),
        out_specs=jax.tree.map(lambda _: ON_CHIP, outs),
        scratch_shapes=list(scratch),
        cost_estimate=pl.CostEstimate(flops=flops, transcendentals=exps, bytes_accessed=moved),
        compiler_params=pltpu.CompilerParams(vmem_limit_bytes=vmem),
    )(*args)


def pack_kernel(turned_ref, out_ref, key_ref, value_ref, sems):
    size = out_ref.shape[0]
    copies = (
        pltpu.make_async_copy(turned_ref.at[: 2 * size], key_ref, sems.at[0]),
        pltpu.make_async_copy(turned_ref.at[2 * size :], value_ref.at[:size], sems.at[1]),
        pltpu.make_async_copy(out_ref, value_ref.at[size:], sems.at[2]),
    )
    for copy in copies:
        copy.start()
    for copy in copies:
        copy.wait()


def pack(turned, out_weight):
    size, feature = out_weight.shape
    return call(
        pack_kernel,
        [jax.ShapeDtypeStruct((2 * size, feature), BF16)] * 2,
        (turned, out_weight),
        n_any=2,
        scratch=[pltpu.SemaphoreType.DMA((3,))],
    )


def first(mask, values):
    picked = jnp.sum(jnp.where(mask, values, 0), axis=1, keepdims=True)
    return jnp.sum(picked, axis=0, keepdims=True)


def norm_rows(values, gain):
    average = jnp.mean(values, axis=1, keepdims=True)
    centred = values - average
    variance = jnp.mean(centred * centred, axis=1, keepdims=True)
    return (centred * lax.rsqrt(variance + epsilon) * gain).astype(BF16)


def prepare_kernel(mine, small_refs, pick_ref, states_from, table_from, out_refs, scratch, sems):
    normed_ref, picked_ref, rows_ref, qtable_ref, meta_ref = out_refs[:5]
    copies = [
        pltpu.make_async_copy(source, target, sems.at[i])
        for i, (source, target) in enumerate(zip((*small_refs, pick_ref), scratch))
    ]
    late = []
    if mine:
        states_ref = scratch[7]
        late = [
            pltpu.make_async_copy(states_from, states_ref, sems.at[7]),
            pltpu.make_async_copy(table_from, out_refs[5], sems.at[8]),
        ]
    else:
        states_ref = states_from
    for copy in (*copies, *late):
        copy.start()
    sequence_ref, length_ref, owner_ref, codes_ref, tokens_ref, gain_ref, pick_ref = scratch[:7]
    span, feature = normed_ref.shape
    masks = codes_ref.shape[0]
    core = lax.axis_index("core")
    core = core if mine else 1 - core
    copy_id = (
        (lax.axis_index("z") * 2 + core) * 4 + lax.axis_index("y")
    ) * 4 + lax.axis_index("x")
    copies[5].wait()
    block = 16

    def norm_all():
        gain = gain_ref[...].reshape(1, -1)

        def step(i, carry):
            at = pl.multiple_of(i * block, block)
            values = states_ref[pl.ds(at, block), :].astype(F32)
            normed_ref[pl.ds(at, block), :] = norm_rows(values, gain)
            return carry

        lax.fori_loop(0, span // block, step, 0, unroll=20)

    if not mine:
        norm_all()
    for copy in (*copies[:5], copies[6]):
        copy.wait()

    def numbers(count):
        return lax.broadcasted_iota(jnp.int32, (1, count), 1)

    own = numbers(codes_ref.shape[1]) == copy_id
    sequence = first(own, sequence_ref[...].reshape(1, -1))
    owner = first(own, owner_ref[...].reshape(1, -1))
    length = first(numbers(length_ref.shape[0]) == sequence, length_ref[...].reshape(1, -1))
    codes = jnp.sum(jnp.where(own, codes_ref[...], 0), axis=1, keepdims=True)
    quotient = jnp.floor(codes.astype(F32) / length.astype(F32)).astype(jnp.int32)
    positions = codes - quotient * length
    positions = jnp.where(positions < 0, positions + length, positions)
    positions = jnp.where(positions >= length, positions - length, positions)
    hit = lax.broadcasted_iota(jnp.int32, (masks, span), 1) == positions
    line = lax.broadcasted_iota(jnp.int32, tokens_ref.shape, 0)
    tokens = jnp.sum(jnp.where(line == sequence, tokens_ref[...], 0), axis=0, keepdims=True)
    targets = jnp.sum(jnp.where(hit, tokens, 0), axis=1, keepdims=True)
    lane = lax.broadcasted_iota(jnp.int32, meta_ref.shape, 1)
    meta_ref[...] = jnp.where(lane == 0, targets, jnp.where(lane == 1, length, owner))
    hot = hit.astype(F32).astype(BF16)
    picks = nn_dot(hot, pick_ref[...])
    wide = picks.shape[1] // 4
    picks = picks[:, :wide] + picks[:, wide : 2 * wide] + picks[:, 2 * wide : 3 * wide]
    cosine, sine = picks[:, : wide // 2], picks[:, wide // 2 :]
    qtable_ref[...] = jnp.concatenate([cosine] * 4 + [-sine, sine] * 2, axis=1)
    for copy in late:
        copy.wait()
    if mine:
        norm_all()
    rows = nn_dot(hot, states_ref[...])
    rows_ref[...] = rows
    picked_ref[...] = norm_rows(rows, gain_ref[...].reshape(1, -1))


def attend(table_ref, normed_refs, picked_refs, qtable_refs, meta_refs, key_refs, value_refs):
    size = key_refs[0].shape[0] // 2
    masks = picked_refs[0].shape[0]
    heads = len(key_refs)
    width = heads * size
    weight = jnp.concatenate(
        [r[size:, :] for r in key_refs] + [r[:size, :] for r in value_refs], axis=0
    )
    query_weight = jnp.concatenate([r[:size, :] for r in key_refs], axis=0)
    picked = jnp.concatenate([r[...] for r in picked_refs], axis=0)
    queries = nt_dot(picked, query_weight) * 0.125
    results = []
    for which in range(2):
        length = meta_refs[which][0:1, 1:2]
        projected = nt_dot(normed_refs[which][...], weight)
        own = queries[masks * which : masks * (which + 1), :]
        turned_keys, turned_queries = [], []
        for i in range(heads // 2):
            lanes = slice(128 * i, 128 * (i + 1))
            turned_keys.append(rotate(projected[:, lanes], table_ref[...], size // 2))
            turned_queries.append(rotate(own[:, lanes], qtable_refs[which][...], size // 2))
        key_rows = jnp.concatenate(turned_keys, axis=1).astype(BF16)
        query_rows = jnp.concatenate(turned_queries, axis=1).astype(BF16)
        spread = jnp.concatenate([query_rows] * heads, axis=0)
        row = lax.broadcasted_iota(jnp.int32, spread.shape, 0) // masks
        lane = lax.broadcasted_iota(jnp.int32, spread.shape, 1) // size
        spread = jnp.where(row == lane, spread, jnp.zeros_like(spread))
        logits = nt_dot(spread, key_rows)
        alive = lax.broadcasted_iota(jnp.int32, logits.shape, 1) < length
        logits = jnp.where(alive, logits, -1e30)
        largest = jnp.max(logits, axis=1, keepdims=True)
        weights = jnp.exp(logits - largest)
        total = jnp.sum(weights, axis=1, keepdims=True)
        probs = (weights * (1.0 / total)).astype(BF16)
        results.append((probs, projected[:, width:].astype(BF16)))
    return results


def attend_kernel(*refs):
    inputs, (probs_ref, values_ref) = refs[:-2], refs[-2:]
    for which, (probs, values) in enumerate(attend(*inputs)):
        probs_ref[which] = probs
        values_ref[which] = values


def mix_columns(columns, probs, values, masks, size):
    right = (lax.axis_index("x") + lax.axis_index("y")) % 2 == lax.axis_index("core")

    def rows_of(step, which):
        start = masks * (which + (2 if step == 3 else 0))
        return probs[(0, 1, 2, 1)[step]](start, start + masks)

    stack = []
    for column in columns:
        which = column // 2
        for i in range(2):
            even = rows_of((0, 2)[i], which)
            odd = rows_of((1, 3)[i], which)
            if column % 2:
                even, odd = odd, even
            stack.append(jnp.where(right, even, odd))
    mixed = nn_dot(jnp.concatenate(stack, axis=0), values)
    lane = lax.broadcasted_iota(jnp.int32, (masks, mixed.shape[1]), 1) // size
    context = mixed[:masks, :]
    for head in range(1, len(stack)):
        context = jnp.where(lane == head, mixed[masks * head : masks * (head + 1), :], context)
    return context.astype(BF16)


def rows_reader(ref, copy):
    return lambda start, end: ref[copy, start:end, :]


def probs_kernel(*refs):
    inputs, probs_ref = refs[:-1], refs[-1]
    for which, (probs, _) in enumerate(attend(*inputs)):
        probs_ref[which] = probs


def mix_kernel(probs_refs, values_refs, normed_refs, far_refs, block_refs, partial_ref):
    size = block_refs[0].shape[0] // 2
    masks = probs_refs[0].shape[1] // 2
    value_weight = jnp.concatenate([r[:size, :] for r in far_refs], axis=0)
    contexts = []
    for copy in range(2):
        readers = [rows_reader(r, copy) for r in probs_refs]
        far = nt_dot(normed_refs[copy][...], value_weight).astype(BF16)
        values = (values_refs[0][copy], values_refs[1][copy], far)
        contexts.append(
            jnp.concatenate(
                [
                    mix_columns(columns, readers, value, masks, size)
                    for columns, value in zip(((0,), (1, 3), (2,)), values)
                ],
                axis=1,
            )
        )
    weight = jnp.concatenate([r[size:, :] for r in (*block_refs, *far_refs)], axis=0)
    partial_ref[...] = nn_dot(jnp.concatenate(contexts, axis=0), weight)


def join_kernel(low_ref, high_ref, line_ref):
    rows = low_ref.shape[0]
    line_ref[:rows, :] = low_ref[...]
    line_ref[rows:, :] = high_ref[...]


def join(low, high):
    line = jax.ShapeDtypeStruct((2 * low.shape[0], low.shape[1]), low.dtype)
    return call(join_kernel, line, (low, high))


def part(array, start, end):
    def kernel(array_ref, part_ref):
        part_ref[...] = array_ref[start:end, :]

    return call(kernel, jax.ShapeDtypeStruct((end - start, array.shape[1]), array.dtype), (array,))


def halves(ref):
    rows = ref.shape[0] // 2
    return ref.at[:rows], ref.at[rows:]


def score_kernel(
    rows_refs, partial_ref, arrived_ref, meta_refs, gain_ref, bias_ref, dense_ref, decoder_ref,
    placed_ref,
):
    masks = rows_refs[0].shape[0]
    residual = jnp.concatenate(
        [
            rows_refs[0][...] + (partial_ref[:masks, :] + arrived_ref[masks:, :]),
            rows_refs[1][...] + (partial_ref[masks:, :] + arrived_ref[:masks, :]),
        ],
        axis=0,
    )
    targets = jnp.concatenate([r[:, 0:1] for r in meta_refs], axis=0)
    average = jnp.mean(residual, axis=1, keepdims=True)
    centred = residual - average
    variance = jnp.mean(centred * centred, axis=1, keepdims=True)
    normed = (centred * lax.rsqrt(variance + epsilon) * gain_ref[...]).astype(BF16)
    dense = nn_dot(normed, dense_ref[...])
    active = 0.5 * dense * (1.0 + lax.erf(dense * np.float32(0.5**0.5)))
    average = jnp.mean(active, axis=1, keepdims=True)
    centred = active - average
    variance = jnp.mean(centred * centred, axis=1, keepdims=True)
    headed = (centred * lax.rsqrt(variance + epsilon)).astype(BF16)
    logits = nt_dot(headed, decoder_ref[...]) + bias_ref[...]
    largest = jnp.max(logits, axis=1, keepdims=True)
    total = jnp.sum(jnp.exp(logits - largest), axis=1, keepdims=True)
    vocab = lax.broadcasted_iota(jnp.int32, logits.shape, 1)
    chosen = jnp.sum(jnp.where(vocab == targets, logits, 0.0), axis=1, keepdims=True)
    score = chosen - largest - jnp.log(total)
    devices, width = placed_ref.shape
    member = lax.broadcasted_iota(jnp.int32, (devices, masks), 0) % 16
    part = lax.broadcasted_iota(jnp.int32, (devices, masks), 1) // 4
    take = (member == part).astype(F32)
    fits = (
        lax.broadcasted_iota(jnp.int32, (masks, width), 0) % 4
        == lax.broadcasted_iota(jnp.int32, (masks, width), 1) % 4
    )
    layer = lax.broadcasted_iota(jnp.int32, (devices, width), 0) // 16
    slot = lax.broadcasted_iota(jnp.int32, (devices, width), 1) // 4
    wanted = 16 * (2 * layer + lax.axis_index("core")) + slot
    placed = jnp.zeros((devices, width), F32)
    for which in range(2):
        own = jnp.where(fits, score[masks * which : masks * (which + 1), :], 0.0)
        laid = nn_dot(take, own, precision=lax.Precision.HIGHEST)
        placed = jnp.where(wanted == meta_refs[which][0:1, 2:3], laid, placed)
    placed_ref[...] = placed


def collect_kernel(arrived_ref, scores_ref):
    own, rows = scores_ref.shape
    total = jnp.sum(arrived_ref[...], axis=0, keepdims=True)
    count = total.shape[1]
    row = lax.broadcasted_iota(jnp.int32, (count, count), 0)
    lane = lax.broadcasted_iota(jnp.int32, (count, count), 1)
    column = jnp.sum(jnp.where(row == lane, total, 0.0), axis=1, keepdims=True)
    row = lax.broadcasted_iota(jnp.int32, (count, rows), 0)
    slot = lax.broadcasted_iota(jnp.int32, (count, rows), 1)
    parts = [
        jnp.sum(jnp.where(row == slot * own + i, column, 0.0), axis=0, keepdims=True)
        for i in range(own)
    ]
    scores_ref[...] = jnp.concatenate(parts, axis=0)


def pull(array, axis, offset):
    size = lax.axis_size(axis)
    return lax.ppermute(array, axis, [((i + offset) % size, i) for i in range(size)])


def swap(array):
    return lax.ppermute(array, "core", [(0, 1), (1, 0)])


def after(array, *others):
    return lax.optimization_barrier((array, *others))[0]


def gather_line(block, axis, reach):
    near, far = [], []
    for core in range(2):
        for y in range(4):
            for x in range(4):
                def device(step):
                    to_y = (y + step) % 4 if axis == "y" else y
                    to_x = (x + step) % 4 if axis == "x" else x
                    return (((x + y) % 2) * 4 + to_y) * 4 + to_x

                source = (core * 4 + y) * 4 + x
                own = (x + y) % 2 == core
                near.append((source, device(-1 if own else 0)))
                far.append((source, device(1 if own else 2)))
    pairs = far if reach else near
    return lax.ppermute(block, ("core", "y", "x"), pairs)


def on_device(
    hidden_states,
    ln_attn_gain,
    w_qkv,
    output_weight,
    ln_final_gain,
    dense_weight,
    decoder_weight,
    decoder_bias,
    seq_tokens,
    seq_lengths,
    copy_sequence,
    mask_code,
    copy_owner,
):
    _, span, feature = hidden_states.shape
    size = output_weight.shape[0]
    masks = mask_code.shape[1]
    table, pick_table = (jnp.asarray(t) for t in rotary_tables(span, size))
    shape = jax.ShapeDtypeStruct

    def prepare_call(mine, states):
        small = [copy_sequence, seq_lengths, copy_owner, mask_code.T, seq_tokens, ln_attn_gain]
        outs = [
            shape((span, feature), BF16),
            shape((masks, feature), BF16),
            shape((masks, feature), F32),
            shape((masks, 256), F32),
            shape((masks, 128), jnp.int32),
        ]
        args = [*small, pick_table, table, states] if mine else [*small, pick_table, states]
        scratch = [pltpu.VMEM(a.shape, a.dtype) for a in (*small, pick_table)]
        if mine:
            outs.append(shape(table.shape, F32))
            scratch.append(pltpu.VMEM(states.shape, states.dtype))
        n, m = len(args), len(outs)

        def kernel(*refs):
            prepare_kernel(
                mine, refs[:6], refs[6], refs[n - 1], refs[7], refs[n : n + m], refs[n + m : -1],
                refs[-1],
            )

        return call(
            kernel,
            outs,
            args,
            n_any=9 if mine else 7,
            scratch=[*scratch, pltpu.SemaphoreType.DMA((9,))],
            flops=4 * masks * span * feature + 10 * span * feature,
        )

    def attend_args(ready, key_blocks, value_blocks):
        per_copy = [r[i] for i in (0, 1, 3, 4) for r in ready]
        return (ready[0][5], *per_copy, *key_blocks, *value_blocks)

    def attend_refs(refs, keys, values):
        return (refs[0], refs[1:3], refs[3:5], refs[5:7], refs[7:9], keys, values)

    def attend_call(ready, key_lines, value_lines):
        count = len(key_lines)

        def kernel(*refs):
            lines = [halves(r) for r in refs[9:-2]]
            keys = [h for line in lines[:count] for h in line]
            values = [h for line in lines[count:] for h in line]
            attend_kernel(*attend_refs(refs, keys, values), *refs[-2:])

        heads = 2 * count
        return call(
            kernel,
            [
                shape((2, heads * masks, span), BF16),
                shape((2, span, heads * size), BF16),
            ],
            attend_args(ready, key_lines, value_lines),
            flops=4 * span * feature * heads * 128,
            exps=2 * heads * masks * span,
        )

    states = hidden_states[0]
    key_block, value_block = pack(jnp.transpose(w_qkv[:, 0, :]), output_weight[:, 0, :])
    key_low = gather_line(key_block, "x", False)
    value_low = gather_line(value_block, "y", False)
    key_high = gather_line(key_block, "x", True)
    value_high = gather_line(value_block, "y", True)
    states_other = swap(states)
    key_line = join(key_low, key_high)
    key_ahead = pull(key_line, "y", 1)
    key_behind = pull(key_line, "y", 3)
    value_line = join(value_low, value_high)
    value_ahead = pull(value_line, "x", 1)
    value_behind = pull(value_line, "x", 3)
    mine = prepare_call(True, after(states, key_line, value_line))
    other = prepare_call(False, after(states_other, mine[0]))
    ready = (mine, other)
    own_probs, own_values = attend_call(ready, (key_line,), (value_line,))
    rows = key_line.shape[0]
    key_far = (
        pull(part(after(key_ahead, own_probs), 0, rows // 2), "y", 1),
        pull(part(after(key_behind, own_probs), rows // 2, rows), "y", 3),
    )
    value_far = (
        pull(part(after(value_ahead, own_probs), 0, rows // 2), "x", 1),
        pull(part(after(value_behind, own_probs), rows // 2, rows), "x", 3),
    )
    near_probs, near_values = attend_call(
        ready, (key_ahead, key_behind), (value_ahead, value_behind)
    )
    key_far = tuple(after(b, near_probs) for b in key_far)
    far_args = attend_args(ready, key_far, ())

    def far_kernel(*refs):
        probs_kernel(*attend_refs(refs, refs[9:11], ()), refs[-1])

    far_probs = call(
        far_kernel,
        shape((2, 2 * masks, span), BF16),
        far_args,
        flops=4 * span * feature * 256,
        exps=4 * masks * span,
    )
    value_far = tuple(after(b, far_probs) for b in value_far)

    def mix(*refs):
        blocks = [h for r in refs[9:12] for h in halves(r)]
        mix_kernel(refs[:3], refs[3:5], refs[5:7], refs[7:9], blocks, refs[12])

    partial = call(
        mix,
        shape((2 * masks, feature), F32),
        (
            own_probs, near_probs, far_probs, own_values, near_values, mine[0], other[0],
            *value_far, value_line, value_ahead, value_behind,
        ),
        flops=4 * span * feature * 256 + 4 * masks * feature * 8 * size,
    )

    def score(*refs):
        score_kernel(refs[:2], *refs[2:4], refs[4:6], *refs[6:])

    placed = call(
        score,
        shape((128, 64), F32),
        (
            mine[2], other[2], partial, swap(partial), mine[4], other[4],
            ln_final_gain.reshape(1, -1), decoder_bias.reshape(1, -1), dense_weight,
            decoder_weight.T,
        ),
        flops=4 * masks * feature * feature,
    )
    arrived = lax.all_to_all(placed, ("z", "y", "x"), 0, 0, tiled=True)
    return call(collect_kernel, shape((4, 16), F32), (arrived,)).T


def solution(mesh):
    fine = Mesh(mesh.devices.reshape(8, 2, 4, 4), ("z", "core", "y", "x"))
    dp, mp = ("z", "core"), ("y", "x")
    placed = (
        P(("z", "core", "y", "x"), None, None),
        P(),
        P(None, mp, None),
        P(None, mp, None),
        P(),
        P(),
        P(),
        P(),
        P(),
        P(),
        P(),
        P(),
        P(),
    )
    return jax.shard_map(
        on_device, mesh=fine, in_specs=placed, out_specs=P(dp, mp), check_vma=False
    )
```

```python
import numpy as np
import jax
import jax.numpy as jnp
from jax import lax
from jax.experimental import pallas as pl
from jax.experimental.pallas import tpu as pltpu
from jax.sharding import Mesh, PartitionSpec as P

epsilon = 1e-05
F32 = jnp.float32
BF16 = jnp.bfloat16


def rotary_tables(seq_span, head_size):
    half = head_size // 2
    power = (np.arange(half, dtype=np.float32) * np.float32(2.0 / head_size)).astype(np.float32)
    frequency = (np.float32(1.0) / np.power(np.float32(10000.0), power)).astype(np.float32)
    angles = (np.arange(seq_span, dtype=np.float32)[:, None] * frequency[None, :]).astype(np.float32)
    cosine = np.cos(angles.astype(np.float64)).astype(np.float32)
    sine = np.sin(angles.astype(np.float64)).astype(np.float32)
    wide = np.concatenate([cosine] * 4 + [-sine, sine] * 2, axis=1)
    rest = np.concatenate([cosine, sine], axis=1)
    parts = []
    for _ in range(3):
        parts.append(rest.astype(BF16))
        rest = rest - parts[-1].astype(np.float32)
    parts.append(np.zeros_like(parts[0]))
    return wide, np.concatenate(parts, axis=1)


def nt_dot(a, b):
    return lax.dot_general(a, b, (((1,), (1,)), ((), ())), preferred_element_type=F32)


def nn_dot(a, b, **options):
    return lax.dot_general(a, b, (((1,), (0,)), ((), ())), preferred_element_type=F32, **options)


def rotate(part, table, half):
    cos_table, sin_table = table[:, :128], table[:, 128:]
    width = part.shape[1]
    lane = lax.broadcasted_iota(jnp.int32, part.shape, 1) % (2 * half)
    turned = jnp.where(
        lane < half,
        pltpu.roll(part, width - half, 1),
        pltpu.roll(part, half, 1),
    )
    return part * cos_table + turned * sin_table


IN_PLACE = pl.BlockSpec(memory_space=pltpu.MemorySpace.HBM)
ON_CHIP = pl.BlockSpec(memory_space=pltpu.MemorySpace.VMEM)


def call(kernel, outs, args, n_any=0, scratch=(), flops=0, exps=0, vmem=24 * 1024 * 1024):
    moved = sum(a.size * a.dtype.itemsize for a in list(args) + jax.tree.leaves(outs))
    place = pltpu.with_memory_space_constraint
    args = [place(a, pltpu.HBM) if i < n_any else a for i, a in enumerate(args)]
    return pl.pallas_call(
        kernel,
        out_shape=outs,
        in_specs=[IN_PLACE] * n_any + [ON_CHIP] * (len(args) - n_any),
        out_specs=jax.tree.map(lambda _: ON_CHIP, outs),
        scratch_shapes=list(scratch),
        cost_estimate=pl.CostEstimate(flops=flops, transcendentals=exps, bytes_accessed=moved),
        compiler_params=pltpu.CompilerParams(vmem_limit_bytes=vmem),
    )(*args)


def pack_kernel(turned_ref, out_ref, key_ref, value_ref, sems):
    size = out_ref.shape[0]
    copies = (
        pltpu.make_async_copy(turned_ref.at[: 2 * size], key_ref, sems.at[0]),
        pltpu.make_async_copy(turned_ref.at[2 * size :], value_ref.at[:size], sems.at[1]),
        pltpu.make_async_copy(out_ref, value_ref.at[size:], sems.at[2]),
    )
    for copy in copies:
        copy.start()
    for copy in copies:
        copy.wait()


def pack(turned, out_weight):
    size, feature = out_weight.shape
    return call(
        pack_kernel,
        [jax.ShapeDtypeStruct((2 * size, feature), BF16)] * 2,
        (turned, out_weight),
        n_any=2,
        scratch=[pltpu.SemaphoreType.DMA((3,))],
    )


def first(mask, values):
    picked = jnp.sum(jnp.where(mask, values, 0), axis=1, keepdims=True)
    return jnp.sum(picked, axis=0, keepdims=True)


def norm_rows(values, gain):
    average = jnp.mean(values, axis=1, keepdims=True)
    centred = values - average
    variance = jnp.mean(centred * centred, axis=1, keepdims=True)
    return (centred * lax.rsqrt(variance + epsilon) * gain).astype(BF16)


def prepare_kernel(mine, small_refs, pick_ref, states_from, table_from, out_refs, scratch, sems):
    normed_ref, picked_ref, rows_ref, qtable_ref, meta_ref = out_refs[:5]
    copies = [
        pltpu.make_async_copy(source, target, sems.at[i])
        for i, (source, target) in enumerate(zip((*small_refs, pick_ref), scratch))
    ]
    late = []
    if mine:
        states_ref = scratch[7]
        late = [
            pltpu.make_async_copy(states_from, states_ref, sems.at[7]),
            pltpu.make_async_copy(table_from, out_refs[5], sems.at[8]),
        ]
    else:
        states_ref = states_from
    for copy in (*copies, *late):
        copy.start()
    sequence_ref, length_ref, owner_ref, codes_ref, tokens_ref, gain_ref, pick_ref = scratch[:7]
    span, feature = normed_ref.shape
    masks = codes_ref.shape[0]
    core = lax.axis_index("core")
    core = core if mine else 1 - core
    copy_id = (
        (lax.axis_index("z") * 2 + core) * 4 + lax.axis_index("y")
    ) * 4 + lax.axis_index("x")
    copies[5].wait()
    block = 16

    def norm_all():
        gain = gain_ref[...].reshape(1, -1)

        def step(i, carry):
            at = pl.multiple_of(i * block, block)
            values = states_ref[pl.ds(at, block), :].astype(F32)
            normed_ref[pl.ds(at, block), :] = norm_rows(values, gain)
            return carry

        lax.fori_loop(0, span // block, step, 0, unroll=20)

    if not mine:
        norm_all()
    for copy in (*copies[:5], copies[6]):
        copy.wait()

    def numbers(count):
        return lax.broadcasted_iota(jnp.int32, (1, count), 1)

    own = numbers(codes_ref.shape[1]) == copy_id
    sequence = first(own, sequence_ref[...].reshape(1, -1))
    owner = first(own, owner_ref[...].reshape(1, -1))
    length = first(numbers(length_ref.shape[0]) == sequence, length_ref[...].reshape(1, -1))
    codes = jnp.sum(jnp.where(own, codes_ref[...], 0), axis=1, keepdims=True)
    quotient = jnp.floor(codes.astype(F32) / length.astype(F32)).astype(jnp.int32)
    positions = codes - quotient * length
    positions = jnp.where(positions < 0, positions + length, positions)
    positions = jnp.where(positions >= length, positions - length, positions)
    hit = lax.broadcasted_iota(jnp.int32, (masks, span), 1) == positions
    line = lax.broadcasted_iota(jnp.int32, tokens_ref.shape, 0)
    tokens = jnp.sum(jnp.where(line == sequence, tokens_ref[...], 0), axis=0, keepdims=True)
    targets = jnp.sum(jnp.where(hit, tokens, 0), axis=1, keepdims=True)
    lane = lax.broadcasted_iota(jnp.int32, meta_ref.shape, 1)
    meta_ref[...] = jnp.where(lane == 0, targets, jnp.where(lane == 1, length, owner))
    hot = hit.astype(F32).astype(BF16)
    picks = nn_dot(hot, pick_ref[...])
    wide = picks.shape[1] // 4
    picks = picks[:, :wide] + picks[:, wide : 2 * wide] + picks[:, 2 * wide : 3 * wide]
    cosine, sine = picks[:, : wide // 2], picks[:, wide // 2 :]
    qtable_ref[...] = jnp.concatenate([cosine] * 4 + [-sine, sine] * 2, axis=1)
    for copy in late:
        copy.wait()
    if mine:
        norm_all()
    rows = nn_dot(hot, states_ref[...])
    rows_ref[...] = rows
    picked_ref[...] = norm_rows(rows, gain_ref[...].reshape(1, -1))


def attend(table_ref, normed_refs, picked_refs, qtable_refs, meta_refs, key_refs, value_refs):
    size = key_refs[0].shape[0] // 2
    masks = picked_refs[0].shape[0]
    heads = len(key_refs)
    width = heads * size
    weight = jnp.concatenate(
        [r[size:, :] for r in key_refs] + [r[:size, :] for r in value_refs], axis=0
    )
    query_weight = jnp.concatenate([r[:size, :] for r in key_refs], axis=0)
    picked = jnp.concatenate([r[...] for r in picked_refs], axis=0)
    queries = nt_dot(picked, query_weight) * 0.125
    results = []
    for which in range(2):
        length = meta_refs[which][0:1, 1:2]
        projected = nt_dot(normed_refs[which][...], weight)
        own = queries[masks * which : masks * (which + 1), :]
        turned_keys, turned_queries = [], []
        for i in range(heads // 2):
            lanes = slice(128 * i, 128 * (i + 1))
            turned_keys.append(rotate(projected[:, lanes], table_ref[...], size // 2))
            turned_queries.append(rotate(own[:, lanes], qtable_refs[which][...], size // 2))
        key_rows = jnp.concatenate(turned_keys, axis=1).astype(BF16)
        query_rows = jnp.concatenate(turned_queries, axis=1).astype(BF16)
        spread = jnp.concatenate([query_rows] * heads, axis=0)
        row = lax.broadcasted_iota(jnp.int32, spread.shape, 0) // masks
        lane = lax.broadcasted_iota(jnp.int32, spread.shape, 1) // size
        spread = jnp.where(row == lane, spread, jnp.zeros_like(spread))
        logits = nt_dot(spread, key_rows)
        alive = lax.broadcasted_iota(jnp.int32, logits.shape, 1) < length
        logits = jnp.where(alive, logits, -1e30)
        largest = jnp.max(logits, axis=1, keepdims=True)
        weights = jnp.exp(logits - largest)
        total = jnp.sum(weights, axis=1, keepdims=True)
        probs = (weights * (1.0 / total)).astype(BF16)
        results.append((probs, projected[:, width:].astype(BF16)))
    return results


def attend_kernel(*refs):
    inputs, (probs_ref, values_ref) = refs[:-2], refs[-2:]
    for which, (probs, values) in enumerate(attend(*inputs)):
        probs_ref[which] = probs
        values_ref[which] = values


def mix_columns(columns, probs, values, masks, size):
    right = (lax.axis_index("x") + lax.axis_index("y")) % 2 == lax.axis_index("core")

    def rows_of(step, which):
        start = masks * (which + (2 if step == 3 else 0))
        return probs[(0, 1, 2, 1)[step]](start, start + masks)

    stack = []
    for column in columns:
        which = column // 2
        for i in range(2):
            even = rows_of((0, 2)[i], which)
            odd = rows_of((1, 3)[i], which)
            if column % 2:
                even, odd = odd, even
            stack.append(jnp.where(right, even, odd))
    mixed = nn_dot(jnp.concatenate(stack, axis=0), values)
    lane = lax.broadcasted_iota(jnp.int32, (masks, mixed.shape[1]), 1) // size
    context = mixed[:masks, :]
    for head in range(1, len(stack)):
        context = jnp.where(lane == head, mixed[masks * head : masks * (head + 1), :], context)
    return context.astype(BF16)


def rows_reader(ref, copy):
    return lambda start, end: ref[copy, start:end, :]


def probs_kernel(*refs):
    inputs, probs_ref = refs[:-1], refs[-1]
    for which, (probs, _) in enumerate(attend(*inputs)):
        probs_ref[which] = probs


def mix_kernel(probs_refs, values_refs, normed_refs, far_refs, block_refs, partial_ref):
    size = block_refs[0].shape[0] // 2
    masks = probs_refs[0].shape[1] // 2
    value_weight = jnp.concatenate([r[:size, :] for r in far_refs], axis=0)
    contexts = []
    for copy in range(2):
        readers = [rows_reader(r, copy) for r in probs_refs]
        far = nt_dot(normed_refs[copy][...], value_weight).astype(BF16)
        values = (values_refs[0][copy], values_refs[1][copy], far)
        contexts.append(
            jnp.concatenate(
                [
                    mix_columns(columns, readers, value, masks, size)
                    for columns, value in zip(((0,), (1, 3), (2,)), values)
                ],
                axis=1,
            )
        )
    weight = jnp.concatenate([r[size:, :] for r in (*block_refs, *far_refs)], axis=0)
    partial_ref[...] = nn_dot(jnp.concatenate(contexts, axis=0), weight)


def join_kernel(low_ref, high_ref, line_ref):
    rows = low_ref.shape[0]
    line_ref[:rows, :] = low_ref[...]
    line_ref[rows:, :] = high_ref[...]


def join(low, high):
    line = jax.ShapeDtypeStruct((2 * low.shape[0], low.shape[1]), low.dtype)
    return call(join_kernel, line, (low, high))


def part(array, start, end):
    def kernel(array_ref, part_ref):
        part_ref[...] = array_ref[start:end, :]

    return call(kernel, jax.ShapeDtypeStruct((end - start, array.shape[1]), array.dtype), (array,))


def halves(ref):
    rows = ref.shape[0] // 2
    return ref.at[:rows], ref.at[rows:]


def score_kernel(
    rows_refs, partial_ref, arrived_ref, meta_refs, gain_ref, bias_ref, dense_ref, decoder_ref,
    placed_ref,
):
    masks = rows_refs[0].shape[0]
    residual = jnp.concatenate(
        [
            rows_refs[0][...] + (partial_ref[:masks, :] + arrived_ref[masks:, :]),
            rows_refs[1][...] + (partial_ref[masks:, :] + arrived_ref[:masks, :]),
        ],
        axis=0,
    )
    targets = jnp.concatenate([r[:, 0:1] for r in meta_refs], axis=0)
    average = jnp.mean(residual, axis=1, keepdims=True)
    centred = residual - average
    variance = jnp.mean(centred * centred, axis=1, keepdims=True)
    normed = (centred * lax.rsqrt(variance + epsilon) * gain_ref[...]).astype(BF16)
    dense = nn_dot(normed, dense_ref[...])
    active = 0.5 * dense * (1.0 + lax.erf(dense * np.float32(0.5**0.5)))
    average = jnp.mean(active, axis=1, keepdims=True)
    centred = active - average
    variance = jnp.mean(centred * centred, axis=1, keepdims=True)
    headed = (centred * lax.rsqrt(variance + epsilon)).astype(BF16)
    logits = nt_dot(headed, decoder_ref[...]) + bias_ref[...]
    largest = jnp.max(logits, axis=1, keepdims=True)
    total = jnp.sum(jnp.exp(logits - largest), axis=1, keepdims=True)
    vocab = lax.broadcasted_iota(jnp.int32, logits.shape, 1)
    chosen = jnp.sum(jnp.where(vocab == targets, logits, 0.0), axis=1, keepdims=True)
    score = chosen - largest - jnp.log(total)
    devices, width = placed_ref.shape
    member = lax.broadcasted_iota(jnp.int32, (devices, masks), 0) % 16
    part = lax.broadcasted_iota(jnp.int32, (devices, masks), 1) // 4
    take = (member == part).astype(F32)
    fits = (
        lax.broadcasted_iota(jnp.int32, (masks, width), 0) % 4
        == lax.broadcasted_iota(jnp.int32, (masks, width), 1) % 4
    )
    layer = lax.broadcasted_iota(jnp.int32, (devices, width), 0) // 16
    slot = lax.broadcasted_iota(jnp.int32, (devices, width), 1) // 4
    wanted = 16 * (2 * layer + lax.axis_index("core")) + slot
    placed = jnp.zeros((devices, width), F32)
    for which in range(2):
        own = jnp.where(fits, score[masks * which : masks * (which + 1), :], 0.0)
        laid = nn_dot(take, own, precision=lax.Precision.HIGHEST)
        placed = jnp.where(wanted == meta_refs[which][0:1, 2:3], laid, placed)
    placed_ref[...] = placed


def collect_kernel(arrived_ref, scores_ref):
    own, rows = scores_ref.shape
    total = jnp.sum(arrived_ref[...], axis=0, keepdims=True)
    count = total.shape[1]
    row = lax.broadcasted_iota(jnp.int32, (count, count), 0)
    lane = lax.broadcasted_iota(jnp.int32, (count, count), 1)
    column = jnp.sum(jnp.where(row == lane, total, 0.0), axis=1, keepdims=True)
    row = lax.broadcasted_iota(jnp.int32, (count, rows), 0)
    slot = lax.broadcasted_iota(jnp.int32, (count, rows), 1)
    parts = [
        jnp.sum(jnp.where(row == slot * own + i, column, 0.0), axis=0, keepdims=True)
        for i in range(own)
    ]
    scores_ref[...] = jnp.concatenate(parts, axis=0)


def pull(array, axis, offset):
    size = lax.axis_size(axis)
    return lax.ppermute(array, axis, [((i + offset) % size, i) for i in range(size)])


def swap(array):
    return lax.ppermute(array, "core", [(0, 1), (1, 0)])


def after(array, *others):
    return lax.optimization_barrier((array, *others))[0]


def gather_line(block, axis, reach):
    near, far = [], []
    for core in range(2):
        for y in range(4):
            for x in range(4):
                def device(step):
                    to_y = (y + step) % 4 if axis == "y" else y
                    to_x = (x + step) % 4 if axis == "x" else x
                    return (((x + y) % 2) * 4 + to_y) * 4 + to_x

                source = (core * 4 + y) * 4 + x
                own = (x + y) % 2 == core
                near.append((source, device(-1 if own else 0)))
                far.append((source, device(1 if own else 2)))
    pairs = far if reach else near
    return lax.ppermute(block, ("core", "y", "x"), pairs)


def on_device(
    hidden_states,
    ln_attn_gain,
    w_qkv,
    output_weight,
    ln_final_gain,
    dense_weight,
    decoder_weight,
    decoder_bias,
    seq_tokens,
    seq_lengths,
    copy_sequence,
    mask_code,
    copy_owner,
):
    _, span, feature = hidden_states.shape
    size = output_weight.shape[0]
    masks = mask_code.shape[1]
    table, pick_table = (jnp.asarray(t) for t in rotary_tables(span, size))
    shape = jax.ShapeDtypeStruct

    def prepare_call(mine, states):
        small = [copy_sequence, seq_lengths, copy_owner, mask_code.T, seq_tokens, ln_attn_gain]
        outs = [
            shape((span, feature), BF16),
            shape((masks, feature), BF16),
            shape((masks, feature), F32),
            shape((masks, 256), F32),
            shape((masks, 128), jnp.int32),
        ]
        args = [*small, pick_table, table, states] if mine else [*small, pick_table, states]
        scratch = [pltpu.VMEM(a.shape, a.dtype) for a in (*small, pick_table)]
        if mine:
            outs.append(shape(table.shape, F32))
            scratch.append(pltpu.VMEM(states.shape, states.dtype))
        n, m = len(args), len(outs)

        def kernel(*refs):
            prepare_kernel(
                mine, refs[:6], refs[6], refs[n - 1], refs[7], refs[n : n + m], refs[n + m : -1],
                refs[-1],
            )

        return call(
            kernel,
            outs,
            args,
            n_any=9 if mine else 7,
            scratch=[*scratch, pltpu.SemaphoreType.DMA((9,))],
            flops=4 * masks * span * feature + 10 * span * feature,
        )

    def attend_args(ready, key_blocks, value_blocks):
        per_copy = [r[i] for i in (0, 1, 3, 4) for r in ready]
        return (ready[0][5], *per_copy, *key_blocks, *value_blocks)

    def attend_refs(refs, keys, values):
        return (refs[0], refs[1:3], refs[3:5], refs[5:7], refs[7:9], keys, values)

    def attend_call(ready, key_lines, value_lines):
        count = len(key_lines)

        def kernel(*refs):
            lines = [halves(r) for r in refs[9:-2]]
            keys = [h for line in lines[:count] for h in line]
            values = [h for line in lines[count:] for h in line]
            attend_kernel(*attend_refs(refs, keys, values), *refs[-2:])

        heads = 2 * count
        return call(
            kernel,
            [
                shape((2, heads * masks, span), BF16),
                shape((2, span, heads * size), BF16),
            ],
            attend_args(ready, key_lines, value_lines),
            flops=4 * span * feature * heads * 128,
            exps=2 * heads * masks * span,
        )

    states = hidden_states[0]
    key_block, value_block = pack(jnp.transpose(w_qkv[:, 0, :]), output_weight[:, 0, :])
    key_low = gather_line(key_block, "x", False)
    value_low = gather_line(value_block, "y", False)
    key_high = gather_line(key_block, "x", True)
    value_high = gather_line(value_block, "y", True)
    states_other = swap(states)
    key_line = join(key_low, key_high)
    key_ahead = pull(key_line, "y", 1)
    key_behind = pull(key_line, "y", 3)
    value_line = join(value_low, value_high)
    value_ahead = pull(value_line, "x", 1)
    value_behind = pull(value_line, "x", 3)
    mine = prepare_call(True, after(states, key_line, value_line))
    other = prepare_call(False, after(states_other, mine[0]))
    ready = (mine, other)
    own_probs, own_values = attend_call(ready, (key_line,), (value_line,))
    rows = key_line.shape[0]
    cut = rows * 5 // 8
    key_far = (
        pull(part(after(key_ahead, own_probs), 0, cut), "y", 1),
        pull(part(after(key_behind, own_probs), cut, rows), "y", 3),
    )
    value_far = (
        pull(part(after(value_ahead, own_probs), 0, rows // 2), "x", 1),
        pull(part(after(value_behind, own_probs), rows // 2, rows), "x", 3),
    )
    near_probs, near_values = attend_call(
        ready, (key_ahead, key_behind), (value_ahead, value_behind)
    )
    key_far = tuple(after(b, near_probs) for b in key_far)
    far_args = attend_args(ready, key_far, ())

    def far_kernel(*refs):
        low_ref, high_ref, line_ref = refs[9], refs[10], refs[12]
        line_ref[:cut, :] = low_ref[...]
        line_ref[cut:, :] = high_ref[...]
        probs_kernel(*attend_refs(refs, halves(line_ref), ()), refs[11])

    far_probs = call(
        far_kernel,
        shape((2, 2 * masks, span), BF16),
        far_args,
        scratch=[pltpu.VMEM((rows, feature), BF16)],
        flops=4 * span * feature * 256,
        exps=4 * masks * span,
    )
    value_far = tuple(after(b, far_probs) for b in value_far)

    def mix(*refs):
        blocks = [h for r in refs[9:12] for h in halves(r)]
        mix_kernel(refs[:3], refs[3:5], refs[5:7], refs[7:9], blocks, refs[12])

    partial = call(
        mix,
        shape((2 * masks, feature), F32),
        (
            own_probs, near_probs, far_probs, own_values, near_values, mine[0], other[0],
            *value_far, value_line, value_ahead, value_behind,
        ),
        flops=4 * span * feature * 256 + 4 * masks * feature * 8 * size,
    )

    def score(*refs):
        score_kernel(refs[:2], *refs[2:4], refs[4:6], *refs[6:])

    placed = call(
        score,
        shape((128, 64), F32),
        (
            mine[2], other[2], partial, swap(partial), mine[4], other[4],
            ln_final_gain.reshape(1, -1), decoder_bias.reshape(1, -1), dense_weight,
            decoder_weight.T,
        ),
        flops=4 * masks * feature * feature,
    )
    arrived = lax.all_to_all(placed, ("z", "y", "x"), 0, 0, tiled=True)
    return call(collect_kernel, shape((4, 16), F32), (arrived,)).T


def solution(mesh):
    fine = Mesh(mesh.devices.reshape(8, 2, 4, 4), ("z", "core", "y", "x"))
    dp, mp = ("z", "core"), ("y", "x")
    placed = (
        P(("z", "core", "y", "x"), None, None),
        P(),
        P(None, mp, None),
        P(None, mp, None),
        P(),
        P(),
        P(),
        P(),
        P(),
        P(),
        P(),
        P(),
        P(),
    )
    return jax.shard_map(
        on_device, mesh=fine, in_specs=placed, out_specs=P(dp, mp), check_vma=False
    )
```

```python
import numpy as np
import jax
import jax.numpy as jnp
from jax import lax
from jax.experimental import pallas as pl
from jax.experimental.pallas import tpu as pltpu
from jax.sharding import Mesh, PartitionSpec as P

epsilon = 1e-05
F32 = jnp.float32
BF16 = jnp.bfloat16


def rotary_tables(seq_span, head_size):
    half = head_size // 2
    power = (np.arange(half, dtype=np.float32) * np.float32(2.0 / head_size)).astype(np.float32)
    frequency = (np.float32(1.0) / np.power(np.float32(10000.0), power)).astype(np.float32)
    angles = (np.arange(seq_span, dtype=np.float32)[:, None] * frequency[None, :]).astype(np.float32)
    cosine = np.cos(angles.astype(np.float64)).astype(np.float32)
    sine = np.sin(angles.astype(np.float64)).astype(np.float32)
    wide = np.concatenate([cosine] * 4 + [-sine, sine] * 2, axis=1)
    rest = np.concatenate([cosine, sine], axis=1)
    parts = []
    for _ in range(3):
        parts.append(rest.astype(BF16))
        rest = rest - parts[-1].astype(np.float32)
    parts.append(np.zeros_like(parts[0]))
    return wide, np.concatenate(parts, axis=1)


def nt_dot(a, b):
    return lax.dot_general(a, b, (((1,), (1,)), ((), ())), preferred_element_type=F32)


def nn_dot(a, b, **options):
    return lax.dot_general(a, b, (((1,), (0,)), ((), ())), preferred_element_type=F32, **options)


def rotate(part, table, half):
    cos_table, sin_table = table[:, :128], table[:, 128:]
    width = part.shape[1]
    lane = lax.broadcasted_iota(jnp.int32, part.shape, 1) % (2 * half)
    turned = jnp.where(
        lane < half,
        pltpu.roll(part, width - half, 1),
        pltpu.roll(part, half, 1),
    )
    return part * cos_table + turned * sin_table


IN_PLACE = pl.BlockSpec(memory_space=pltpu.MemorySpace.HBM)
ON_CHIP = pl.BlockSpec(memory_space=pltpu.MemorySpace.VMEM)


def call(kernel, outs, args, n_any=0, scratch=(), flops=0, exps=0, vmem=24 * 1024 * 1024):
    moved = sum(a.size * a.dtype.itemsize for a in list(args) + jax.tree.leaves(outs))
    place = pltpu.with_memory_space_constraint
    args = [place(a, pltpu.HBM) if i < n_any else a for i, a in enumerate(args)]
    return pl.pallas_call(
        kernel,
        out_shape=outs,
        in_specs=[IN_PLACE] * n_any + [ON_CHIP] * (len(args) - n_any),
        out_specs=jax.tree.map(lambda _: ON_CHIP, outs),
        scratch_shapes=list(scratch),
        cost_estimate=pl.CostEstimate(flops=flops, transcendentals=exps, bytes_accessed=moved),
        compiler_params=pltpu.CompilerParams(vmem_limit_bytes=vmem),
    )(*args)


def pack(*sources):
    def kernel(*refs):
        packed_ref, sems = refs[-2:]
        copies, at = [], 0
        for i, (ref, (_, start, end)) in enumerate(zip(refs, sources)):
            target = packed_ref.at[at : at + end - start]
            copies.append(pltpu.make_async_copy(ref.at[start:end], target, sems.at[i]))
            at += end - start
        for copy in copies:
            copy.start()
        for copy in copies:
            copy.wait()

    rows = sum(end - start for _, start, end in sources)
    arrays = [array for array, _, _ in sources]
    return call(
        kernel,
        jax.ShapeDtypeStruct((rows, arrays[0].shape[1]), BF16),
        arrays,
        n_any=len(arrays),
        scratch=[pltpu.SemaphoreType.DMA((len(arrays),))],
    )


def first(mask, values):
    picked = jnp.sum(jnp.where(mask, values, 0), axis=1, keepdims=True)
    return jnp.sum(picked, axis=0, keepdims=True)


def norm_rows(values, gain):
    average = jnp.mean(values, axis=1, keepdims=True)
    centred = values - average
    variance = jnp.mean(centred * centred, axis=1, keepdims=True)
    return (centred * lax.rsqrt(variance + epsilon) * gain).astype(BF16)


def prepare_kernel(mine, small_refs, pick_ref, states_from, table_from, out_refs, scratch, sems):
    normed_ref, picked_ref, rows_ref, qtable_ref, meta_ref = out_refs[:5]
    copies = [
        pltpu.make_async_copy(source, target, sems.at[i])
        for i, (source, target) in enumerate(zip((*small_refs, pick_ref), scratch))
    ]
    late = []
    if mine:
        states_ref = scratch[7]
        late = [
            pltpu.make_async_copy(states_from, states_ref, sems.at[7]),
            pltpu.make_async_copy(table_from, out_refs[5], sems.at[8]),
        ]
    else:
        states_ref = states_from
    for copy in (*copies, *late):
        copy.start()
    sequence_ref, length_ref, owner_ref, codes_ref, tokens_ref, gain_ref, pick_ref = scratch[:7]
    span, feature = normed_ref.shape
    masks = codes_ref.shape[0]
    core = lax.axis_index("core")
    core = core if mine else 1 - core
    copy_id = (
        (lax.axis_index("z") * 2 + core) * 4 + lax.axis_index("y")
    ) * 4 + lax.axis_index("x")
    copies[5].wait()
    block = 16

    def norm_all():
        gain = gain_ref[...].reshape(1, -1)

        def step(i, carry):
            at = pl.multiple_of(i * block, block)
            values = states_ref[pl.ds(at, block), :].astype(F32)
            normed_ref[pl.ds(at, block), :] = norm_rows(values, gain)
            return carry

        lax.fori_loop(0, span // block, step, 0, unroll=20)

    if not mine:
        norm_all()
    for copy in (*copies[:5], copies[6]):
        copy.wait()

    def numbers(count):
        return lax.broadcasted_iota(jnp.int32, (1, count), 1)

    own = numbers(codes_ref.shape[1]) == copy_id
    sequence = first(own, sequence_ref[...].reshape(1, -1))
    owner = first(own, owner_ref[...].reshape(1, -1))
    length = first(numbers(length_ref.shape[0]) == sequence, length_ref[...].reshape(1, -1))
    codes = jnp.sum(jnp.where(own, codes_ref[...], 0), axis=1, keepdims=True)
    quotient = jnp.floor(codes.astype(F32) / length.astype(F32)).astype(jnp.int32)
    positions = codes - quotient * length
    positions = jnp.where(positions < 0, positions + length, positions)
    positions = jnp.where(positions >= length, positions - length, positions)
    hit = lax.broadcasted_iota(jnp.int32, (masks, span), 1) == positions
    line = lax.broadcasted_iota(jnp.int32, tokens_ref.shape, 0)
    tokens = jnp.sum(jnp.where(line == sequence, tokens_ref[...], 0), axis=0, keepdims=True)
    targets = jnp.sum(jnp.where(hit, tokens, 0), axis=1, keepdims=True)
    lane = lax.broadcasted_iota(jnp.int32, meta_ref.shape, 1)
    meta_ref[...] = jnp.where(lane == 0, targets, jnp.where(lane == 1, length, owner))
    hot = hit.astype(F32).astype(BF16)
    picks = nn_dot(hot, pick_ref[...])
    wide = picks.shape[1] // 4
    picks = picks[:, :wide] + picks[:, wide : 2 * wide] + picks[:, 2 * wide : 3 * wide]
    cosine, sine = picks[:, : wide // 2], picks[:, wide // 2 :]
    qtable_ref[...] = jnp.concatenate([cosine] * 4 + [-sine, sine] * 2, axis=1)
    for copy in late:
        copy.wait()
    if mine:
        norm_all()
    rows = nn_dot(hot, states_ref[...])
    rows_ref[...] = rows
    picked_ref[...] = norm_rows(rows, gain_ref[...].reshape(1, -1))


def attend(table_ref, normed_refs, picked_refs, qtable_refs, meta_refs, key_refs, value_refs):
    size = key_refs[0].shape[0] // 2
    masks = picked_refs[0].shape[0]
    heads = len(key_refs)
    width = heads * size
    weight = jnp.concatenate(
        [r[size:, :] for r in key_refs] + [r[:size, :] for r in value_refs], axis=0
    )
    query_weight = jnp.concatenate([r[:size, :] for r in key_refs], axis=0)
    picked = jnp.concatenate([r[...] for r in picked_refs], axis=0)
    queries = nt_dot(picked, query_weight) * 0.125
    results = []
    for which in range(2):
        length = meta_refs[which][0:1, 1:2]
        projected = nt_dot(normed_refs[which][...], weight)
        own = queries[masks * which : masks * (which + 1), :]
        turned_keys, turned_queries = [], []
        for i in range(heads // 2):
            lanes = slice(128 * i, 128 * (i + 1))
            turned_keys.append(rotate(projected[:, lanes], table_ref[...], size // 2))
            turned_queries.append(rotate(own[:, lanes], qtable_refs[which][...], size // 2))
        key_rows = jnp.concatenate(turned_keys, axis=1).astype(BF16)
        query_rows = jnp.concatenate(turned_queries, axis=1).astype(BF16)
        spread = jnp.concatenate([query_rows] * heads, axis=0)
        row = lax.broadcasted_iota(jnp.int32, spread.shape, 0) // masks
        lane = lax.broadcasted_iota(jnp.int32, spread.shape, 1) // size
        spread = jnp.where(row == lane, spread, jnp.zeros_like(spread))
        logits = nt_dot(spread, key_rows)
        alive = lax.broadcasted_iota(jnp.int32, logits.shape, 1) < length
        logits = jnp.where(alive, logits, -1e30)
        largest = jnp.max(logits, axis=1, keepdims=True)
        weights = jnp.exp(logits - largest)
        total = jnp.sum(weights, axis=1, keepdims=True)
        probs = (weights * (1.0 / total)).astype(BF16)
        results.append((probs, projected[:, width:].astype(BF16)))
    return results


def attend_kernel(*refs):
    inputs, (probs_ref, values_ref) = refs[:-2], refs[-2:]
    for which, (probs, values) in enumerate(attend(*inputs)):
        probs_ref[which] = probs
        values_ref[which] = values


def mix_columns(columns, probs, values, masks, size):
    right = (lax.axis_index("x") + lax.axis_index("y")) % 2 == lax.axis_index("core")

    def rows_of(step, which):
        start = masks * (which + (2 if step == 3 else 0))
        return probs[(0, 1, 2, 1)[step]](start, start + masks)

    stack = []
    for column in columns:
        which = column // 2
        for i in range(2):
            even = rows_of((0, 2)[i], which)
            odd = rows_of((1, 3)[i], which)
            if column % 2:
                even, odd = odd, even
            stack.append(jnp.where(right, even, odd))
    mixed = nn_dot(jnp.concatenate(stack, axis=0), values)
    lane = lax.broadcasted_iota(jnp.int32, (masks, mixed.shape[1]), 1) // size
    context = mixed[:masks, :]
    for head in range(1, len(stack)):
        context = jnp.where(lane == head, mixed[masks * head : masks * (head + 1), :], context)
    return context.astype(BF16)


def rows_reader(ref, copy):
    return lambda start, end: ref[copy, start:end, :]


def probs_kernel(*refs):
    inputs, probs_ref = refs[:-1], refs[-1]
    for which, (probs, _) in enumerate(attend(*inputs)):
        probs_ref[which] = probs


def mix_kernel(
    probs_refs, values_refs, normed_refs, far_refs, block_refs, partial_ref, sent_ref
):
    size = block_refs[0].shape[0] // 2
    masks = probs_refs[0].shape[1] // 2
    value_weight = jnp.concatenate([r[:size, :] for r in far_refs], axis=0)
    contexts = []
    for copy in range(2):
        readers = [rows_reader(r, copy) for r in probs_refs]
        far = nt_dot(normed_refs[copy][...], value_weight).astype(BF16)
        values = (values_refs[0][copy], values_refs[1][copy], far)
        contexts.append(
            jnp.concatenate(
                [
                    mix_columns(columns, readers, value, masks, size)
                    for columns, value in zip(((0,), (1, 3), (2,)), values)
                ],
                axis=1,
            )
        )
    weight = jnp.concatenate([r[size:, :] for r in (*block_refs, *far_refs)], axis=0)
    partial = nn_dot(jnp.concatenate(contexts, axis=0), weight)
    partial_ref[...] = partial
    sent_ref[...] = partial.astype(BF16)


def join_kernel(low_ref, high_ref, line_ref):
    rows = low_ref.shape[0]
    line_ref[:rows, :] = low_ref[...]
    line_ref[rows:, :] = high_ref[...]


def join(low, high):
    line = jax.ShapeDtypeStruct((2 * low.shape[0], low.shape[1]), low.dtype)
    return call(join_kernel, line, (low, high))


def part(array, start, end):
    def kernel(array_ref, part_ref):
        part_ref[...] = array_ref[start:end, :]

    return call(kernel, jax.ShapeDtypeStruct((end - start, array.shape[1]), array.dtype), (array,))


def halves(ref):
    rows = ref.shape[0] // 2
    return ref.at[:rows], ref.at[rows:]


def score_kernel(
    rows_refs, partial_ref, arrived_ref, meta_refs, gain_ref, bias_ref, dense_ref, decoder_ref,
    placed_ref,
):
    masks = rows_refs[0].shape[0]
    arrived = arrived_ref[...].astype(F32)
    residual = jnp.concatenate(
        [
            rows_refs[0][...] + (partial_ref[:masks, :] + arrived[masks:, :]),
            rows_refs[1][...] + (partial_ref[masks:, :] + arrived[:masks, :]),
        ],
        axis=0,
    )
    targets = jnp.concatenate([r[:, 0:1] for r in meta_refs], axis=0)
    average = jnp.mean(residual, axis=1, keepdims=True)
    centred = residual - average
    variance = jnp.mean(centred * centred, axis=1, keepdims=True)
    normed = (centred * lax.rsqrt(variance + epsilon) * gain_ref[...]).astype(BF16)
    dense = nn_dot(normed, dense_ref[...])
    active = 0.5 * dense * (1.0 + lax.erf(dense * np.float32(0.5**0.5)))
    average = jnp.mean(active, axis=1, keepdims=True)
    centred = active - average
    variance = jnp.mean(centred * centred, axis=1, keepdims=True)
    headed = (centred * lax.rsqrt(variance + epsilon)).astype(BF16)
    logits = nt_dot(headed, decoder_ref[...]) + bias_ref[...]
    largest = jnp.max(logits, axis=1, keepdims=True)
    total = jnp.sum(jnp.exp(logits - largest), axis=1, keepdims=True)
    vocab = lax.broadcasted_iota(jnp.int32, logits.shape, 1)
    chosen = jnp.sum(jnp.where(vocab == targets, logits, 0.0), axis=1, keepdims=True)
    score = chosen - largest - jnp.log(total)
    devices, width = placed_ref.shape
    member = lax.broadcasted_iota(jnp.int32, (devices, masks), 0) % 16
    part = lax.broadcasted_iota(jnp.int32, (devices, masks), 1) // 4
    take = (member == part).astype(F32)
    fits = (
        lax.broadcasted_iota(jnp.int32, (masks, width), 0) % 4
        == lax.broadcasted_iota(jnp.int32, (masks, width), 1) % 4
    )
    layer = lax.broadcasted_iota(jnp.int32, (devices, width), 0) // 16
    slot = lax.broadcasted_iota(jnp.int32, (devices, width), 1) // 4
    wanted = 16 * (2 * layer + lax.axis_index("core")) + slot
    placed = jnp.zeros((devices, width), F32)
    for which in range(2):
        own = jnp.where(fits, score[masks * which : masks * (which + 1), :], 0.0)
        laid = nn_dot(take, own, precision=lax.Precision.HIGHEST)
        placed = jnp.where(wanted == meta_refs[which][0:1, 2:3], laid, placed)
    placed_ref[...] = placed


def collect_kernel(arrived_ref, scores_ref):
    own, rows = scores_ref.shape
    total = jnp.sum(arrived_ref[...], axis=0, keepdims=True)
    count = total.shape[1]
    row = lax.broadcasted_iota(jnp.int32, (count, count), 0)
    lane = lax.broadcasted_iota(jnp.int32, (count, count), 1)
    column = jnp.sum(jnp.where(row == lane, total, 0.0), axis=1, keepdims=True)
    row = lax.broadcasted_iota(jnp.int32, (count, rows), 0)
    slot = lax.broadcasted_iota(jnp.int32, (count, rows), 1)
    parts = [
        jnp.sum(jnp.where(row == slot * own + i, column, 0.0), axis=0, keepdims=True)
        for i in range(own)
    ]
    scores_ref[...] = jnp.concatenate(parts, axis=0)


def pull(array, axis, offset):
    size = lax.axis_size(axis)
    return lax.ppermute(array, axis, [((i + offset) % size, i) for i in range(size)])


def swap(array):
    return lax.ppermute(array, "core", [(0, 1), (1, 0)])


def after(array, *others):
    return lax.optimization_barrier((array, *others))[0]


def gather_line(block, axis, reach):
    near, far = [], []
    for core in range(2):
        for y in range(4):
            for x in range(4):
                def device(step):
                    to_y = (y + step) % 4 if axis == "y" else y
                    to_x = (x + step) % 4 if axis == "x" else x
                    return (((x + y) % 2) * 4 + to_y) * 4 + to_x

                source = (core * 4 + y) * 4 + x
                own = (x + y) % 2 == core
                near.append((source, device(-1 if own else 0)))
                far.append((source, device(1 if own else 2)))
    pairs = far if reach else near
    return lax.ppermute(block, ("core", "y", "x"), pairs)


def on_device(
    hidden_states,
    ln_attn_gain,
    w_qkv,
    output_weight,
    ln_final_gain,
    dense_weight,
    decoder_weight,
    decoder_bias,
    seq_tokens,
    seq_lengths,
    copy_sequence,
    mask_code,
    copy_owner,
):
    _, span, feature = hidden_states.shape
    size = output_weight.shape[0]
    masks = mask_code.shape[1]
    table, pick_table = (jnp.asarray(t) for t in rotary_tables(span, size))
    shape = jax.ShapeDtypeStruct

    def prepare_call(mine, states):
        small = [copy_sequence, seq_lengths, copy_owner, mask_code.T, seq_tokens, ln_attn_gain]
        outs = [
            shape((span, feature), BF16),
            shape((masks, feature), BF16),
            shape((masks, feature), F32),
            shape((masks, 256), F32),
            shape((masks, 128), jnp.int32),
        ]
        args = [*small, pick_table, table, states] if mine else [*small, pick_table, states]
        scratch = [pltpu.VMEM(a.shape, a.dtype) for a in (*small, pick_table)]
        if mine:
            outs.append(shape(table.shape, F32))
            scratch.append(pltpu.VMEM(states.shape, states.dtype))
        n, m = len(args), len(outs)

        def kernel(*refs):
            prepare_kernel(
                mine, refs[:6], refs[6], refs[n - 1], refs[7], refs[n : n + m], refs[n + m : -1],
                refs[-1],
            )

        return call(
            kernel,
            outs,
            args,
            n_any=9 if mine else 7,
            scratch=[*scratch, pltpu.SemaphoreType.DMA((9,))],
            flops=4 * masks * span * feature + 10 * span * feature,
        )

    def attend_args(ready, key_blocks, value_blocks):
        per_copy = [r[i] for i in (0, 1, 3, 4) for r in ready]
        return (ready[0][5], *per_copy, *key_blocks, *value_blocks)

    def attend_refs(refs, keys, values):
        return (refs[0], refs[1:3], refs[3:5], refs[5:7], refs[7:9], keys, values)

    def attend_call(ready, key_lines, value_lines):
        count = len(key_lines)

        def kernel(*refs):
            lines = [halves(r) for r in refs[9:-2]]
            keys = [h for line in lines[:count] for h in line]
            values = [h for line in lines[count:] for h in line]
            attend_kernel(*attend_refs(refs, keys, values), *refs[-2:])

        heads = 2 * count
        return call(
            kernel,
            [
                shape((2, heads * masks, span), BF16),
                shape((2, span, heads * size), BF16),
            ],
            attend_args(ready, key_lines, value_lines),
            flops=4 * span * feature * heads * 128,
            exps=2 * heads * masks * span,
        )

    states = hidden_states[0]
    turned = jnp.transpose(w_qkv[:, 0, :])
    key_block = pack((turned, 0, 2 * size))
    value_block = pack((turned, 2 * size, 3 * size), (output_weight[:, 0, :], 0, size))
    key_low = gather_line(key_block, "x", False)
    value_low = gather_line(value_block, "y", False)
    key_high = gather_line(key_block, "x", True)
    value_high = gather_line(value_block, "y", True)
    states_other = swap(states)
    key_line = join(key_low, key_high)
    key_ahead = pull(key_line, "y", 1)
    key_behind = pull(key_line, "y", 3)
    value_line = join(value_low, value_high)
    value_ahead = pull(value_line, "x", 1)
    value_behind = pull(value_line, "x", 3)
    mine = prepare_call(True, after(states, key_line, value_line))
    other = prepare_call(False, after(states_other, mine[0]))
    ready = (mine, other)
    own_probs, own_values = attend_call(ready, (key_line,), (value_line,))
    rows = key_line.shape[0]
    key_far = (
        pull(part(after(key_ahead, own_probs), 0, rows // 2), "y", 1),
        pull(part(after(key_behind, own_probs), rows // 2, rows), "y", 3),
    )
    value_far = (
        pull(part(after(value_ahead, own_probs), 0, rows // 2), "x", 1),
        pull(part(after(value_behind, own_probs), rows // 2, rows), "x", 3),
    )
    near_probs, near_values = attend_call(
        ready, (key_ahead, key_behind), (value_ahead, value_behind)
    )
    key_far = tuple(after(b, near_probs) for b in key_far)
    far_args = attend_args(ready, key_far, ())

    def far_kernel(*refs):
        probs_kernel(*attend_refs(refs, refs[9:11], ()), refs[-1])

    far_probs = call(
        far_kernel,
        shape((2, 2 * masks, span), BF16),
        far_args,
        flops=4 * span * feature * 256,
        exps=4 * masks * span,
    )
    value_far = tuple(after(b, far_probs) for b in value_far)

    def mix(*refs):
        blocks = [h for r in refs[9:12] for h in halves(r)]
        mix_kernel(refs[:3], refs[3:5], refs[5:7], refs[7:9], blocks, *refs[12:])

    partial, sent = call(
        mix,
        [shape((2 * masks, feature), F32), shape((2 * masks, feature), BF16)],
        (
            own_probs, near_probs, far_probs, own_values, near_values, mine[0], other[0],
            *value_far, value_line, value_ahead, value_behind,
        ),
        flops=4 * span * feature * 256 + 4 * masks * feature * 8 * size,
    )

    def score(*refs):
        score_kernel(refs[:2], *refs[2:4], refs[4:6], *refs[6:])

    placed = call(
        score,
        shape((128, 64), F32),
        (
            mine[2], other[2], partial, swap(sent), mine[4], other[4],
            ln_final_gain.reshape(1, -1), decoder_bias.reshape(1, -1), dense_weight,
            decoder_weight.T,
        ),
        flops=4 * masks * feature * feature,
    )
    arrived = lax.all_to_all(placed, ("z", "y", "x"), 0, 0, tiled=True)
    return call(collect_kernel, shape((4, 16), F32), (arrived,)).T


def solution(mesh):
    fine = Mesh(mesh.devices.reshape(8, 2, 4, 4), ("z", "core", "y", "x"))
    dp, mp = ("z", "core"), ("y", "x")
    placed = (
        P(("z", "core", "y", "x"), None, None),
        P(),
        P(None, mp, None),
        P(None, mp, None),
        P(),
        P(),
        P(),
        P(),
        P(),
        P(),
        P(),
        P(),
        P(),
    )
    return jax.shard_map(
        on_device, mesh=fine, in_specs=placed, out_specs=P(dp, mp), check_vma=False
    )
```

```python
import numpy as np
import jax
import jax.numpy as jnp
from jax import lax
from jax.experimental import pallas as pl
from jax.experimental.pallas import tpu as pltpu
from jax.sharding import Mesh, PartitionSpec as P

epsilon = 1e-05
F32 = jnp.float32
BF16 = jnp.bfloat16


def rotary_tables(seq_span, head_size):
    half = head_size // 2
    power = (np.arange(half, dtype=np.float32) * np.float32(2.0 / head_size)).astype(np.float32)
    frequency = (np.float32(1.0) / np.power(np.float32(10000.0), power)).astype(np.float32)
    angles = (np.arange(seq_span, dtype=np.float32)[:, None] * frequency[None, :]).astype(np.float32)
    cosine = np.cos(angles.astype(np.float64)).astype(np.float32)
    sine = np.sin(angles.astype(np.float64)).astype(np.float32)
    wide = np.concatenate([cosine] * 4 + [-sine, sine] * 2, axis=1)
    rest = np.concatenate([cosine, sine], axis=1)
    parts = []
    for _ in range(3):
        parts.append(rest.astype(BF16))
        rest = rest - parts[-1].astype(np.float32)
    parts.append(np.zeros_like(parts[0]))
    return wide, np.concatenate(parts, axis=1)


def nt_dot(a, b):
    return lax.dot_general(a, b, (((1,), (1,)), ((), ())), preferred_element_type=F32)


def nn_dot(a, b, **options):
    return lax.dot_general(a, b, (((1,), (0,)), ((), ())), preferred_element_type=F32, **options)


def rotate(part, table, half):
    cos_table, sin_table = table[:, :128], table[:, 128:]
    width = part.shape[1]
    lane = lax.broadcasted_iota(jnp.int32, part.shape, 1) % (2 * half)
    turned = jnp.where(
        lane < half,
        pltpu.roll(part, width - half, 1),
        pltpu.roll(part, half, 1),
    )
    return part * cos_table + turned * sin_table


IN_PLACE = pl.BlockSpec(memory_space=pltpu.MemorySpace.HBM)
ON_CHIP = pl.BlockSpec(memory_space=pltpu.MemorySpace.VMEM)


def call(kernel, outs, args, n_any=0, scratch=(), flops=0, exps=0, vmem=24 * 1024 * 1024):
    moved = sum(a.size * a.dtype.itemsize for a in list(args) + jax.tree.leaves(outs))
    place = pltpu.with_memory_space_constraint
    args = [place(a, pltpu.HBM) if i < n_any else a for i, a in enumerate(args)]
    return pl.pallas_call(
        kernel,
        out_shape=outs,
        in_specs=[IN_PLACE] * n_any + [ON_CHIP] * (len(args) - n_any),
        out_specs=jax.tree.map(lambda _: ON_CHIP, outs),
        scratch_shapes=list(scratch),
        cost_estimate=pl.CostEstimate(flops=flops, transcendentals=exps, bytes_accessed=moved),
        compiler_params=pltpu.CompilerParams(vmem_limit_bytes=vmem),
    )(*args)


def pack_kernel(turned_ref, out_ref, key_ref, value_ref, sems):
    size = out_ref.shape[0]
    copies = (
        pltpu.make_async_copy(turned_ref.at[: 2 * size], key_ref, sems.at[0]),
        pltpu.make_async_copy(turned_ref.at[2 * size :], value_ref.at[:size], sems.at[1]),
        pltpu.make_async_copy(out_ref, value_ref.at[size:], sems.at[2]),
    )
    for copy in copies:
        copy.start()
    for copy in copies:
        copy.wait()


def pack(turned, out_weight):
    size, feature = out_weight.shape
    return call(
        pack_kernel,
        [jax.ShapeDtypeStruct((2 * size, feature), BF16)] * 2,
        (turned, out_weight),
        n_any=2,
        scratch=[pltpu.SemaphoreType.DMA((3,))],
    )


def first(mask, values):
    picked = jnp.sum(jnp.where(mask, values, 0), axis=1, keepdims=True)
    return jnp.sum(picked, axis=0, keepdims=True)


def norm_rows(values, gain):
    average = jnp.mean(values, axis=1, keepdims=True)
    centred = values - average
    variance = jnp.mean(centred * centred, axis=1, keepdims=True)
    return (centred * lax.rsqrt(variance + epsilon) * gain).astype(BF16)


def prepare_kernel(mine, small_refs, pick_ref, states_from, table_from, out_refs, scratch, sems):
    normed_ref, picked_ref, rows_ref, qtable_ref, meta_ref = out_refs[:5]
    copies = [
        pltpu.make_async_copy(source, target, sems.at[i])
        for i, (source, target) in enumerate(zip((*small_refs, pick_ref), scratch))
    ]
    late = []
    if mine:
        states_ref = scratch[7]
        late = [
            pltpu.make_async_copy(states_from, states_ref, sems.at[7]),
            pltpu.make_async_copy(table_from, out_refs[5], sems.at[8]),
        ]
    else:
        states_ref = states_from
    for copy in (*copies, *late):
        copy.start()
    sequence_ref, length_ref, owner_ref, codes_ref, tokens_ref, gain_ref, pick_ref = scratch[:7]
    span, feature = normed_ref.shape
    masks = codes_ref.shape[0]
    core = lax.axis_index("core")
    core = core if mine else 1 - core
    copy_id = (
        (lax.axis_index("z") * 2 + core) * 4 + lax.axis_index("y")
    ) * 4 + lax.axis_index("x")
    copies[5].wait()
    block = 16

    def norm_all():
        gain = gain_ref[...].reshape(1, -1)

        def step(i, carry):
            at = pl.multiple_of(i * block, block)
            values = states_ref[pl.ds(at, block), :].astype(F32)
            normed_ref[pl.ds(at, block), :] = norm_rows(values, gain)
            return carry

        lax.fori_loop(0, span // block, step, 0, unroll=20)

    if not mine:
        norm_all()
    for copy in (*copies[:5], copies[6]):
        copy.wait()

    def numbers(count):
        return lax.broadcasted_iota(jnp.int32, (1, count), 1)

    own = numbers(codes_ref.shape[1]) == copy_id
    sequence = first(own, sequence_ref[...].reshape(1, -1))
    owner = first(own, owner_ref[...].reshape(1, -1))
    length = first(numbers(length_ref.shape[0]) == sequence, length_ref[...].reshape(1, -1))
    codes = jnp.sum(jnp.where(own, codes_ref[...], 0), axis=1, keepdims=True)
    quotient = jnp.floor(codes.astype(F32) / length.astype(F32)).astype(jnp.int32)
    positions = codes - quotient * length
    positions = jnp.where(positions < 0, positions + length, positions)
    positions = jnp.where(positions >= length, positions - length, positions)
    hit = lax.broadcasted_iota(jnp.int32, (masks, span), 1) == positions
    line = lax.broadcasted_iota(jnp.int32, tokens_ref.shape, 0)
    tokens = jnp.sum(jnp.where(line == sequence, tokens_ref[...], 0), axis=0, keepdims=True)
    targets = jnp.sum(jnp.where(hit, tokens, 0), axis=1, keepdims=True)
    lane = lax.broadcasted_iota(jnp.int32, meta_ref.shape, 1)
    meta_ref[...] = jnp.where(lane == 0, targets, jnp.where(lane == 1, length, owner))
    hot = hit.astype(F32).astype(BF16)
    picks = nn_dot(hot, pick_ref[...])
    wide = picks.shape[1] // 4
    picks = picks[:, :wide] + picks[:, wide : 2 * wide] + picks[:, 2 * wide : 3 * wide]
    cosine, sine = picks[:, : wide // 2], picks[:, wide // 2 :]
    qtable_ref[...] = jnp.concatenate([cosine] * 4 + [-sine, sine] * 2, axis=1)
    for copy in late:
        copy.wait()
    if mine:
        norm_all()
    rows = nn_dot(hot, states_ref[...])
    rows_ref[...] = rows
    picked_ref[...] = norm_rows(rows, gain_ref[...].reshape(1, -1))


def attend(table_ref, normed_refs, picked_refs, qtable_refs, meta_refs, key_refs, value_refs):
    size = key_refs[0].shape[0] // 2
    masks = picked_refs[0].shape[0]
    heads = len(key_refs)
    width = heads * size
    weight = jnp.concatenate(
        [r[size:, :] for r in key_refs] + [r[:size, :] for r in value_refs], axis=0
    )
    query_weight = jnp.concatenate([r[:size, :] for r in key_refs], axis=0)
    picked = jnp.concatenate([r[...] for r in picked_refs], axis=0)
    queries = nt_dot(picked, query_weight) * 0.125
    results = []
    for which in range(2):
        length = meta_refs[which][0:1, 1:2]
        projected = nt_dot(normed_refs[which][...], weight)
        own = queries[masks * which : masks * (which + 1), :]
        turned_keys, turned_queries = [], []
        for i in range(heads // 2):
            lanes = slice(128 * i, 128 * (i + 1))
            turned_keys.append(rotate(projected[:, lanes], table_ref[...], size // 2))
            turned_queries.append(rotate(own[:, lanes], qtable_refs[which][...], size // 2))
        key_rows = jnp.concatenate(turned_keys, axis=1).astype(BF16)
        query_rows = jnp.concatenate(turned_queries, axis=1).astype(BF16)
        spread = jnp.concatenate([query_rows] * heads, axis=0)
        row = lax.broadcasted_iota(jnp.int32, spread.shape, 0) // masks
        lane = lax.broadcasted_iota(jnp.int32, spread.shape, 1) // size
        spread = jnp.where(row == lane, spread, jnp.zeros_like(spread))
        logits = nt_dot(spread, key_rows)
        alive = lax.broadcasted_iota(jnp.int32, logits.shape, 1) < length
        logits = jnp.where(alive, logits, -1e30)
        largest = jnp.max(logits, axis=1, keepdims=True)
        weights = jnp.exp(logits - largest)
        total = jnp.sum(weights, axis=1, keepdims=True)
        probs = (weights * (1.0 / total)).astype(BF16)
        results.append((probs, projected[:, width:].astype(BF16)))
    return results


def attend_kernel(*refs):
    inputs, (probs_ref, values_ref) = refs[:-2], refs[-2:]
    for which, (probs, values) in enumerate(attend(*inputs)):
        probs_ref[which] = probs
        values_ref[which] = values


def mix_columns(columns, probs, values, masks, size):
    right = (lax.axis_index("x") + lax.axis_index("y")) % 2 == lax.axis_index("core")

    def rows_of(step, which):
        start = masks * (which + (2 if step == 3 else 0))
        return probs[(0, 1, 2, 1)[step]](start, start + masks)

    stack = []
    for column in columns:
        which = column // 2
        for i in range(2):
            even = rows_of((0, 2)[i], which)
            odd = rows_of((1, 3)[i], which)
            if column % 2:
                even, odd = odd, even
            stack.append(jnp.where(right, even, odd))
    mixed = nn_dot(jnp.concatenate(stack, axis=0), values)
    lane = lax.broadcasted_iota(jnp.int32, (masks, mixed.shape[1]), 1) // size
    context = mixed[:masks, :]
    for head in range(1, len(stack)):
        context = jnp.where(lane == head, mixed[masks * head : masks * (head + 1), :], context)
    return context.astype(BF16)


def rows_reader(ref, copy):
    return lambda start, end: ref[copy, start:end, :]


def probs_kernel(*refs):
    inputs, probs_ref = refs[:-1], refs[-1]
    for which, (probs, _) in enumerate(attend(*inputs)):
        probs_ref[which] = probs


def mix_kernel(
    probs_refs, values_refs, normed_refs, far_refs, block_refs, partial_ref, sent_ref
):
    size = block_refs[0].shape[0] // 2
    masks = probs_refs[0].shape[1] // 2
    value_weight = jnp.concatenate([r[:size, :] for r in far_refs], axis=0)
    contexts = []
    for copy in range(2):
        readers = [rows_reader(r, copy) for r in probs_refs]
        far = nt_dot(normed_refs[copy][...], value_weight).astype(BF16)
        values = (values_refs[0][copy], values_refs[1][copy], far)
        contexts.append(
            jnp.concatenate(
                [
                    mix_columns(columns, readers, value, masks, size)
                    for columns, value in zip(((0,), (1, 3), (2,)), values)
                ],
                axis=1,
            )
        )
    weight = jnp.concatenate([r[size:, :] for r in (*block_refs, *far_refs)], axis=0)
    partial = nn_dot(jnp.concatenate(contexts, axis=0), weight)
    partial_ref[...] = partial
    sent_ref[...] = partial.astype(BF16)


def join_kernel(low_ref, high_ref, line_ref):
    rows = low_ref.shape[0]
    line_ref[:rows, :] = low_ref[...]
    line_ref[rows:, :] = high_ref[...]


def join(low, high):
    line = jax.ShapeDtypeStruct((2 * low.shape[0], low.shape[1]), low.dtype)
    return call(join_kernel, line, (low, high))


def part(array, start, end):
    def kernel(array_ref, part_ref):
        part_ref[...] = array_ref[start:end, :]

    return call(kernel, jax.ShapeDtypeStruct((end - start, array.shape[1]), array.dtype), (array,))


def halves(ref):
    rows = ref.shape[0] // 2
    return ref.at[:rows], ref.at[rows:]


def score_kernel(
    rows_refs, partial_ref, arrived_ref, meta_refs, gain_ref, bias_ref, dense_ref, decoder_ref,
    placed_ref,
):
    masks = rows_refs[0].shape[0]
    arrived = arrived_ref[...].astype(F32)
    residual = jnp.concatenate(
        [
            rows_refs[0][...] + (partial_ref[:masks, :] + arrived[masks:, :]),
            rows_refs[1][...] + (partial_ref[masks:, :] + arrived[:masks, :]),
        ],
        axis=0,
    )
    targets = jnp.concatenate([r[:, 0:1] for r in meta_refs], axis=0)
    average = jnp.mean(residual, axis=1, keepdims=True)
    centred = residual - average
    variance = jnp.mean(centred * centred, axis=1, keepdims=True)
    normed = (centred * lax.rsqrt(variance + epsilon) * gain_ref[...]).astype(BF16)
    dense = nn_dot(normed, dense_ref[...])
    active = 0.5 * dense * (1.0 + lax.erf(dense * np.float32(0.5**0.5)))
    average = jnp.mean(active, axis=1, keepdims=True)
    centred = active - average
    variance = jnp.mean(centred * centred, axis=1, keepdims=True)
    headed = (centred * lax.rsqrt(variance + epsilon)).astype(BF16)
    logits = nt_dot(headed, decoder_ref[...]) + bias_ref[...]
    largest = jnp.max(logits, axis=1, keepdims=True)
    total = jnp.sum(jnp.exp(logits - largest), axis=1, keepdims=True)
    vocab = lax.broadcasted_iota(jnp.int32, logits.shape, 1)
    chosen = jnp.sum(jnp.where(vocab == targets, logits, 0.0), axis=1, keepdims=True)
    score = chosen - largest - jnp.log(total)
    devices, width = placed_ref.shape
    member = lax.broadcasted_iota(jnp.int32, (devices, masks), 0) % 16
    part = lax.broadcasted_iota(jnp.int32, (devices, masks), 1) // 4
    take = (member == part).astype(F32)
    fits = (
        lax.broadcasted_iota(jnp.int32, (masks, width), 0) % 4
        == lax.broadcasted_iota(jnp.int32, (masks, width), 1) % 4
    )
    layer = lax.broadcasted_iota(jnp.int32, (devices, width), 0) // 16
    slot = lax.broadcasted_iota(jnp.int32, (devices, width), 1) // 4
    wanted = 16 * (2 * layer + lax.axis_index("core")) + slot
    placed = jnp.zeros((devices, width), F32)
    for which in range(2):
        own = jnp.where(fits, score[masks * which : masks * (which + 1), :], 0.0)
        laid = nn_dot(take, own, precision=lax.Precision.HIGHEST)
        placed = jnp.where(wanted == meta_refs[which][0:1, 2:3], laid, placed)
    placed_ref[...] = placed


def collect_kernel(arrived_ref, scores_ref):
    own, rows = scores_ref.shape
    total = jnp.sum(arrived_ref[...], axis=0, keepdims=True)
    count = total.shape[1]
    row = lax.broadcasted_iota(jnp.int32, (count, count), 0)
    lane = lax.broadcasted_iota(jnp.int32, (count, count), 1)
    column = jnp.sum(jnp.where(row == lane, total, 0.0), axis=1, keepdims=True)
    row = lax.broadcasted_iota(jnp.int32, (count, rows), 0)
    slot = lax.broadcasted_iota(jnp.int32, (count, rows), 1)
    parts = [
        jnp.sum(jnp.where(row == slot * own + i, column, 0.0), axis=0, keepdims=True)
        for i in range(own)
    ]
    scores_ref[...] = jnp.concatenate(parts, axis=0)


def pull(array, axis, offset):
    size = lax.axis_size(axis)
    return lax.ppermute(array, axis, [((i + offset) % size, i) for i in range(size)])


def swap(array):
    return lax.ppermute(array, "core", [(0, 1), (1, 0)])


def after(array, *others):
    return lax.optimization_barrier((array, *others))[0]


def gather_line(block, axis, reach):
    near, far = [], []
    for core in range(2):
        for y in range(4):
            for x in range(4):
                def device(step):
                    to_y = (y + step) % 4 if axis == "y" else y
                    to_x = (x + step) % 4 if axis == "x" else x
                    return (((x + y) % 2) * 4 + to_y) * 4 + to_x

                source = (core * 4 + y) * 4 + x
                own = (x + y) % 2 == core
                near.append((source, device(-1 if own else 0)))
                far.append((source, device(1 if own else 2)))
    pairs = far if reach else near
    return lax.ppermute(block, ("core", "y", "x"), pairs)


def on_device(
    hidden_states,
    ln_attn_gain,
    w_qkv,
    output_weight,
    ln_final_gain,
    dense_weight,
    decoder_weight,
    decoder_bias,
    seq_tokens,
    seq_lengths,
    copy_sequence,
    mask_code,
    copy_owner,
):
    _, span, feature = hidden_states.shape
    size = output_weight.shape[0]
    masks = mask_code.shape[1]
    table, pick_table = (jnp.asarray(t) for t in rotary_tables(span, size))
    shape = jax.ShapeDtypeStruct

    def prepare_call(mine, states):
        small = [copy_sequence, seq_lengths, copy_owner, mask_code.T, seq_tokens, ln_attn_gain]
        outs = [
            shape((span, feature), BF16),
            shape((masks, feature), BF16),
            shape((masks, feature), F32),
            shape((masks, 256), F32),
            shape((masks, 128), jnp.int32),
        ]
        args = [*small, pick_table, table, states] if mine else [*small, pick_table, states]
        scratch = [pltpu.VMEM(a.shape, a.dtype) for a in (*small, pick_table)]
        if mine:
            outs.append(shape(table.shape, F32))
            scratch.append(pltpu.VMEM(states.shape, states.dtype))
        n, m = len(args), len(outs)

        def kernel(*refs):
            prepare_kernel(
                mine, refs[:6], refs[6], refs[n - 1], refs[7], refs[n : n + m], refs[n + m : -1],
                refs[-1],
            )

        return call(
            kernel,
            outs,
            args,
            n_any=9 if mine else 7,
            scratch=[*scratch, pltpu.SemaphoreType.DMA((9,))],
            flops=4 * masks * span * feature + 10 * span * feature,
        )

    def attend_args(ready, key_blocks, value_blocks):
        per_copy = [r[i] for i in (0, 1, 3, 4) for r in ready]
        return (ready[0][5], *per_copy, *key_blocks, *value_blocks)

    def attend_refs(refs, keys, values):
        return (refs[0], refs[1:3], refs[3:5], refs[5:7], refs[7:9], keys, values)

    def attend_call(ready, key_lines, value_lines):
        count = len(key_lines)

        def kernel(*refs):
            lines = [halves(r) for r in refs[9:-2]]
            keys = [h for line in lines[:count] for h in line]
            values = [h for line in lines[count:] for h in line]
            attend_kernel(*attend_refs(refs, keys, values), *refs[-2:])

        heads = 2 * count
        return call(
            kernel,
            [
                shape((2, heads * masks, span), BF16),
                shape((2, span, heads * size), BF16),
            ],
            attend_args(ready, key_lines, value_lines),
            flops=4 * span * feature * heads * 128,
            exps=2 * heads * masks * span,
        )

    states = hidden_states[0]
    key_block, value_block = pack(jnp.transpose(w_qkv[:, 0, :]), output_weight[:, 0, :])
    key_low = gather_line(key_block, "x", False)
    value_low = gather_line(value_block, "y", False)
    key_high = gather_line(key_block, "x", True)
    value_high = gather_line(value_block, "y", True)
    key_line = join(key_low, key_high)
    key_ahead = pull(key_line, "y", 1)
    key_behind = pull(key_line, "y", 3)
    value_line = join(value_low, value_high)
    value_ahead = pull(value_line, "x", 1)
    value_behind = pull(value_line, "x", 3)
    states_other = swap(after(states, key_line, value_line))
    mine = prepare_call(True, after(states, key_line, value_line))
    other = prepare_call(False, after(states_other, mine[0]))
    ready = (mine, other)
    own_probs, own_values = attend_call(ready, (key_line,), (value_line,))
    rows = key_line.shape[0]
    key_far = (
        pull(part(after(key_ahead, own_probs), 0, rows // 2), "y", 1),
        pull(part(after(key_behind, own_probs), rows // 2, rows), "y", 3),
    )
    value_far = (
        pull(part(after(value_ahead, own_probs), 0, rows // 2), "x", 1),
        pull(part(after(value_behind, own_probs), rows // 2, rows), "x", 3),
    )
    near_probs, near_values = attend_call(
        ready, (key_ahead, key_behind), (value_ahead, value_behind)
    )
    key_far = tuple(after(b, near_probs) for b in key_far)
    far_args = attend_args(ready, key_far, ())

    def far_kernel(*refs):
        probs_kernel(*attend_refs(refs, refs[9:11], ()), refs[-1])

    far_probs = call(
        far_kernel,
        shape((2, 2 * masks, span), BF16),
        far_args,
        flops=4 * span * feature * 256,
        exps=4 * masks * span,
    )
    value_far = tuple(after(b, far_probs) for b in value_far)

    def mix(*refs):
        blocks = [h for r in refs[9:12] for h in halves(r)]
        mix_kernel(refs[:3], refs[3:5], refs[5:7], refs[7:9], blocks, *refs[12:])

    partial, sent = call(
        mix,
        [shape((2 * masks, feature), F32), shape((2 * masks, feature), BF16)],
        (
            own_probs, near_probs, far_probs, own_values, near_values, mine[0], other[0],
            *value_far, value_line, value_ahead, value_behind,
        ),
        flops=4 * span * feature * 256 + 4 * masks * feature * 8 * size,
    )

    def score(*refs):
        score_kernel(refs[:2], *refs[2:4], refs[4:6], *refs[6:])

    placed = call(
        score,
        shape((128, 64), F32),
        (
            mine[2], other[2], partial, swap(sent), mine[4], other[4],
            ln_final_gain.reshape(1, -1), decoder_bias.reshape(1, -1), dense_weight,
            decoder_weight.T,
        ),
        flops=4 * masks * feature * feature,
    )
    arrived = lax.all_to_all(placed, ("z", "y", "x"), 0, 0, tiled=True)
    return call(collect_kernel, shape((4, 16), F32), (arrived,)).T


def solution(mesh):
    fine = Mesh(mesh.devices.reshape(8, 2, 4, 4), ("z", "core", "y", "x"))
    dp, mp = ("z", "core"), ("y", "x")
    placed = (
        P(("z", "core", "y", "x"), None, None),
        P(),
        P(None, mp, None),
        P(None, mp, None),
        P(),
        P(),
        P(),
        P(),
        P(),
        P(),
        P(),
        P(),
        P(),
    )
    return jax.shard_map(
        on_device, mesh=fine, in_specs=placed, out_specs=P(dp, mp), check_vma=False
    )
```

```python
import numpy as np
import jax
import jax.numpy as jnp
from jax import lax
from jax.experimental import pallas as pl
from jax.experimental.pallas import tpu as pltpu
from jax.sharding import Mesh, PartitionSpec as P

epsilon = 1e-05
F32 = jnp.float32
BF16 = jnp.bfloat16


def rotary_tables(seq_span, head_size):
    half = head_size // 2
    power = (np.arange(half, dtype=np.float32) * np.float32(2.0 / head_size)).astype(np.float32)
    frequency = (np.float32(1.0) / np.power(np.float32(10000.0), power)).astype(np.float32)
    angles = (np.arange(seq_span, dtype=np.float32)[:, None] * frequency[None, :]).astype(np.float32)
    cosine = np.cos(angles.astype(np.float64)).astype(np.float32)
    sine = np.sin(angles.astype(np.float64)).astype(np.float32)
    wide = np.concatenate([cosine] * 4 + [-sine, sine] * 2, axis=1)
    rest = np.concatenate([cosine, sine], axis=1)
    parts = []
    for _ in range(3):
        parts.append(rest.astype(BF16))
        rest = rest - parts[-1].astype(np.float32)
    parts.append(np.zeros_like(parts[0]))
    return wide, np.concatenate(parts, axis=1)


def nt_dot(a, b):
    return lax.dot_general(a, b, (((1,), (1,)), ((), ())), preferred_element_type=F32)


def nn_dot(a, b, **options):
    return lax.dot_general(a, b, (((1,), (0,)), ((), ())), preferred_element_type=F32, **options)


def rotate(part, table, half):
    cos_table, sin_table = table[:, :128], table[:, 128:]
    width = part.shape[1]
    lane = lax.broadcasted_iota(jnp.int32, part.shape, 1) % (2 * half)
    turned = jnp.where(
        lane < half,
        pltpu.roll(part, width - half, 1),
        pltpu.roll(part, half, 1),
    )
    return part * cos_table + turned * sin_table


IN_PLACE = pl.BlockSpec(memory_space=pltpu.MemorySpace.HBM)
ON_CHIP = pl.BlockSpec(memory_space=pltpu.MemorySpace.VMEM)


def call(kernel, outs, args, n_any=0, scratch=(), flops=0, exps=0, vmem=24 * 1024 * 1024):
    moved = sum(a.size * a.dtype.itemsize for a in list(args) + jax.tree.leaves(outs))
    place = pltpu.with_memory_space_constraint
    args = [place(a, pltpu.HBM) if i < n_any else a for i, a in enumerate(args)]
    return pl.pallas_call(
        kernel,
        out_shape=outs,
        in_specs=[IN_PLACE] * n_any + [ON_CHIP] * (len(args) - n_any),
        out_specs=jax.tree.map(lambda _: ON_CHIP, outs),
        scratch_shapes=list(scratch),
        cost_estimate=pl.CostEstimate(flops=flops, transcendentals=exps, bytes_accessed=moved),
        compiler_params=pltpu.CompilerParams(vmem_limit_bytes=vmem),
    )(*args)


def pack_kernel(turned_ref, out_ref, key_ref, value_ref, sems):
    size = out_ref.shape[0]
    copies = (
        pltpu.make_async_copy(turned_ref.at[: 2 * size], key_ref, sems.at[0]),
        pltpu.make_async_copy(turned_ref.at[2 * size :], value_ref.at[:size], sems.at[1]),
        pltpu.make_async_copy(out_ref, value_ref.at[size:], sems.at[2]),
    )
    for copy in copies:
        copy.start()
    for copy in copies:
        copy.wait()


def pack(turned, out_weight):
    size, feature = out_weight.shape
    return call(
        pack_kernel,
        [jax.ShapeDtypeStruct((2 * size, feature), BF16)] * 2,
        (turned, out_weight),
        n_any=2,
        scratch=[pltpu.SemaphoreType.DMA((3,))],
    )


def first(mask, values):
    picked = jnp.sum(jnp.where(mask, values, 0), axis=1, keepdims=True)
    return jnp.sum(picked, axis=0, keepdims=True)


def norm_rows(values, gain):
    average = jnp.mean(values, axis=1, keepdims=True)
    centred = values - average
    variance = jnp.mean(centred * centred, axis=1, keepdims=True)
    return (centred * lax.rsqrt(variance + epsilon) * gain).astype(BF16)


def prepare_kernel(mine, small_refs, pick_ref, states_from, table_from, out_refs, scratch, sems):
    normed_ref, picked_ref, rows_ref, qtable_ref, meta_ref = out_refs[:5]
    copies = [
        pltpu.make_async_copy(source, target, sems.at[i])
        for i, (source, target) in enumerate(zip((*small_refs, pick_ref), scratch))
    ]
    late = []
    if mine:
        states_ref = scratch[7]
        late = [
            pltpu.make_async_copy(states_from, states_ref, sems.at[7]),
            pltpu.make_async_copy(table_from, out_refs[5], sems.at[8]),
        ]
    else:
        states_ref = states_from
    for copy in (*copies, *late):
        copy.start()
    sequence_ref, length_ref, owner_ref, codes_ref, tokens_ref, gain_ref, pick_ref = scratch[:7]
    span, feature = normed_ref.shape
    masks = codes_ref.shape[0]
    core = lax.axis_index("core")
    core = core if mine else 1 - core
    copy_id = (
        (lax.axis_index("z") * 2 + core) * 4 + lax.axis_index("y")
    ) * 4 + lax.axis_index("x")
    copies[5].wait()
    block = 16

    def norm_all():
        gain = gain_ref[...].reshape(1, -1)

        def step(i, carry):
            at = pl.multiple_of(i * block, block)
            values = states_ref[pl.ds(at, block), :].astype(F32)
            normed_ref[pl.ds(at, block), :] = norm_rows(values, gain)
            return carry

        lax.fori_loop(0, span // block, step, 0, unroll=20)

    if not mine:
        norm_all()
    for copy in (*copies[:5], copies[6]):
        copy.wait()

    def numbers(count):
        return lax.broadcasted_iota(jnp.int32, (1, count), 1)

    own = numbers(codes_ref.shape[1]) == copy_id
    sequence = first(own, sequence_ref[...].reshape(1, -1))
    owner = first(own, owner_ref[...].reshape(1, -1))
    length = first(numbers(length_ref.shape[0]) == sequence, length_ref[...].reshape(1, -1))
    codes = jnp.sum(jnp.where(own, codes_ref[...], 0), axis=1, keepdims=True)
    quotient = jnp.floor(codes.astype(F32) / length.astype(F32)).astype(jnp.int32)
    positions = codes - quotient * length
    positions = jnp.where(positions < 0, positions + length, positions)
    positions = jnp.where(positions >= length, positions - length, positions)
    hit = lax.broadcasted_iota(jnp.int32, (masks, span), 1) == positions
    line = lax.broadcasted_iota(jnp.int32, tokens_ref.shape, 0)
    tokens = jnp.sum(jnp.where(line == sequence, tokens_ref[...], 0), axis=0, keepdims=True)
    targets = jnp.sum(jnp.where(hit, tokens, 0), axis=1, keepdims=True)
    lane = lax.broadcasted_iota(jnp.int32, meta_ref.shape, 1)
    meta_ref[...] = jnp.where(lane == 0, targets, jnp.where(lane == 1, length, owner))
    hot = hit.astype(F32).astype(BF16)
    picks = nn_dot(hot, pick_ref[...])
    wide = picks.shape[1] // 4
    picks = picks[:, :wide] + picks[:, wide : 2 * wide] + picks[:, 2 * wide : 3 * wide]
    cosine, sine = picks[:, : wide // 2], picks[:, wide // 2 :]
    qtable_ref[...] = jnp.concatenate([cosine] * 4 + [-sine, sine] * 2, axis=1)
    for copy in late:
        copy.wait()
    if mine:
        norm_all()
    rows = nn_dot(hot, states_ref[...])
    rows_ref[...] = rows
    picked_ref[...] = norm_rows(rows, gain_ref[...].reshape(1, -1))


def attend(
    table_ref, normed_refs, picked_refs, qtable_refs, meta_refs, key_refs, value_refs, kept=None
):
    size = key_refs[0].shape[0] // 2
    masks = picked_refs[0].shape[0]
    heads = len(key_refs)
    width = heads * size
    weight = jnp.concatenate(
        [r[size:, :] for r in key_refs] + [r[:size, :] for r in value_refs], axis=0
    )
    query_weight = jnp.concatenate([r[:size, :] for r in key_refs], axis=0)
    picked = jnp.concatenate([r[...] for r in picked_refs], axis=0)
    queries = nt_dot(picked, query_weight) * 0.125
    results = []
    for which in range(2):
        length = meta_refs[which][0:1, 1:2]
        projected = nt_dot(normed_refs[which][...], weight)
        own = queries[masks * which : masks * (which + 1), :]
        turned_keys, turned_queries = [], []
        for i in range(heads // 2):
            lanes = slice(128 * i, 128 * (i + 1))
            turned_keys.append(rotate(projected[:, lanes], table_ref[...], size // 2))
            turned_queries.append(rotate(own[:, lanes], qtable_refs[which][...], size // 2))
        key_rows = jnp.concatenate(turned_keys, axis=1).astype(BF16)
        query_rows = jnp.concatenate(turned_queries, axis=1).astype(BF16)
        spread = jnp.concatenate([query_rows] * (kept or heads), axis=0)
        row = lax.broadcasted_iota(jnp.int32, spread.shape, 0) // masks
        lane = lax.broadcasted_iota(jnp.int32, spread.shape, 1) // size
        spread = jnp.where(row == lane, spread, jnp.zeros_like(spread))
        logits = nt_dot(spread, key_rows)
        alive = lax.broadcasted_iota(jnp.int32, logits.shape, 1) < length
        logits = jnp.where(alive, logits, -1e30)
        largest = jnp.max(logits, axis=1, keepdims=True)
        weights = jnp.exp(logits - largest)
        total = jnp.sum(weights, axis=1, keepdims=True)
        probs = (weights * (1.0 / total)).astype(BF16)
        results.append((probs, projected[:, width:].astype(BF16)))
    return results


def attend_kernel(*refs):
    inputs, (probs_ref, values_ref) = refs[:-2], refs[-2:]
    for which, (probs, values) in enumerate(attend(*inputs)):
        probs_ref[which] = probs
        values_ref[which] = values


def mix_columns(columns, probs, values, masks, size):
    right = (lax.axis_index("x") + lax.axis_index("y")) % 2 == lax.axis_index("core")

    def rows_of(step, which):
        start = masks * (which + (2 if step == 3 else 0))
        return probs[(0, 1, 2, 1)[step]](start, start + masks)

    stack = []
    for column in columns:
        which = column // 2
        for i in range(2):
            even = rows_of((0, 2)[i], which)
            odd = rows_of((1, 3)[i], which)
            if column % 2:
                even, odd = odd, even
            stack.append(jnp.where(right, even, odd))
    mixed = nn_dot(jnp.concatenate(stack, axis=0), values)
    lane = lax.broadcasted_iota(jnp.int32, (masks, mixed.shape[1]), 1) // size
    context = mixed[:masks, :]
    for head in range(1, len(stack)):
        context = jnp.where(lane == head, mixed[masks * head : masks * (head + 1), :], context)
    return context.astype(BF16)


def rows_reader(ref, copy):
    return lambda start, end: ref[copy, start:end, :]


def probs_kernel(*refs):
    inputs, block_ref, probs_ref = refs[:-2], refs[-2], refs[-1]
    for which, (probs, _) in enumerate(attend(*inputs, (block_ref, block_ref), (), kept=1)):
        probs_ref[which] = probs


def mix_kernel(
    probs_refs, values_refs, normed_refs, far_refs, block_refs, partial_ref, sent_ref
):
    size = block_refs[0].shape[0] // 2
    masks = probs_refs[0].shape[1] // 2
    value_weight = jnp.concatenate([r[:size, :] for r in far_refs], axis=0)
    contexts = []
    for copy in range(2):
        readers = [rows_reader(r, copy) for r in probs_refs[:2]]
        ends = [r[copy] for r in probs_refs[2:]]
        readers.append(lambda start, end, ends=ends: ends[start // masks])
        far = nt_dot(normed_refs[copy][...], value_weight).astype(BF16)
        values = (values_refs[0][copy], values_refs[1][copy], far)
        contexts.append(
            jnp.concatenate(
                [
                    mix_columns(columns, readers, value, masks, size)
                    for columns, value in zip(((0,), (1, 3), (2,)), values)
                ],
                axis=1,
            )
        )
    weight = jnp.concatenate([r[size:, :] for r in (*block_refs, *far_refs)], axis=0)
    partial = nn_dot(jnp.concatenate(contexts, axis=0), weight)
    partial_ref[...] = partial
    sent_ref[...] = partial.astype(BF16)


def join_kernel(low_ref, high_ref, line_ref):
    rows = low_ref.shape[0]
    line_ref[:rows, :] = low_ref[...]
    line_ref[rows:, :] = high_ref[...]


def join(low, high):
    line = jax.ShapeDtypeStruct((2 * low.shape[0], low.shape[1]), low.dtype)
    return call(join_kernel, line, (low, high))


def part(array, start, end):
    def kernel(array_ref, part_ref):
        part_ref[...] = array_ref[start:end, :]

    return call(kernel, jax.ShapeDtypeStruct((end - start, array.shape[1]), array.dtype), (array,))


def halves(ref):
    rows = ref.shape[0] // 2
    return ref.at[:rows], ref.at[rows:]


def score_kernel(
    rows_refs, partial_ref, arrived_ref, meta_refs, gain_ref, bias_ref, dense_ref, decoder_ref,
    placed_ref,
):
    masks = rows_refs[0].shape[0]
    arrived = arrived_ref[...].astype(F32)
    residual = jnp.concatenate(
        [
            rows_refs[0][...] + (partial_ref[:masks, :] + arrived[masks:, :]),
            rows_refs[1][...] + (partial_ref[masks:, :] + arrived[:masks, :]),
        ],
        axis=0,
    )
    targets = jnp.concatenate([r[:, 0:1] for r in meta_refs], axis=0)
    average = jnp.mean(residual, axis=1, keepdims=True)
    centred = residual - average
    variance = jnp.mean(centred * centred, axis=1, keepdims=True)
    normed = (centred * lax.rsqrt(variance + epsilon) * gain_ref[...]).astype(BF16)
    dense = nn_dot(normed, dense_ref[...])
    active = 0.5 * dense * (1.0 + lax.erf(dense * np.float32(0.5**0.5)))
    average = jnp.mean(active, axis=1, keepdims=True)
    centred = active - average
    variance = jnp.mean(centred * centred, axis=1, keepdims=True)
    headed = (centred * lax.rsqrt(variance + epsilon)).astype(BF16)
    logits = nt_dot(headed, decoder_ref[...]) + bias_ref[...]
    largest = jnp.max(logits, axis=1, keepdims=True)
    total = jnp.sum(jnp.exp(logits - largest), axis=1, keepdims=True)
    vocab = lax.broadcasted_iota(jnp.int32, logits.shape, 1)
    chosen = jnp.sum(jnp.where(vocab == targets, logits, 0.0), axis=1, keepdims=True)
    score = chosen - largest - jnp.log(total)
    devices, width = placed_ref.shape
    member = lax.broadcasted_iota(jnp.int32, (devices, masks), 0) % 16
    part = lax.broadcasted_iota(jnp.int32, (devices, masks), 1) // 4
    take = (member == part).astype(F32)
    fits = (
        lax.broadcasted_iota(jnp.int32, (masks, width), 0) % 4
        == lax.broadcasted_iota(jnp.int32, (masks, width), 1) % 4
    )
    layer = lax.broadcasted_iota(jnp.int32, (devices, width), 0) // 16
    slot = lax.broadcasted_iota(jnp.int32, (devices, width), 1) // 4
    wanted = 16 * (2 * layer + lax.axis_index("core")) + slot
    placed = jnp.zeros((devices, width), F32)
    for which in range(2):
        own = jnp.where(fits, score[masks * which : masks * (which + 1), :], 0.0)
        laid = nn_dot(take, own, precision=lax.Precision.HIGHEST)
        placed = jnp.where(wanted == meta_refs[which][0:1, 2:3], laid, placed)
    placed_ref[...] = placed


def collect_kernel(arrived_ref, scores_ref):
    own, rows = scores_ref.shape
    total = jnp.sum(arrived_ref[...], axis=0, keepdims=True)
    count = total.shape[1]
    row = lax.broadcasted_iota(jnp.int32, (count, count), 0)
    lane = lax.broadcasted_iota(jnp.int32, (count, count), 1)
    column = jnp.sum(jnp.where(row == lane, total, 0.0), axis=1, keepdims=True)
    row = lax.broadcasted_iota(jnp.int32, (count, rows), 0)
    slot = lax.broadcasted_iota(jnp.int32, (count, rows), 1)
    parts = [
        jnp.sum(jnp.where(row == slot * own + i, column, 0.0), axis=0, keepdims=True)
        for i in range(own)
    ]
    scores_ref[...] = jnp.concatenate(parts, axis=0)


def pull(array, axis, offset):
    size = lax.axis_size(axis)
    return lax.ppermute(array, axis, [((i + offset) % size, i) for i in range(size)])


def swap(array):
    return lax.ppermute(array, "core", [(0, 1), (1, 0)])


def after(array, *others):
    return lax.optimization_barrier((array, *others))[0]


def gather_line(block, axis, reach):
    near, far = [], []
    for core in range(2):
        for y in range(4):
            for x in range(4):
                def device(step):
                    to_y = (y + step) % 4 if axis == "y" else y
                    to_x = (x + step) % 4 if axis == "x" else x
                    return (((x + y) % 2) * 4 + to_y) * 4 + to_x

                source = (core * 4 + y) * 4 + x
                own = (x + y) % 2 == core
                near.append((source, device(-1 if own else 0)))
                far.append((source, device(1 if own else 2)))
    pairs = far if reach else near
    return lax.ppermute(block, ("core", "y", "x"), pairs)


def on_device(
    hidden_states,
    ln_attn_gain,
    w_qkv,
    output_weight,
    ln_final_gain,
    dense_weight,
    decoder_weight,
    decoder_bias,
    seq_tokens,
    seq_lengths,
    copy_sequence,
    mask_code,
    copy_owner,
):
    _, span, feature = hidden_states.shape
    size = output_weight.shape[0]
    masks = mask_code.shape[1]
    table, pick_table = (jnp.asarray(t) for t in rotary_tables(span, size))
    shape = jax.ShapeDtypeStruct

    def prepare_call(mine, states):
        small = [copy_sequence, seq_lengths, copy_owner, mask_code.T, seq_tokens, ln_attn_gain]
        outs = [
            shape((span, feature), BF16),
            shape((masks, feature), BF16),
            shape((masks, feature), F32),
            shape((masks, 256), F32),
            shape((masks, 128), jnp.int32),
        ]
        args = [*small, pick_table, table, states] if mine else [*small, pick_table, states]
        scratch = [pltpu.VMEM(a.shape, a.dtype) for a in (*small, pick_table)]
        if mine:
            outs.append(shape(table.shape, F32))
            scratch.append(pltpu.VMEM(states.shape, states.dtype))
        n, m = len(args), len(outs)

        def kernel(*refs):
            prepare_kernel(
                mine, refs[:6], refs[6], refs[n - 1], refs[7], refs[n : n + m], refs[n + m : -1],
                refs[-1],
            )

        return call(
            kernel,
            outs,
            args,
            n_any=9 if mine else 7,
            scratch=[*scratch, pltpu.SemaphoreType.DMA((9,))],
            flops=4 * masks * span * feature + 10 * span * feature,
        )

    def attend_args(ready, key_blocks, value_blocks):
        per_copy = [r[i] for i in (0, 1, 3, 4) for r in ready]
        return (ready[0][5], *per_copy, *key_blocks, *value_blocks)

    def attend_refs(refs, keys, values):
        return (refs[0], refs[1:3], refs[3:5], refs[5:7], refs[7:9], keys, values)

    def attend_call(ready, key_lines, value_lines):
        count = len(key_lines)

        def kernel(*refs):
            lines = [halves(r) for r in refs[9:-2]]
            keys = [h for line in lines[:count] for h in line]
            values = [h for line in lines[count:] for h in line]
            attend_kernel(*attend_refs(refs, keys, values), *refs[-2:])

        heads = 2 * count
        return call(
            kernel,
            [
                shape((2, heads * masks, span), BF16),
                shape((2, span, heads * size), BF16),
            ],
            attend_args(ready, key_lines, value_lines),
            flops=4 * span * feature * heads * 128,
            exps=2 * heads * masks * span,
        )

    states = hidden_states[0]
    key_block, value_block = pack(jnp.transpose(w_qkv[:, 0, :]), output_weight[:, 0, :])
    key_low = gather_line(key_block, "x", False)
    value_low = gather_line(value_block, "y", False)
    key_high = gather_line(key_block, "x", True)
    value_high = gather_line(value_block, "y", True)
    states_other = swap(states)
    key_line = join(key_low, key_high)
    key_ahead = pull(key_line, "y", 1)
    key_behind = pull(key_line, "y", 3)
    value_line = join(value_low, value_high)
    value_ahead = pull(value_line, "x", 1)
    value_behind = pull(value_line, "x", 3)
    mine = prepare_call(True, after(states, key_line, value_line))
    other = prepare_call(False, after(states_other, mine[0]))
    ready = (mine, other)
    own_probs, own_values = attend_call(ready, (key_line,), (value_line,))
    rows = key_line.shape[0]
    key_far = (
        pull(part(after(key_ahead, own_probs), 0, rows // 2), "y", 1),
        pull(part(after(key_behind, own_probs), rows // 2, rows), "y", 3),
    )
    value_far = (
        pull(part(after(value_ahead, own_probs), 0, rows // 2), "x", 1),
        pull(part(after(value_behind, own_probs), rows // 2, rows), "x", 3),
    )
    near_probs, near_values = attend_call(
        ready, (key_ahead, key_behind), (value_ahead, value_behind)
    )
    key_far = tuple(after(b, near_probs) for b in key_far)

    def far_call(block):
        def kernel(*refs):
            probs_kernel(*attend_refs(refs, (), ())[:5], *refs[9:])

        return call(
            kernel,
            shape((2, masks, span), BF16),
            attend_args(ready, (block,), ()),
            flops=4 * span * feature * 256,
            exps=2 * masks * span,
        )

    low_probs = far_call(key_far[0])
    far_probs = far_call(after(key_far[1], low_probs))
    value_far = tuple(after(b, far_probs) for b in value_far)

    def mix(*refs):
        blocks = [h for r in refs[10:13] for h in halves(r)]
        mix_kernel(refs[:4], refs[4:6], refs[6:8], refs[8:10], blocks, *refs[13:])

    partial, sent = call(
        mix,
        [shape((2 * masks, feature), F32), shape((2 * masks, feature), BF16)],
        (
            own_probs, near_probs, low_probs, far_probs, own_values, near_values, mine[0], other[0],
            *value_far, value_line, value_ahead, value_behind,
        ),
        flops=4 * span * feature * 256 + 4 * masks * feature * 8 * size,
    )

    def score(*refs):
        score_kernel(refs[:2], *refs[2:4], refs[4:6], *refs[6:])

    placed = call(
        score,
        shape((128, 64), F32),
        (
            mine[2], other[2], partial, swap(sent), mine[4], other[4],
            ln_final_gain.reshape(1, -1), decoder_bias.reshape(1, -1), dense_weight,
            decoder_weight.T,
        ),
        flops=4 * masks * feature * feature,
    )
    arrived = lax.all_to_all(placed, ("z", "y", "x"), 0, 0, tiled=True)
    return call(collect_kernel, shape((4, 16), F32), (arrived,)).T


def solution(mesh):
    fine = Mesh(mesh.devices.reshape(8, 2, 4, 4), ("z", "core", "y", "x"))
    dp, mp = ("z", "core"), ("y", "x")
    placed = (
        P(("z", "core", "y", "x"), None, None),
        P(),
        P(None, mp, None),
        P(None, mp, None),
        P(),
        P(),
        P(),
        P(),
        P(),
        P(),
        P(),
        P(),
        P(),
    )
    return jax.shard_map(
        on_device, mesh=fine, in_specs=placed, out_specs=P(dp, mp), check_vma=False
    )
```

```python
import numpy as np
import jax
import jax.numpy as jnp
from jax import lax
from jax.experimental import pallas as pl
from jax.experimental.pallas import tpu as pltpu
from jax.sharding import Mesh, PartitionSpec as P

epsilon = 1e-05
F32 = jnp.float32
BF16 = jnp.bfloat16


def rotary_tables(seq_span, head_size):
    half = head_size // 2
    power = (np.arange(half, dtype=np.float32) * np.float32(2.0 / head_size)).astype(np.float32)
    frequency = (np.float32(1.0) / np.power(np.float32(10000.0), power)).astype(np.float32)
    angles = (np.arange(seq_span, dtype=np.float32)[:, None] * frequency[None, :]).astype(np.float32)
    cosine = np.cos(angles.astype(np.float64)).astype(np.float32)
    sine = np.sin(angles.astype(np.float64)).astype(np.float32)
    wide = np.concatenate([cosine] * 4 + [-sine, sine] * 2, axis=1)
    rest = np.concatenate([cosine, sine], axis=1)
    parts = []
    for _ in range(3):
        parts.append(rest.astype(BF16))
        rest = rest - parts[-1].astype(np.float32)
    parts.append(np.zeros_like(parts[0]))
    return wide, np.concatenate(parts, axis=1)


def nt_dot(a, b):
    return lax.dot_general(a, b, (((1,), (1,)), ((), ())), preferred_element_type=F32)


def nn_dot(a, b, **options):
    return lax.dot_general(a, b, (((1,), (0,)), ((), ())), preferred_element_type=F32, **options)


def rotate(part, table, half):
    cos_table, sin_table = table[:, :128], table[:, 128:]
    width = part.shape[1]
    lane = lax.broadcasted_iota(jnp.int32, part.shape, 1) % (2 * half)
    turned = jnp.where(
        lane < half,
        pltpu.roll(part, width - half, 1),
        pltpu.roll(part, half, 1),
    )
    return part * cos_table + turned * sin_table


IN_PLACE = pl.BlockSpec(memory_space=pltpu.MemorySpace.HBM)
ON_CHIP = pl.BlockSpec(memory_space=pltpu.MemorySpace.VMEM)


def call(kernel, outs, args, n_any=0, scratch=(), flops=0, exps=0, vmem=24 * 1024 * 1024):
    moved = sum(a.size * a.dtype.itemsize for a in list(args) + jax.tree.leaves(outs))
    place = pltpu.with_memory_space_constraint
    args = [place(a, pltpu.HBM) if i < n_any else a for i, a in enumerate(args)]
    return pl.pallas_call(
        kernel,
        out_shape=outs,
        in_specs=[IN_PLACE] * n_any + [ON_CHIP] * (len(args) - n_any),
        out_specs=jax.tree.map(lambda _: ON_CHIP, outs),
        scratch_shapes=list(scratch),
        cost_estimate=pl.CostEstimate(flops=flops, transcendentals=exps, bytes_accessed=moved),
        compiler_params=pltpu.CompilerParams(vmem_limit_bytes=vmem),
    )(*args)


def pack_kernel(turned_ref, out_ref, key_ref, value_ref, sems):
    size = out_ref.shape[0]
    copies = (
        pltpu.make_async_copy(turned_ref.at[: 2 * size], key_ref, sems.at[0]),
        pltpu.make_async_copy(turned_ref.at[2 * size :], value_ref.at[:size], sems.at[1]),
        pltpu.make_async_copy(out_ref, value_ref.at[size:], sems.at[2]),
    )
    for copy in copies:
        copy.start()
    for copy in copies:
        copy.wait()


def pack(turned, out_weight):
    size, feature = out_weight.shape
    return call(
        pack_kernel,
        [jax.ShapeDtypeStruct((2 * size, feature), BF16)] * 2,
        (turned, out_weight),
        n_any=2,
        scratch=[pltpu.SemaphoreType.DMA((3,))],
    )


def first(mask, values):
    picked = jnp.sum(jnp.where(mask, values, 0), axis=1, keepdims=True)
    return jnp.sum(picked, axis=0, keepdims=True)


def norm_rows(values, gain):
    average = jnp.mean(values, axis=1, keepdims=True)
    centred = values - average
    variance = jnp.mean(centred * centred, axis=1, keepdims=True)
    return (centred * lax.rsqrt(variance + epsilon) * gain).astype(BF16)


def prepare_kernel(mine, small_refs, pick_ref, states_from, table_from, out_refs, scratch, sems):
    normed_ref, picked_ref, rows_ref, qtable_ref, meta_ref = out_refs[:5]
    copies = [
        pltpu.make_async_copy(source, target, sems.at[i])
        for i, (source, target) in enumerate(zip((*small_refs, pick_ref), scratch))
    ]
    late = []
    if mine:
        states_ref = scratch[7]
        late = [
            pltpu.make_async_copy(states_from, states_ref, sems.at[7]),
            pltpu.make_async_copy(table_from, out_refs[5], sems.at[8]),
        ]
    else:
        states_ref = states_from
    for copy in (*copies, *late):
        copy.start()
    sequence_ref, length_ref, owner_ref, codes_ref, tokens_ref, gain_ref, pick_ref = scratch[:7]
    span, feature = normed_ref.shape
    masks = codes_ref.shape[0]
    core = lax.axis_index("core")
    core = core if mine else 1 - core
    copy_id = (
        (lax.axis_index("z") * 2 + core) * 4 + lax.axis_index("y")
    ) * 4 + lax.axis_index("x")
    copies[5].wait()
    block = 16

    def norm_all():
        gain = gain_ref[...].reshape(1, -1)

        def step(i, carry):
            at = pl.multiple_of(i * block, block)
            values = states_ref[pl.ds(at, block), :].astype(F32)
            normed_ref[pl.ds(at, block), :] = norm_rows(values, gain)
            return carry

        lax.fori_loop(0, span // block, step, 0, unroll=20)

    if not mine:
        norm_all()
    for copy in (*copies[:5], copies[6]):
        copy.wait()

    def numbers(count):
        return lax.broadcasted_iota(jnp.int32, (1, count), 1)

    own = numbers(codes_ref.shape[1]) == copy_id
    sequence = first(own, sequence_ref[...].reshape(1, -1))
    owner = first(own, owner_ref[...].reshape(1, -1))
    length = first(numbers(length_ref.shape[0]) == sequence, length_ref[...].reshape(1, -1))
    codes = jnp.sum(jnp.where(own, codes_ref[...], 0), axis=1, keepdims=True)
    quotient = jnp.floor(codes.astype(F32) / length.astype(F32)).astype(jnp.int32)
    positions = codes - quotient * length
    positions = jnp.where(positions < 0, positions + length, positions)
    positions = jnp.where(positions >= length, positions - length, positions)
    hit = lax.broadcasted_iota(jnp.int32, (masks, span), 1) == positions
    line = lax.broadcasted_iota(jnp.int32, tokens_ref.shape, 0)
    tokens = jnp.sum(jnp.where(line == sequence, tokens_ref[...], 0), axis=0, keepdims=True)
    targets = jnp.sum(jnp.where(hit, tokens, 0), axis=1, keepdims=True)
    lane = lax.broadcasted_iota(jnp.int32, meta_ref.shape, 1)
    meta_ref[...] = jnp.where(lane == 0, targets, jnp.where(lane == 1, length, owner))
    hot = hit.astype(F32).astype(BF16)
    picks = nn_dot(hot, pick_ref[...])
    wide = picks.shape[1] // 4
    picks = picks[:, :wide] + picks[:, wide : 2 * wide] + picks[:, 2 * wide : 3 * wide]
    cosine, sine = picks[:, : wide // 2], picks[:, wide // 2 :]
    qtable_ref[...] = jnp.concatenate([cosine] * 4 + [-sine, sine] * 2, axis=1)
    for copy in late:
        copy.wait()
    if mine:
        norm_all()
    rows = nn_dot(hot, states_ref[...])
    rows_ref[...] = rows
    picked_ref[...] = norm_rows(rows, gain_ref[...].reshape(1, -1))


def attend(table_ref, normed_refs, picked_refs, qtable_refs, meta_refs, key_refs, value_refs):
    size = key_refs[0].shape[0] // 2
    masks = picked_refs[0].shape[0]
    heads = len(key_refs)
    width = heads * size
    half = size // 2
    if value_refs:
        beside = [r[:size, :] for r in value_refs]
    else:
        beside = [r[start : start + half, :] for r in key_refs for start in (size + half, size)]
    weight = jnp.concatenate([r[size:, :] for r in key_refs] + beside, axis=0)
    query_weight = jnp.concatenate([r[:size, :] for r in key_refs], axis=0)
    picked = jnp.concatenate([r[...] for r in picked_refs], axis=0)
    queries = nt_dot(picked, query_weight) * 0.125
    results = []
    for which in range(2):
        length = meta_refs[which][0:1, 1:2]
        projected = nt_dot(normed_refs[which][...], weight)
        own = queries[masks * which : masks * (which + 1), :]
        turned_keys, turned_queries = [], []
        for i in range(heads // 2):
            lanes = slice(128 * i, 128 * (i + 1))
            if value_refs:
                turned_keys.append(rotate(projected[:, lanes], table_ref[...], half))
            else:
                exchanged = projected[:, width + 128 * i : width + 128 * (i + 1)]
                table = table_ref[...]
                turned_keys.append(
                    projected[:, lanes] * table[:, :128] + exchanged * table[:, 128:]
                )
            turned_queries.append(rotate(own[:, lanes], qtable_refs[which][...], size // 2))
        key_rows = jnp.concatenate(turned_keys, axis=1).astype(BF16)
        query_rows = jnp.concatenate(turned_queries, axis=1).astype(BF16)
        spread = jnp.concatenate([query_rows] * heads, axis=0)
        row = lax.broadcasted_iota(jnp.int32, spread.shape, 0) // masks
        lane = lax.broadcasted_iota(jnp.int32, spread.shape, 1) // size
        spread = jnp.where(row == lane, spread, jnp.zeros_like(spread))
        logits = nt_dot(spread, key_rows)
        alive = lax.broadcasted_iota(jnp.int32, logits.shape, 1) < length
        logits = jnp.where(alive, logits, -1e30)
        largest = jnp.max(logits, axis=1, keepdims=True)
        weights = jnp.exp(logits - largest)
        total = jnp.sum(weights, axis=1, keepdims=True)
        probs = (weights * (1.0 / total)).astype(BF16)
        results.append((probs, projected[:, width:].astype(BF16)))
    return results


def attend_kernel(*refs):
    inputs, (probs_ref, values_ref) = refs[:-2], refs[-2:]
    for which, (probs, values) in enumerate(attend(*inputs)):
        probs_ref[which] = probs
        values_ref[which] = values


def mix_columns(columns, probs, values, masks, size):
    right = (lax.axis_index("x") + lax.axis_index("y")) % 2 == lax.axis_index("core")

    def rows_of(step, which):
        start = masks * (which + (2 if step == 3 else 0))
        return probs[(0, 1, 2, 1)[step]](start, start + masks)

    stack = []
    for column in columns:
        which = column // 2
        for i in range(2):
            even = rows_of((0, 2)[i], which)
            odd = rows_of((1, 3)[i], which)
            if column % 2:
                even, odd = odd, even
            stack.append(jnp.where(right, even, odd))
    mixed = nn_dot(jnp.concatenate(stack, axis=0), values)
    lane = lax.broadcasted_iota(jnp.int32, (masks, mixed.shape[1]), 1) // size
    context = mixed[:masks, :]
    for head in range(1, len(stack)):
        context = jnp.where(lane == head, mixed[masks * head : masks * (head + 1), :], context)
    return context.astype(BF16)


def rows_reader(ref, copy):
    return lambda start, end: ref[copy, start:end, :]


def probs_kernel(*refs):
    inputs, probs_ref = refs[:-1], refs[-1]
    for which, (probs, _) in enumerate(attend(*inputs)):
        probs_ref[which] = probs


def mix_kernel(
    probs_refs, values_refs, normed_refs, far_refs, block_refs, partial_ref, sent_ref
):
    size = block_refs[0].shape[0] // 2
    masks = probs_refs[0].shape[1] // 2
    value_weight = jnp.concatenate([r[:size, :] for r in far_refs], axis=0)
    contexts = []
    for copy in range(2):
        readers = [rows_reader(r, copy) for r in probs_refs]
        far = nt_dot(normed_refs[copy][...], value_weight).astype(BF16)
        values = (values_refs[0][copy], values_refs[1][copy], far)
        contexts.append(
            jnp.concatenate(
                [
                    mix_columns(columns, readers, value, masks, size)
                    for columns, value in zip(((0,), (1, 3), (2,)), values)
                ],
                axis=1,
            )
        )
    weight = jnp.concatenate([r[size:, :] for r in (*block_refs, *far_refs)], axis=0)
    partial = nn_dot(jnp.concatenate(contexts, axis=0), weight)
    partial_ref[...] = partial
    sent_ref[...] = partial.astype(BF16)


def join_kernel(low_ref, high_ref, line_ref):
    rows = low_ref.shape[0]
    line_ref[:rows, :] = low_ref[...]
    line_ref[rows:, :] = high_ref[...]


def join(low, high):
    line = jax.ShapeDtypeStruct((2 * low.shape[0], low.shape[1]), low.dtype)
    return call(join_kernel, line, (low, high))


def part(array, start, end):
    def kernel(array_ref, part_ref):
        part_ref[...] = array_ref[start:end, :]

    return call(kernel, jax.ShapeDtypeStruct((end - start, array.shape[1]), array.dtype), (array,))


def halves(ref):
    rows = ref.shape[0] // 2
    return ref.at[:rows], ref.at[rows:]


def score_kernel(
    rows_refs, partial_ref, arrived_ref, meta_refs, gain_ref, bias_ref, dense_ref, decoder_ref,
    placed_ref,
):
    masks = rows_refs[0].shape[0]
    arrived = arrived_ref[...].astype(F32)
    residual = jnp.concatenate(
        [
            rows_refs[0][...] + (partial_ref[:masks, :] + arrived[masks:, :]),
            rows_refs[1][...] + (partial_ref[masks:, :] + arrived[:masks, :]),
        ],
        axis=0,
    )
    targets = jnp.concatenate([r[:, 0:1] for r in meta_refs], axis=0)
    average = jnp.mean(residual, axis=1, keepdims=True)
    centred = residual - average
    variance = jnp.mean(centred * centred, axis=1, keepdims=True)
    normed = (centred * lax.rsqrt(variance + epsilon) * gain_ref[...]).astype(BF16)
    dense = nn_dot(normed, dense_ref[...])
    active = 0.5 * dense * (1.0 + lax.erf(dense * np.float32(0.5**0.5)))
    average = jnp.mean(active, axis=1, keepdims=True)
    centred = active - average
    variance = jnp.mean(centred * centred, axis=1, keepdims=True)
    headed = (centred * lax.rsqrt(variance + epsilon)).astype(BF16)
    logits = nt_dot(headed, decoder_ref[...]) + bias_ref[...]
    largest = jnp.max(logits, axis=1, keepdims=True)
    total = jnp.sum(jnp.exp(logits - largest), axis=1, keepdims=True)
    vocab = lax.broadcasted_iota(jnp.int32, logits.shape, 1)
    chosen = jnp.sum(jnp.where(vocab == targets, logits, 0.0), axis=1, keepdims=True)
    score = chosen - largest - jnp.log(total)
    devices, width = placed_ref.shape
    member = lax.broadcasted_iota(jnp.int32, (devices, masks), 0) % 16
    part = lax.broadcasted_iota(jnp.int32, (devices, masks), 1) // 4
    take = (member == part).astype(F32)
    fits = (
        lax.broadcasted_iota(jnp.int32, (masks, width), 0) % 4
        == lax.broadcasted_iota(jnp.int32, (masks, width), 1) % 4
    )
    layer = lax.broadcasted_iota(jnp.int32, (devices, width), 0) // 16
    slot = lax.broadcasted_iota(jnp.int32, (devices, width), 1) // 4
    wanted = 16 * (2 * layer + lax.axis_index("core")) + slot
    placed = jnp.zeros((devices, width), F32)
    for which in range(2):
        own = jnp.where(fits, score[masks * which : masks * (which + 1), :], 0.0)
        laid = nn_dot(take, own, precision=lax.Precision.HIGHEST)
        placed = jnp.where(wanted == meta_refs[which][0:1, 2:3], laid, placed)
    placed_ref[...] = placed


def collect_kernel(arrived_ref, scores_ref):
    own, rows = scores_ref.shape
    total = jnp.sum(arrived_ref[...], axis=0, keepdims=True)
    count = total.shape[1]
    row = lax.broadcasted_iota(jnp.int32, (count, count), 0)
    lane = lax.broadcasted_iota(jnp.int32, (count, count), 1)
    column = jnp.sum(jnp.where(row == lane, total, 0.0), axis=1, keepdims=True)
    row = lax.broadcasted_iota(jnp.int32, (count, rows), 0)
    slot = lax.broadcasted_iota(jnp.int32, (count, rows), 1)
    parts = [
        jnp.sum(jnp.where(row == slot * own + i, column, 0.0), axis=0, keepdims=True)
        for i in range(own)
    ]
    scores_ref[...] = jnp.concatenate(parts, axis=0)


def pull(array, axis, offset):
    size = lax.axis_size(axis)
    return lax.ppermute(array, axis, [((i + offset) % size, i) for i in range(size)])


def swap(array):
    return lax.ppermute(array, "core", [(0, 1), (1, 0)])


def after(array, *others):
    return lax.optimization_barrier((array, *others))[0]


def gather_line(block, axis, reach):
    near, far = [], []
    for core in range(2):
        for y in range(4):
            for x in range(4):
                def device(step):
                    to_y = (y + step) % 4 if axis == "y" else y
                    to_x = (x + step) % 4 if axis == "x" else x
                    return (((x + y) % 2) * 4 + to_y) * 4 + to_x

                source = (core * 4 + y) * 4 + x
                own = (x + y) % 2 == core
                near.append((source, device(-1 if own else 0)))
                far.append((source, device(1 if own else 2)))
    pairs = far if reach else near
    return lax.ppermute(block, ("core", "y", "x"), pairs)


def on_device(
    hidden_states,
    ln_attn_gain,
    w_qkv,
    output_weight,
    ln_final_gain,
    dense_weight,
    decoder_weight,
    decoder_bias,
    seq_tokens,
    seq_lengths,
    copy_sequence,
    mask_code,
    copy_owner,
):
    _, span, feature = hidden_states.shape
    size = output_weight.shape[0]
    masks = mask_code.shape[1]
    table, pick_table = (jnp.asarray(t) for t in rotary_tables(span, size))
    shape = jax.ShapeDtypeStruct

    def prepare_call(mine, states):
        small = [copy_sequence, seq_lengths, copy_owner, mask_code.T, seq_tokens, ln_attn_gain]
        outs = [
            shape((span, feature), BF16),
            shape((masks, feature), BF16),
            shape((masks, feature), F32),
            shape((masks, 256), F32),
            shape((masks, 128), jnp.int32),
        ]
        args = [*small, pick_table, table, states] if mine else [*small, pick_table, states]
        scratch = [pltpu.VMEM(a.shape, a.dtype) for a in (*small, pick_table)]
        if mine:
            outs.append(shape(table.shape, F32))
            scratch.append(pltpu.VMEM(states.shape, states.dtype))
        n, m = len(args), len(outs)

        def kernel(*refs):
            prepare_kernel(
                mine, refs[:6], refs[6], refs[n - 1], refs[7], refs[n : n + m], refs[n + m : -1],
                refs[-1],
            )

        return call(
            kernel,
            outs,
            args,
            n_any=9 if mine else 7,
            scratch=[*scratch, pltpu.SemaphoreType.DMA((9,))],
            flops=4 * masks * span * feature + 10 * span * feature,
        )

    def attend_args(ready, key_blocks, value_blocks):
        per_copy = [r[i] for i in (0, 1, 3, 4) for r in ready]
        return (ready[0][5], *per_copy, *key_blocks, *value_blocks)

    def attend_refs(refs, keys, values):
        return (refs[0], refs[1:3], refs[3:5], refs[5:7], refs[7:9], keys, values)

    def attend_call(ready, key_lines, value_lines):
        count = len(key_lines)

        def kernel(*refs):
            lines = [halves(r) for r in refs[9:-2]]
            keys = [h for line in lines[:count] for h in line]
            values = [h for line in lines[count:] for h in line]
            attend_kernel(*attend_refs(refs, keys, values), *refs[-2:])

        heads = 2 * count
        return call(
            kernel,
            [
                shape((2, heads * masks, span), BF16),
                shape((2, span, heads * size), BF16),
            ],
            attend_args(ready, key_lines, value_lines),
            flops=4 * span * feature * heads * 128,
            exps=2 * heads * masks * span,
        )

    states = hidden_states[0]
    key_block, value_block = pack(jnp.transpose(w_qkv[:, 0, :]), output_weight[:, 0, :])
    key_low = gather_line(key_block, "x", False)
    value_low = gather_line(value_block, "y", False)
    key_high = gather_line(key_block, "x", True)
    value_high = gather_line(value_block, "y", True)
    states_other = swap(states)
    key_line = join(key_low, key_high)
    key_ahead = pull(key_line, "y", 1)
    key_behind = pull(key_line, "y", 3)
    value_line = join(value_low, value_high)
    value_ahead = pull(value_line, "x", 1)
    value_behind = pull(value_line, "x", 3)
    mine = prepare_call(True, after(states, key_line, value_line))
    other = prepare_call(False, after(states_other, mine[0]))
    ready = (mine, other)
    own_probs, own_values = attend_call(ready, (key_line,), (value_line,))
    rows = key_line.shape[0]
    key_far = (
        pull(part(after(key_ahead, own_probs), 0, rows // 2), "y", 1),
        pull(part(after(key_behind, own_probs), rows // 2, rows), "y", 3),
    )
    value_far = (
        pull(part(after(value_ahead, own_probs), 0, rows // 2), "x", 1),
        pull(part(after(value_behind, own_probs), rows // 2, rows), "x", 3),
    )
    near_probs, near_values = attend_call(
        ready, (key_ahead, key_behind), (value_ahead, value_behind)
    )
    key_far = tuple(after(b, near_probs) for b in key_far)
    far_args = attend_args(ready, key_far, ())

    def far_kernel(*refs):
        probs_kernel(*attend_refs(refs, refs[9:11], ()), refs[-1])

    far_probs = call(
        far_kernel,
        shape((2, 2 * masks, span), BF16),
        far_args,
        flops=4 * span * feature * 256,
        exps=4 * masks * span,
    )
    value_far = tuple(after(b, far_probs) for b in value_far)

    def mix(*refs):
        blocks = [h for r in refs[9:12] for h in halves(r)]
        mix_kernel(refs[:3], refs[3:5], refs[5:7], refs[7:9], blocks, *refs[12:])

    partial, sent = call(
        mix,
        [shape((2 * masks, feature), F32), shape((2 * masks, feature), BF16)],
        (
            own_probs, near_probs, far_probs, own_values, near_values, mine[0], other[0],
            *value_far, value_line, value_ahead, value_behind,
        ),
        flops=4 * span * feature * 256 + 4 * masks * feature * 8 * size,
    )

    def score(*refs):
        score_kernel(refs[:2], *refs[2:4], refs[4:6], *refs[6:])

    placed = call(
        score,
        shape((128, 64), F32),
        (
            mine[2], other[2], partial, swap(sent), mine[4], other[4],
            ln_final_gain.reshape(1, -1), decoder_bias.reshape(1, -1), dense_weight,
            decoder_weight.T,
        ),
        flops=4 * masks * feature * feature,
    )
    arrived = lax.all_to_all(placed, ("z", "y", "x"), 0, 0, tiled=True)
    return call(collect_kernel, shape((4, 16), F32), (arrived,)).T


def solution(mesh):
    fine = Mesh(mesh.devices.reshape(8, 2, 4, 4), ("z", "core", "y", "x"))
    dp, mp = ("z", "core"), ("y", "x")
    placed = (
        P(("z", "core", "y", "x"), None, None),
        P(),
        P(None, mp, None),
        P(None, mp, None),
        P(),
        P(),
        P(),
        P(),
        P(),
        P(),
        P(),
        P(),
        P(),
    )
    return jax.shard_map(
        on_device, mesh=fine, in_specs=placed, out_specs=P(dp, mp), check_vma=False
    )
```

```python
import numpy as np
import jax
import jax.numpy as jnp
from jax import lax
from jax.experimental import pallas as pl
from jax.experimental.pallas import tpu as pltpu
from jax.sharding import Mesh, PartitionSpec as P

epsilon = 1e-05
F32 = jnp.float32
BF16 = jnp.bfloat16


def rotary_tables(seq_span, head_size):
    half = head_size // 2
    power = (np.arange(half, dtype=np.float32) * np.float32(2.0 / head_size)).astype(np.float32)
    frequency = (np.float32(1.0) / np.power(np.float32(10000.0), power)).astype(np.float32)
    angles = (np.arange(seq_span, dtype=np.float32)[:, None] * frequency[None, :]).astype(np.float32)
    cosine = np.cos(angles.astype(np.float64)).astype(np.float32)
    sine = np.sin(angles.astype(np.float64)).astype(np.float32)
    wide = np.concatenate([cosine] * 4 + [-sine, sine] * 2, axis=1)
    rest = np.concatenate([cosine, sine], axis=1)
    parts = []
    for _ in range(3):
        parts.append(rest.astype(BF16))
        rest = rest - parts[-1].astype(np.float32)
    parts.append(np.zeros_like(parts[0]))
    return wide, np.concatenate(parts, axis=1)


def nt_dot(a, b):
    return lax.dot_general(a, b, (((1,), (1,)), ((), ())), preferred_element_type=F32)


def nn_dot(a, b, **options):
    return lax.dot_general(a, b, (((1,), (0,)), ((), ())), preferred_element_type=F32, **options)


def rotate(part, table, half):
    cos_table, sin_table = table[:, :128], table[:, 128:]
    width = part.shape[1]
    lane = lax.broadcasted_iota(jnp.int32, part.shape, 1) % (2 * half)
    turned = jnp.where(
        lane < half,
        pltpu.roll(part, width - half, 1),
        pltpu.roll(part, half, 1),
    )
    return part * cos_table + turned * sin_table


IN_PLACE = pl.BlockSpec(memory_space=pltpu.MemorySpace.HBM)
ON_CHIP = pl.BlockSpec(memory_space=pltpu.MemorySpace.VMEM)


def call(kernel, outs, args, n_any=0, scratch=(), flops=0, exps=0, vmem=24 * 1024 * 1024):
    moved = sum(a.size * a.dtype.itemsize for a in list(args) + jax.tree.leaves(outs))
    place = pltpu.with_memory_space_constraint
    args = [place(a, pltpu.HBM) if i < n_any else a for i, a in enumerate(args)]
    return pl.pallas_call(
        kernel,
        out_shape=outs,
        in_specs=[IN_PLACE] * n_any + [ON_CHIP] * (len(args) - n_any),
        out_specs=jax.tree.map(lambda _: ON_CHIP, outs),
        scratch_shapes=list(scratch),
        cost_estimate=pl.CostEstimate(flops=flops, transcendentals=exps, bytes_accessed=moved),
        compiler_params=pltpu.CompilerParams(vmem_limit_bytes=vmem),
    )(*args)


def pack_kernel(turned_ref, out_ref, key_ref, value_ref, sems):
    size = out_ref.shape[0]
    copies = (
        pltpu.make_async_copy(turned_ref.at[: 2 * size], key_ref, sems.at[0]),
        pltpu.make_async_copy(turned_ref.at[2 * size :], value_ref.at[:size], sems.at[1]),
        pltpu.make_async_copy(out_ref, value_ref.at[size:], sems.at[2]),
    )
    for copy in copies:
        copy.start()
    for copy in copies:
        copy.wait()


def pack(turned, out_weight):
    size, feature = out_weight.shape
    return call(
        pack_kernel,
        [jax.ShapeDtypeStruct((2 * size, feature), BF16)] * 2,
        (turned, out_weight),
        n_any=2,
        scratch=[pltpu.SemaphoreType.DMA((3,))],
    )


def first(mask, values):
    picked = jnp.sum(jnp.where(mask, values, 0), axis=1, keepdims=True)
    return jnp.sum(picked, axis=0, keepdims=True)


def norm_rows(values, gain):
    average = jnp.mean(values, axis=1, keepdims=True)
    centred = values - average
    variance = jnp.mean(centred * centred, axis=1, keepdims=True)
    return (centred * lax.rsqrt(variance + epsilon) * gain).astype(BF16)


def prepare_kernel(mine, small_refs, pick_ref, states_from, table_from, out_refs, scratch, sems):
    normed_ref, picked_ref, rows_ref, qtable_ref, meta_ref = out_refs[:5]
    copies = [
        pltpu.make_async_copy(source, target, sems.at[i])
        for i, (source, target) in enumerate(zip((*small_refs, pick_ref), scratch))
    ]
    late = []
    if mine:
        states_ref = scratch[7]
        late = [
            pltpu.make_async_copy(states_from, states_ref, sems.at[7]),
            pltpu.make_async_copy(table_from, out_refs[5], sems.at[8]),
        ]
    else:
        states_ref = states_from
    for copy in (*copies, *late):
        copy.start()
    sequence_ref, length_ref, owner_ref, codes_ref, tokens_ref, gain_ref, pick_ref = scratch[:7]
    span, feature = normed_ref.shape
    masks = codes_ref.shape[0]
    core = lax.axis_index("core")
    core = core if mine else 1 - core
    copy_id = (
        (lax.axis_index("z") * 2 + core) * 4 + lax.axis_index("y")
    ) * 4 + lax.axis_index("x")
    copies[5].wait()
    block = 16

    def norm_all():
        gain = gain_ref[...].reshape(1, -1)

        def step(i, carry):
            at = pl.multiple_of(i * block, block)
            values = states_ref[pl.ds(at, block), :].astype(F32)
            normed_ref[pl.ds(at, block), :] = norm_rows(values, gain)
            return carry

        lax.fori_loop(0, span // block, step, 0, unroll=20)

    if not mine:
        norm_all()
    for copy in (*copies[:5], copies[6]):
        copy.wait()

    def numbers(count):
        return lax.broadcasted_iota(jnp.int32, (1, count), 1)

    own = numbers(codes_ref.shape[1]) == copy_id
    sequence = first(own, sequence_ref[...].reshape(1, -1))
    owner = first(own, owner_ref[...].reshape(1, -1))
    length = first(numbers(length_ref.shape[0]) == sequence, length_ref[...].reshape(1, -1))
    codes = jnp.sum(jnp.where(own, codes_ref[...], 0), axis=1, keepdims=True)
    quotient = jnp.floor(codes.astype(F32) / length.astype(F32)).astype(jnp.int32)
    positions = codes - quotient * length
    positions = jnp.where(positions < 0, positions + length, positions)
    positions = jnp.where(positions >= length, positions - length, positions)
    hit = lax.broadcasted_iota(jnp.int32, (masks, span), 1) == positions
    line = lax.broadcasted_iota(jnp.int32, tokens_ref.shape, 0)
    tokens = jnp.sum(jnp.where(line == sequence, tokens_ref[...], 0), axis=0, keepdims=True)
    targets = jnp.sum(jnp.where(hit, tokens, 0), axis=1, keepdims=True)
    lane = lax.broadcasted_iota(jnp.int32, meta_ref.shape, 1)
    meta_ref[...] = jnp.where(lane == 0, targets, jnp.where(lane == 1, length, owner))
    hot = hit.astype(F32).astype(BF16)
    picks = nn_dot(hot, pick_ref[...])
    wide = picks.shape[1] // 4
    picks = picks[:, :wide] + picks[:, wide : 2 * wide] + picks[:, 2 * wide : 3 * wide]
    cosine, sine = picks[:, : wide // 2], picks[:, wide // 2 :]
    qtable_ref[...] = jnp.concatenate([cosine] * 4 + [-sine, sine] * 2, axis=1)
    for copy in late:
        copy.wait()
    if mine:
        norm_all()
    rows = nn_dot(hot, states_ref[...])
    rows_ref[...] = rows
    picked_ref[...] = norm_rows(rows, gain_ref[...].reshape(1, -1))


def attend(table_ref, normed_refs, picked_refs, qtable_refs, meta_refs, key_refs, value_refs):
    size = key_refs[0].shape[0] // 2
    masks = picked_refs[0].shape[0]
    heads = len(key_refs)
    width = heads * size
    half = size // 2
    if value_refs:
        beside = [r[:size, :] for r in value_refs]
    else:
        beside = [r[start : start + half, :] for r in key_refs for start in (size + half, size)]
    weight = jnp.concatenate([r[size:, :] for r in key_refs] + beside, axis=0)
    query_weight = jnp.concatenate([r[:size, :] for r in key_refs], axis=0)
    picked = jnp.concatenate([r[...] for r in picked_refs], axis=0)
    queries = nt_dot(picked, query_weight) * 0.125
    results = []
    for which in range(2):
        length = meta_refs[which][0:1, 1:2]
        projected = nt_dot(normed_refs[which][...], weight)
        own = queries[masks * which : masks * (which + 1), :]
        turned_keys, turned_queries = [], []
        for i in range(heads // 2):
            lanes = slice(128 * i, 128 * (i + 1))
            if value_refs:
                turned_keys.append(rotate(projected[:, lanes], table_ref[...], half))
            else:
                exchanged = projected[:, width + 128 * i : width + 128 * (i + 1)]
                table = table_ref[...]
                turned_keys.append(
                    projected[:, lanes] * table[:, :128] + exchanged * table[:, 128:]
                )
            turned_queries.append(rotate(own[:, lanes], qtable_refs[which][...], size // 2))
        key_rows = jnp.concatenate(turned_keys, axis=1).astype(BF16)
        query_rows = jnp.concatenate(turned_queries, axis=1).astype(BF16)
        spread = jnp.concatenate([query_rows] * heads, axis=0)
        row = lax.broadcasted_iota(jnp.int32, spread.shape, 0) // masks
        lane = lax.broadcasted_iota(jnp.int32, spread.shape, 1) // size
        spread = jnp.where(row == lane, spread, jnp.zeros_like(spread))
        logits = nt_dot(spread, key_rows)
        alive = lax.broadcasted_iota(jnp.int32, logits.shape, 1) < length
        logits = jnp.where(alive, logits, -1e30)
        largest = jnp.max(logits, axis=1, keepdims=True)
        weights = jnp.exp(logits - largest)
        total = jnp.sum(weights, axis=1, keepdims=True)
        probs = (weights * (1.0 / total)).astype(BF16)
        results.append((probs, projected[:, width:].astype(BF16)))
    return results


def attend_kernel(*refs):
    inputs, (probs_ref, values_ref) = refs[:-2], refs[-2:]
    for which, (probs, values) in enumerate(attend(*inputs)):
        probs_ref[which] = probs
        values_ref[which] = values


def mix_columns(columns, probs, values, masks, size):
    right = (lax.axis_index("x") + lax.axis_index("y")) % 2 == lax.axis_index("core")

    def rows_of(step, which):
        start = masks * (which + (2 if step == 3 else 0))
        return probs[(0, 1, 2, 1)[step]](start, start + masks)

    stack = []
    for column in columns:
        which = column // 2
        for i in range(2):
            even = rows_of((0, 2)[i], which)
            odd = rows_of((1, 3)[i], which)
            if column % 2:
                even, odd = odd, even
            stack.append(jnp.where(right, even, odd))
    mixed = nn_dot(jnp.concatenate(stack, axis=0), values)
    lane = lax.broadcasted_iota(jnp.int32, (masks, mixed.shape[1]), 1) // size
    context = mixed[:masks, :]
    for head in range(1, len(stack)):
        context = jnp.where(lane == head, mixed[masks * head : masks * (head + 1), :], context)
    return context.astype(BF16)


def rows_reader(ref, copy):
    return lambda start, end: ref[copy, start:end, :]


def probs_kernel(*refs):
    inputs, probs_ref = refs[:-1], refs[-1]
    for which, (probs, _) in enumerate(attend(*inputs)):
        probs_ref[which] = probs


def mix_kernel(
    probs_refs, values_refs, normed_refs, far_refs, block_refs, partial_ref, sent_ref
):
    size = block_refs[0].shape[0] // 2
    masks = probs_refs[0].shape[1] // 2
    value_weight = jnp.concatenate([r[:size, :] for r in far_refs], axis=0)
    contexts = []
    for copy in range(2):
        readers = [rows_reader(r, copy) for r in probs_refs]
        far = nt_dot(normed_refs[copy][...], value_weight).astype(BF16)
        values = (values_refs[0][copy], values_refs[1][copy], far)
        contexts.append(
            jnp.concatenate(
                [
                    mix_columns(columns, readers, value, masks, size)
                    for columns, value in zip(((0,), (1, 3), (2,)), values)
                ],
                axis=1,
            )
        )
    weight = jnp.concatenate([r[size:, :] for r in (*block_refs, *far_refs)], axis=0)
    partial = nn_dot(jnp.concatenate(contexts, axis=0), weight)
    partial_ref[...] = partial
    sent_ref[...] = partial.astype(BF16)


def join_kernel(low_ref, high_ref, line_ref):
    rows = low_ref.shape[0]
    line_ref[:rows, :] = low_ref[...]
    line_ref[rows:, :] = high_ref[...]


def join(low, high):
    line = jax.ShapeDtypeStruct((2 * low.shape[0], low.shape[1]), low.dtype)
    return call(join_kernel, line, (low, high))


def part(array, start, end):
    def kernel(array_ref, part_ref):
        part_ref[...] = array_ref[start:end, :]

    return call(kernel, jax.ShapeDtypeStruct((end - start, array.shape[1]), array.dtype), (array,))


def halves(ref):
    rows = ref.shape[0] // 2
    return ref.at[:rows], ref.at[rows:]


def score_kernel(
    rows_refs, partial_ref, arrived_ref, meta_refs, gain_ref, bias_ref, dense_ref, decoder_ref,
    placed_ref,
):
    masks = rows_refs[0].shape[0]
    arrived = arrived_ref[...].astype(F32)
    residual = jnp.concatenate(
        [
            rows_refs[0][...] + (partial_ref[:masks, :] + arrived[masks:, :]),
            rows_refs[1][...] + (partial_ref[masks:, :] + arrived[:masks, :]),
        ],
        axis=0,
    )
    targets = jnp.concatenate([r[:, 0:1] for r in meta_refs], axis=0)
    average = jnp.mean(residual, axis=1, keepdims=True)
    centred = residual - average
    variance = jnp.mean(centred * centred, axis=1, keepdims=True)
    normed = (centred * lax.rsqrt(variance + epsilon) * gain_ref[...]).astype(BF16)
    dense = nn_dot(normed, dense_ref[...])
    active = 0.5 * dense * (1.0 + lax.erf(dense * np.float32(0.5**0.5)))
    average = jnp.mean(active, axis=1, keepdims=True)
    centred = active - average
    variance = jnp.mean(centred * centred, axis=1, keepdims=True)
    headed = (centred * lax.rsqrt(variance + epsilon)).astype(BF16)
    logits = nt_dot(headed, decoder_ref[...]) + bias_ref[...]
    largest = jnp.max(logits, axis=1, keepdims=True)
    total = jnp.sum(jnp.exp(logits - largest), axis=1, keepdims=True)
    vocab = lax.broadcasted_iota(jnp.int32, logits.shape, 1)
    chosen = jnp.sum(jnp.where(vocab == targets, logits, 0.0), axis=1, keepdims=True)
    score = chosen - largest - jnp.log(total)
    devices, width = placed_ref.shape
    member = lax.broadcasted_iota(jnp.int32, (devices, masks), 0) % 16
    part = lax.broadcasted_iota(jnp.int32, (devices, masks), 1) // 4
    take = (member == part).astype(F32)
    fits = (
        lax.broadcasted_iota(jnp.int32, (masks, width), 0) % 4
        == lax.broadcasted_iota(jnp.int32, (masks, width), 1) % 4
    )
    layer = lax.broadcasted_iota(jnp.int32, (devices, width), 0) // 16
    slot = lax.broadcasted_iota(jnp.int32, (devices, width), 1) // 4
    wanted = 16 * (2 * layer + lax.axis_index("core")) + slot
    placed = jnp.zeros((devices, width), F32)
    for which in range(2):
        own = jnp.where(fits, score[masks * which : masks * (which + 1), :], 0.0)
        laid = nn_dot(take, own, precision=lax.Precision.HIGHEST)
        placed = jnp.where(wanted == meta_refs[which][0:1, 2:3], laid, placed)
    placed_ref[...] = placed


def collect_kernel(arrived_ref, scores_ref):
    own, rows = scores_ref.shape
    total = jnp.sum(arrived_ref[...], axis=0, keepdims=True)
    count = total.shape[1]
    row = lax.broadcasted_iota(jnp.int32, (count, count), 0)
    lane = lax.broadcasted_iota(jnp.int32, (count, count), 1)
    column = jnp.sum(jnp.where(row == lane, total, 0.0), axis=1, keepdims=True)
    row = lax.broadcasted_iota(jnp.int32, (count, rows), 0)
    slot = lax.broadcasted_iota(jnp.int32, (count, rows), 1)
    parts = [
        jnp.sum(jnp.where(row == slot * own + i, column, 0.0), axis=0, keepdims=True)
        for i in range(own)
    ]
    scores_ref[...] = jnp.concatenate(parts, axis=0)


def pull(array, axis, offset):
    size = lax.axis_size(axis)
    return lax.ppermute(array, axis, [((i + offset) % size, i) for i in range(size)])


def swap(array):
    return lax.ppermute(array, "core", [(0, 1), (1, 0)])


def after(array, *others):
    return lax.optimization_barrier((array, *others))[0]


def gather_line(block, axis, reach):
    near, far = [], []
    for core in range(2):
        for y in range(4):
            for x in range(4):
                def device(step):
                    to_y = (y + step) % 4 if axis == "y" else y
                    to_x = (x + step) % 4 if axis == "x" else x
                    return (((x + y) % 2) * 4 + to_y) * 4 + to_x

                source = (core * 4 + y) * 4 + x
                own = (x + y) % 2 == core
                near.append((source, device(-1 if own else 0)))
                far.append((source, device(1 if own else 2)))
    pairs = far if reach else near
    return lax.ppermute(block, ("core", "y", "x"), pairs)


def on_device(
    hidden_states,
    ln_attn_gain,
    w_qkv,
    output_weight,
    ln_final_gain,
    dense_weight,
    decoder_weight,
    decoder_bias,
    seq_tokens,
    seq_lengths,
    copy_sequence,
    mask_code,
    copy_owner,
):
    _, span, feature = hidden_states.shape
    size = output_weight.shape[0]
    masks = mask_code.shape[1]
    table, pick_table = (jnp.asarray(t) for t in rotary_tables(span, size))
    shape = jax.ShapeDtypeStruct

    def prepare_call(mine, states):
        small = [copy_sequence, seq_lengths, copy_owner, mask_code.T, seq_tokens, ln_attn_gain]
        outs = [
            shape((span, feature), BF16),
            shape((masks, feature), BF16),
            shape((masks, feature), F32),
            shape((masks, 256), F32),
            shape((masks, 128), jnp.int32),
        ]
        args = [*small, pick_table, table, states] if mine else [*small, pick_table, states]
        scratch = [pltpu.VMEM(a.shape, a.dtype) for a in (*small, pick_table)]
        if mine:
            outs.append(shape(table.shape, F32))
            scratch.append(pltpu.VMEM(states.shape, states.dtype))
        n, m = len(args), len(outs)

        def kernel(*refs):
            prepare_kernel(
                mine, refs[:6], refs[6], refs[n - 1], refs[7], refs[n : n + m], refs[n + m : -1],
                refs[-1],
            )

        return call(
            kernel,
            outs,
            args,
            n_any=9 if mine else 7,
            scratch=[*scratch, pltpu.SemaphoreType.DMA((9,))],
            flops=4 * masks * span * feature + 10 * span * feature,
        )

    def attend_args(ready, key_blocks, value_blocks):
        per_copy = [r[i] for i in (0, 1, 3, 4) for r in ready]
        return (ready[0][5], *per_copy, *key_blocks, *value_blocks)

    def attend_refs(refs, keys, values):
        return (refs[0], refs[1:3], refs[3:5], refs[5:7], refs[7:9], keys, values)

    def attend_call(ready, key_lines, value_lines):
        count = len(key_lines)

        def kernel(*refs):
            lines = [halves(r) for r in refs[9:-2]]
            keys = [h for line in lines[:count] for h in line]
            values = [h for line in lines[count:] for h in line]
            attend_kernel(*attend_refs(refs, keys, values), *refs[-2:])

        heads = 2 * count
        return call(
            kernel,
            [
                shape((2, heads * masks, span), BF16),
                shape((2, span, heads * size), BF16),
            ],
            attend_args(ready, key_lines, value_lines),
            flops=4 * span * feature * heads * 128,
            exps=2 * heads * masks * span,
        )

    states = hidden_states[0]
    key_block, value_block = pack(jnp.transpose(w_qkv[:, 0, :]), output_weight[:, 0, :])
    key_low = gather_line(key_block, "y", False)
    value_low = gather_line(value_block, "x", False)
    key_high = gather_line(key_block, "y", True)
    value_high = gather_line(value_block, "x", True)
    states_other = swap(states)
    key_line = join(key_low, key_high)
    key_ahead = pull(key_line, "x", 1)
    key_behind = pull(key_line, "x", 3)
    value_line = join(value_low, value_high)
    value_ahead = pull(value_line, "y", 1)
    value_behind = pull(value_line, "y", 3)
    mine = prepare_call(True, after(states, key_line, value_line))
    other = prepare_call(False, after(states_other, mine[0]))
    ready = (mine, other)
    own_probs, own_values = attend_call(ready, (key_line,), (value_line,))
    rows = key_line.shape[0]
    key_far = (
        pull(part(after(key_ahead, own_probs), 0, rows // 2), "x", 1),
        pull(part(after(key_behind, own_probs), rows // 2, rows), "x", 3),
    )
    value_far = (
        pull(part(after(value_ahead, own_probs), 0, rows // 2), "y", 1),
        pull(part(after(value_behind, own_probs), rows // 2, rows), "y", 3),
    )
    near_probs, near_values = attend_call(
        ready, (key_ahead, key_behind), (value_ahead, value_behind)
    )
    key_far = tuple(after(b, near_probs) for b in key_far)
    far_args = attend_args(ready, key_far, ())

    def far_kernel(*refs):
        probs_kernel(*attend_refs(refs, refs[9:11], ()), refs[-1])

    far_probs = call(
        far_kernel,
        shape((2, 2 * masks, span), BF16),
        far_args,
        flops=4 * span * feature * 256,
        exps=4 * masks * span,
    )
    value_far = tuple(after(b, far_probs) for b in value_far)

    def mix(*refs):
        blocks = [h for r in refs[9:12] for h in halves(r)]
        mix_kernel(refs[:3], refs[3:5], refs[5:7], refs[7:9], blocks, *refs[12:])

    partial, sent = call(
        mix,
        [shape((2 * masks, feature), F32), shape((2 * masks, feature), BF16)],
        (
            own_probs, near_probs, far_probs, own_values, near_values, mine[0], other[0],
            *value_far, value_line, value_ahead, value_behind,
        ),
        flops=4 * span * feature * 256 + 4 * masks * feature * 8 * size,
    )

    def score(*refs):
        score_kernel(refs[:2], *refs[2:4], refs[4:6], *refs[6:])

    placed = call(
        score,
        shape((128, 64), F32),
        (
            mine[2], other[2], partial, swap(sent), mine[4], other[4],
            ln_final_gain.reshape(1, -1), decoder_bias.reshape(1, -1), dense_weight,
            decoder_weight.T,
        ),
        flops=4 * masks * feature * feature,
    )
    arrived = lax.all_to_all(placed, ("z", "y", "x"), 0, 0, tiled=True)
    return call(collect_kernel, shape((4, 16), F32), (arrived,)).T


def solution(mesh):
    fine = Mesh(mesh.devices.reshape(8, 2, 4, 4), ("z", "core", "y", "x"))
    dp, mp = ("z", "core"), ("y", "x")
    placed = (
        P(("z", "core", "y", "x"), None, None),
        P(),
        P(None, mp, None),
        P(None, mp, None),
        P(),
        P(),
        P(),
        P(),
        P(),
        P(),
        P(),
        P(),
        P(),
    )
    return jax.shard_map(
        on_device, mesh=fine, in_specs=placed, out_specs=P(dp, mp), check_vma=False
    )
```
